128 devices in a mesh: seq: 8 (over z, core), blk: 4 (over y), tp: 4 (over x).
Axes of the slice: x: 4, y: 4, z: 4, core: 2. Of those that a mesh axis runs over, the one named last changes fastest.
Arguments:
- hidden_in: bfloat16 [16384, 1024], P(('seq', 'blk', 'tp')), may hold values from -24 to 24
- ln1_gain: float32 [1024], replicated, may hold values from 0.1 to 1.9
- ln1_bias: float32 [1024], replicated, may hold values from -3 to 3
- qkv_weight: bfloat16 [1024, 3072], replicated, may hold values from -0.1875 to 0.1875
- qv_bias: float32 [2, 1024], replicated, may hold values from -3 to 3
- out_weight: bfloat16 [1024, 1024], replicated, may hold values from -0.75 to 0.75
- out_bias: float32 [1024], replicated, may hold values from -3 to 3
- ln2_gain: float32 [1024], replicated, may hold values from 0.1 to 1.9
- ln2_bias: float32 [1024], replicated, may hold values from -3 to 3
- fc_weight: bfloat16 [1024, 4096], P(None, 'tp'), may hold values from -0.1875 to 0.1875
- fc_bias: float32 [4096], P('tp'), may hold values from -3 to 3
- proj_weight: bfloat16 [4096, 1024], P('tp'), may hold values from -0.09375 to 0.09375
- proj_bias: float32 [1024], replicated, may hold values from -3 to 3
- cotangent: float32 [16384, 1024], P(('seq', 'blk', 'tp')), may hold values from -3 to 3
Outputs:
- block_out: float32 [16384, 1024], P(('seq', 'blk', 'tp'))
- input_grad: float32 [16384, 1024], P(('seq', 'blk', 'tp'))
- ln1_gain_grad: float32 [1024], P(('seq', 'blk'))
- ln1_bias_grad: float32 [1024], P(('seq', 'blk'))
- qkv_weight_grad: float32 [1024, 3072], P(('seq', 'blk'))
- qv_bias_grad: float32 [2, 1024], P(None, ('seq', 'blk'))
- out_weight_grad: float32 [1024, 1024], P(('seq', 'blk'))
- out_bias_grad: float32 [1024], P(('seq', 'blk'))
- ln2_gain_grad: float32 [1024], P(('seq', 'blk'))
- ln2_bias_grad: float32 [1024], P(('seq', 'blk'))
- fc_weight_grad: float32 [1024, 4096], P(None, 'tp')
- fc_bias_grad: float32 [4096], P('tp')
- proj_weight_grad: float32 [4096, 1024], P('tp')
- proj_bias_grad: float32 [1024], P(('seq', 'blk'))
The draws below stay inside these ranges and needn't reach their ends.
All inputs are finite; a program needn't handle non-finite values.
Results may differ from the reference program's by a relative error of at most 0.025.
Values may be sent and summed in bfloat16 or wider, within the bound.
A program may use at most 128 MiB of HBM per device.

```python
import math
import jax
import jax.numpy as jnp
from jax import lax

D = 1024
HEADS = 16
HEAD_DIM = 64
FF = 4096
TOKENS = 16384


def spiked(drawn, rng, source, target, shards_of, factor):
    def block_of(dim):
        return (jnp.arange(drawn.shape[dim]) // (drawn.shape[dim] // shards_of)).reshape((-1,) + (1,) * (drawn.ndim - 1 - dim))

    near = jax.random.permutation(rng, shards_of)[block_of(target)]
    far = (block_of(target) + shards_of // 2) % shards_of
    return jnp.where((block_of(source) == near) | (block_of(source) == far), factor * drawn, drawn)


def levels(stream_key, dims, pieces, least, largest):
    loudness, own = 1.0, jax.random.fold_in(stream_key, 6)
    for dim, parts in pieces:
        steps = jnp.exp(jax.random.uniform(jax.random.fold_in(own, dim), (parts,), jnp.float32, least / len(pieces), largest / len(pieces)))
        loudness = loudness * jnp.repeat(steps, dims[dim] // parts).reshape([-1 if axis == dim else 1 for axis in range(len(dims))])
    return loudness


def bell_draw(stream_key, shape, spread, most, split=(), kind=jnp.bfloat16):
    gain = levels(stream_key, shape, split, -0.22, 0.18) if split else 1.0
    result = jax.random.normal(stream_key, shape, jnp.float32) * spread * gain
    return jnp.minimum(jnp.maximum(result, -most), most).astype(kind)


def bell_draw_with(stream_key, shape, width, bound, cuts, heavy, held_as=jnp.bfloat16):
    drawn = width * jax.random.normal(stream_key, shape, jnp.float32)
    if cuts:
        drawn = drawn * levels(stream_key, shape, cuts, -0.22, 0.18)
    return jnp.clip(spiked(drawn, jax.random.fold_in(stream_key, 3), *heavy), -bound, bound).astype(held_as)


def setup_inputs(seed: int = 0) -> dict:
    streams_of = jax.random.split(jax.random.key(seed), 15)
    hidden_in = bell_draw_with(streams_of[0], (TOKENS, D), 1.0, 24.0, ((0, 128),), (0, 1, 128, 5.5))
    ln1_gain = jnp.clip(1.0 + 0.18 * jax.random.normal(streams_of[1], (D,), jnp.float32), 0.1, 1.9)
    ln1_bias = bell_draw(streams_of[2], (D,), 0.5, 3.0, (), jnp.float32)
    qkv_weight = bell_draw(streams_of[3], (D, 3 * D), D ** -0.5, 0.1875)
    qv_bias = bell_draw(streams_of[4], (2, D), 0.5, 3.0, (), jnp.float32)
    out_weight = bell_draw(streams_of[5], (D, D), (max(D // 16, 1)) ** -0.5, 0.75)
    out_bias = bell_draw(streams_of[6], (D,), 0.5, 3.0, (), jnp.float32)
    ln2_gain = jnp.clip(1.0 + 0.18 * jax.random.normal(streams_of[7], (D,), jnp.float32), 0.1, 1.9)
    ln2_bias = bell_draw(streams_of[8], (D,), 0.5, 3.0, (), jnp.float32)
    fc_weight = bell_draw(streams_of[9], (D, FF), D ** -0.5, 0.1875, ((1, 4),))
    fc_bias = bell_draw(streams_of[10], (FF,), 0.5, 3.0, ((0, 4),), jnp.float32)
    proj_weight = bell_draw(streams_of[11], (FF, D), FF ** -0.5, 0.09375, ((0, 4),))
    proj_bias = bell_draw(streams_of[12], (D,), 0.5, 3.0, (), jnp.float32)
    cotangent = bell_draw_with(streams_of[13], (TOKENS, D), (16 * TOKENS ** -0.5), 3.0, ((0, 128),), (0, 1, 128, 5.5), jnp.float32)
    return dict(hidden_in=hidden_in, ln1_gain=ln1_gain, ln1_bias=ln1_bias, qkv_weight=qkv_weight, qv_bias=qv_bias, out_weight=out_weight, out_bias=out_bias, ln2_gain=ln2_gain, ln2_bias=ln2_bias, fc_weight=fc_weight, fc_bias=fc_bias, proj_weight=proj_weight, proj_bias=proj_bias, cotangent=cotangent)


epsilon = 1e-05
gelu_coef = math.sqrt(2.0 / math.pi)
masked_score = -1e+30

def to_bfloat(values):
    return lax.optimization_barrier(values.astype(jnp.bfloat16))

def normalize(matrix, norm_gain, norm_shift):
    row_mean = lax.optimization_barrier(jnp.mean(matrix, axis=-1, keepdims=True))
    centered = matrix - row_mean
    variance = lax.optimization_barrier(jnp.mean(centered * centered, axis=-1, keepdims=True))
    inverse = lax.rsqrt(variance + epsilon)
    scaled = centered * inverse
    return (scaled, inverse, scaled * norm_gain + norm_shift)

def norm_back(upstream_grad, scaled, inverse, norm_gain):
    weighted = upstream_grad * norm_gain
    first_mean = lax.optimization_barrier(jnp.mean(weighted, axis=-1, keepdims=True))
    second_mean = lax.optimization_barrier(jnp.mean(weighted * scaled, axis=-1, keepdims=True))
    return inverse * (weighted - first_mean - scaled * second_mean)

def gelu_pair(hidden_pre):
    tanh_arg = gelu_coef * (hidden_pre + 0.044715 * hidden_pre * hidden_pre * hidden_pre)
    tanh_value = jnp.tanh(tanh_arg)
    gelu_value = 0.5 * hidden_pre * (1.0 + tanh_value)
    gelu_slope = 0.5 * (1.0 + tanh_value) + 0.5 * hidden_pre * (1.0 - tanh_value * tanh_value) * gelu_coef * (1.0 + 3.0 * 0.044715 * hidden_pre * hidden_pre)
    return (gelu_value, gelu_slope)

def forward_head(head_inputs):
    query_head, key_head, value_head = head_inputs
    block_rows = min(TOKENS, 2048)
    block_total = TOKENS // block_rows
    score_scale = 1.0 / math.sqrt(HEAD_DIM)
    key_place = jnp.arange(TOKENS, dtype=jnp.int32)

    def query_block_step(block_number):
        first_row = block_number * block_rows
        query_block = lax.dynamic_slice_in_dim(query_head, first_row, block_rows, 0)
        scores = jnp.dot(query_block, key_head.T, precision=lax.Precision.HIGHEST) * score_scale
        query_place = first_row + jnp.arange(block_rows, dtype=jnp.int32)
        visible = query_place[:, None] >= key_place[None, :]
        scores = jnp.where(visible, scores, masked_score)
        row_max = lax.optimization_barrier(jnp.max(scores, axis=1))
        attn_prob = jnp.where(visible, jnp.exp(scores - row_max[:, None]), 0.0)
        row_sum = lax.optimization_barrier(jnp.sum(attn_prob, axis=1))
        weighted = jnp.dot(to_bfloat(attn_prob).astype(jnp.float32), value_head, precision=lax.Precision.HIGHEST)
        return (to_bfloat(weighted / row_sum[:, None]), row_max + jnp.log(row_sum))
    contexts, log_totals = lax.map(query_block_step, jnp.arange(block_total, dtype=jnp.int32))
    return (contexts.reshape(TOKENS, HEAD_DIM), log_totals.reshape(TOKENS))

def backward_head(head_inputs):
    query_head, key_head, value_head, context_head, grad_head, log_total = head_inputs
    block_rows = min(TOKENS, 2048)
    block_total = TOKENS // block_rows
    score_scale = 1.0 / math.sqrt(HEAD_DIM)
    key_place = jnp.arange(TOKENS, dtype=jnp.int32)
    delta_rows = lax.optimization_barrier(jnp.sum(grad_head * context_head, axis=1))

    def query_block_step(carry, block_number):
        key_grad, value_grad = carry
        first_row = block_number * block_rows
        query_block = lax.dynamic_slice_in_dim(query_head, first_row, block_rows, 0)
        grad_block = lax.dynamic_slice_in_dim(grad_head, first_row, block_rows, 0)
        total_block = lax.dynamic_slice_in_dim(log_total, first_row, block_rows, 0)
        delta_block = lax.dynamic_slice_in_dim(delta_rows, first_row, block_rows, 0)
        scores = jnp.dot(query_block, key_head.T, precision=lax.Precision.HIGHEST) * score_scale
        query_place = first_row + jnp.arange(block_rows, dtype=jnp.int32)
        visible = query_place[:, None] >= key_place[None, :]
        attn_prob = jnp.where(visible, jnp.exp(scores - total_block[:, None]), 0.0)
        prob_grad = jnp.dot(grad_block, value_head.T, precision=lax.Precision.HIGHEST)
        score_grad = to_bfloat(attn_prob * (prob_grad - delta_block[:, None]) * score_scale).astype(jnp.float32)
        query_part = to_bfloat(jnp.dot(score_grad, key_head, precision=lax.Precision.HIGHEST))
        key_grad = key_grad + jnp.dot(score_grad.T, query_block, precision=lax.Precision.HIGHEST)
        value_grad = value_grad + jnp.dot(to_bfloat(attn_prob).astype(jnp.float32).T, grad_block, precision=lax.Precision.HIGHEST)
        return ((key_grad, value_grad), query_part)
    zero_grad = jnp.zeros((TOKENS, HEAD_DIM), jnp.float32)
    (key_grad, value_grad), query_parts = lax.scan(query_block_step, (zero_grad, zero_grad), jnp.arange(block_total, dtype=jnp.int32))
    return (query_parts.reshape(TOKENS, HEAD_DIM), to_bfloat(key_grad), to_bfloat(value_grad))

def reference(hidden_in, ln1_gain, ln1_bias, qkv_weight, qv_bias, out_weight, out_bias, ln2_gain, ln2_bias, fc_weight, fc_bias, proj_weight, proj_bias, cotangent):
    hidden_f = hidden_in.astype(jnp.float32)
    scaled_one, inverse_one, normed_one = normalize(hidden_f, ln1_gain, ln1_bias)
    normed_bf = to_bfloat(normed_one)
    weight_three = qkv_weight.astype(jnp.float32).reshape(D, 3, D)
    bias_three = jnp.stack([qv_bias[0], jnp.zeros((D,), jnp.float32), qv_bias[1]])
    projected = jnp.einsum('td,dcf->ctf', normed_bf.astype(jnp.float32), weight_three, precision=lax.Precision.HIGHEST)
    qkv_tokens = to_bfloat(projected + bias_three[:, None, :])
    head_form = qkv_tokens.astype(jnp.float32).reshape(3, TOKENS, HEADS, HEAD_DIM).transpose(0, 2, 1, 3)
    context_heads, log_total = lax.map(forward_head, (head_form[0], head_form[1], head_form[2]))
    context_tokens = context_heads.transpose(1, 0, 2).reshape(TOKENS, D)
    residual = hidden_f + jnp.dot(context_tokens, out_weight, preferred_element_type=jnp.float32) + out_bias
    scaled_two, inverse_two, normed_two = normalize(residual, ln2_gain, ln2_bias)
    normed_two_bf = to_bfloat(normed_two)
    hidden_pre = jnp.dot(normed_two_bf, fc_weight, preferred_element_type=jnp.float32) + fc_bias
    gelu_value, gelu_slope = gelu_pair(hidden_pre)
    activation = to_bfloat(gelu_value)
    mlp_out = jnp.dot(activation, proj_weight, preferred_element_type=jnp.float32)
    block_out = residual + mlp_out + proj_bias
    cot_bf = to_bfloat(cotangent)
    hidden_grad = jnp.dot(cot_bf, proj_weight.T, preferred_element_type=jnp.float32) * gelu_slope
    hidden_grad_bf = to_bfloat(hidden_grad)
    proj_weight_grad = jnp.dot(activation.T, cot_bf, preferred_element_type=jnp.float32)
    proj_bias_grad = lax.optimization_barrier(jnp.sum(cotangent, axis=0))
    fc_weight_grad = jnp.dot(normed_two_bf.T, hidden_grad_bf, preferred_element_type=jnp.float32)
    fc_bias_grad = lax.optimization_barrier(jnp.sum(hidden_grad, axis=0))
    normed_two_grad = jnp.dot(hidden_grad_bf, fc_weight.T, preferred_element_type=jnp.float32)
    ln2_gain_grad = lax.optimization_barrier(jnp.sum(normed_two_grad * scaled_two, axis=0))
    ln2_bias_grad = lax.optimization_barrier(jnp.sum(normed_two_grad, axis=0))
    residual_grad = cotangent + norm_back(normed_two_grad, scaled_two, inverse_two, ln2_gain)
    residual_grad_bf = to_bfloat(residual_grad)
    out_weight_grad = jnp.dot(context_tokens.T, residual_grad_bf, preferred_element_type=jnp.float32)
    out_bias_grad = lax.optimization_barrier(jnp.sum(residual_grad, axis=0))
    context_grad = to_bfloat(jnp.dot(residual_grad_bf, out_weight.T, preferred_element_type=jnp.float32))
    grad_heads = context_grad.astype(jnp.float32).reshape(TOKENS, HEADS, HEAD_DIM).transpose(1, 0, 2)
    query_grad, key_grad, value_grad = lax.map(backward_head, (head_form[0], head_form[1], head_form[2], context_heads.astype(jnp.float32), grad_heads, log_total))
    token_grads = jnp.stack([query_grad, key_grad, value_grad]).transpose(0, 2, 1, 3).reshape(3, TOKENS, D)
    token_grads_f = token_grads.astype(jnp.float32)
    qv_bias_grad = jnp.stack([lax.optimization_barrier(jnp.sum(token_grads_f[0], axis=0)), lax.optimization_barrier(jnp.sum(token_grads_f[2], axis=0))])
    qkv_weight_grad = jnp.einsum('td,ctf->dcf', normed_bf.astype(jnp.float32), token_grads_f, precision=lax.Precision.HIGHEST).reshape(D, 3 * D)
    normed_one_grad = jnp.einsum('ctf,dcf->td', token_grads_f, weight_three, precision=lax.Precision.HIGHEST)
    ln1_gain_grad = lax.optimization_barrier(jnp.sum(normed_one_grad * scaled_one, axis=0))
    ln1_bias_grad = lax.optimization_barrier(jnp.sum(normed_one_grad, axis=0))
    input_grad = residual_grad + norm_back(normed_one_grad, scaled_one, inverse_one, ln1_gain)
    return (block_out, input_grad, ln1_gain_grad, ln1_bias_grad, qkv_weight_grad, qv_bias_grad, out_weight_grad, out_bias_grad, ln2_gain_grad, ln2_bias_grad, fc_weight_grad, fc_bias_grad, proj_weight_grad, proj_bias_grad)
```

```python
import functools
import math

import jax
import jax.numpy as jnp
from jax import lax
from jax.experimental import pallas as pl
from jax.experimental.pallas import tpu as pltpu
from jax.sharding import PartitionSpec as P

HEAD_DIM = 64
TOKENS = 128
SEG = 8
KEY_BLOCKS = 8

epsilon = 1e-05
gelu_coef = math.sqrt(2.0 / math.pi)
masked_score = -1e30
f32, bf16 = jnp.float32, jnp.bfloat16


def normalize(matrix, norm_gain, norm_shift):
    row_mean = jnp.mean(matrix, axis=-1, keepdims=True)
    centered = matrix - row_mean
    variance = jnp.mean(centered * centered, axis=-1, keepdims=True)
    inverse = lax.rsqrt(variance + epsilon)
    scaled = centered * inverse
    return (scaled, inverse, scaled * norm_gain + norm_shift)


def norm_back(upstream_grad, scaled, inverse, norm_gain):
    weighted = upstream_grad * norm_gain
    first_mean = jnp.mean(weighted, axis=-1, keepdims=True)
    second_mean = jnp.mean(weighted * scaled, axis=-1, keepdims=True)
    return inverse * (weighted - first_mean - scaled * second_mean)


def gelu_pair(hidden_pre):
    tanh_arg = gelu_coef * (hidden_pre + 0.044715 * hidden_pre * hidden_pre * hidden_pre)
    tanh_value = jnp.tanh(tanh_arg)
    gelu_value = 0.5 * hidden_pre * (1.0 + tanh_value)
    gelu_slope = 0.5 * (1.0 + tanh_value) + 0.5 * hidden_pre * (
        1.0 - tanh_value * tanh_value
    ) * gelu_coef * (1.0 + 3.0 * 0.044715 * hidden_pre * hidden_pre)
    return (gelu_value, gelu_slope)


def dot(a, b):
    return jnp.dot(a, b, preferred_element_type=f32)


def block_diagonal(rows, scale):
    turned = rows.astype(f32).T * scale
    upper = lax.broadcasted_iota(jnp.int32, turned.shape, 0) < HEAD_DIM
    zero = jnp.zeros_like(turned)
    return jnp.concatenate(
        [jnp.where(upper, turned, zero), jnp.where(upper, zero, turned)], axis=1
    ).astype(bf16)


def heads_back(stacked):
    lower = lax.broadcasted_iota(jnp.int32, (TOKENS, TOKENS), 1) < HEAD_DIM
    return jnp.where(lower, stacked[:, :TOKENS].T, stacked[:, TOKENS:].T).astype(bf16)


def visible_keys(place, step, keys):
    key = lax.broadcasted_iota(jnp.int32, (keys, 2 * TOKENS), 0) + step * keys
    query = lax.broadcasted_iota(jnp.int32, (keys, 2 * TOKENS), 1) % TOKENS + place * TOKENS
    return key <= query


def over_queries(place, key_group, step, update, keys):
    @pl.when(step * KEY_BLOCKS <= place)
    def _():
        update(key_group, visible_keys(place, step, keys))

    later = SEG - 1 - key_group
    odd = later % 2

    @pl.when(odd == 1)
    def _():
        update(key_group + 1, None)

    def pair(index, carry):
        group = key_group + 1 + odd + 2 * index
        update(group, None)
        update(group + 1, None)
        return carry

    lax.fori_loop(0, later // 2, pair, 0)


def forward_kernel(cycle, q_ref, kv_ref, ctx_ref, lse_ref, qb, m_s, l_s, acc):
    place = lax.axis_index("blk") * lax.axis_size("tp") + lax.axis_index("tp")
    keys = KEY_BLOCKS * TOKENS
    steps = cycle // KEY_BLOCKS
    for group in range(SEG):
        qb[group] = block_diagonal(q_ref[group], 1.0 / math.sqrt(HEAD_DIM))
    m_s[...] = jnp.full(m_s.shape, masked_score, f32)
    l_s[...] = jnp.zeros(l_s.shape, f32)
    acc[...] = jnp.zeros(acc.shape, f32)

    def key_step(index, carry):
        key_group, step = index // steps, index % steps
        k = kv_ref[pl.ds(step * KEY_BLOCKS, KEY_BLOCKS), key_group, 0].reshape(keys, TOKENS)
        v_t = kv_ref[pl.ds(step * KEY_BLOCKS, KEY_BLOCKS), key_group, 1].reshape(keys, TOKENS).T

        def update(group, visible):
            s = dot(k, qb[group])
            if visible is not None:
                s = jnp.where(visible, s, masked_score)
            m_old = m_s[group]
            m_new = jnp.maximum(m_old, jnp.max(s, axis=0, keepdims=True))
            p = jnp.exp(s - m_new)
            r = jnp.exp(m_old - m_new)
            l_s[group] = l_s[group] * r + jnp.sum(p, axis=0, keepdims=True)
            acc[group] = acc[group] * r + dot(v_t, p.astype(bf16))
            m_s[group] = m_new

        over_queries(place, key_group, step, update, keys)
        return carry

    lax.fori_loop(0, SEG * steps, key_step, 0)
    for group in range(SEG):
        row_sum = l_s[group]
        ctx_ref[group] = heads_back(acc[group] / row_sum)
        lse_ref[group] = m_s[group] + jnp.log(row_sum)


def backward_kernel(cycle, q_ref, kv_ref, do_ref, ctx_ref, lse_ref, dq_ref, dkv_ref,
                    qb, dob, qb_t, dob_t, delta, dqt, dk_s, dv_s):
    place = lax.axis_index("blk") * lax.axis_size("tp") + lax.axis_index("tp")
    keys = KEY_BLOCKS * TOKENS
    steps = cycle // KEY_BLOCKS
    scale = 1.0 / math.sqrt(HEAD_DIM)
    for group in range(SEG):
        q_cols = block_diagonal(q_ref[group], scale)
        qb[group] = q_cols
        qb_t[group] = q_cols.T
        do_cols = block_diagonal(do_ref[group], 1.0)
        dob[group] = do_cols
        dob_t[group] = do_cols.T
        product = (do_ref[group].astype(f32) * ctx_ref[group].astype(f32)).T
        delta[group] = jnp.concatenate(
            [
                jnp.sum(product[:HEAD_DIM], axis=0, keepdims=True),
                jnp.sum(product[HEAD_DIM:], axis=0, keepdims=True),
            ],
            axis=1,
        )
    dqt[...] = jnp.zeros(dqt.shape, f32)

    def key_step(index, carry):
        key_group, step = index // steps, index % steps
        blocks = pl.ds(step * KEY_BLOCKS, KEY_BLOCKS)
        k = kv_ref[blocks, key_group, 0].reshape(keys, TOKENS)
        v = kv_ref[blocks, key_group, 1].reshape(keys, TOKENS)
        k_t = k.T
        dk_s[...] = jnp.zeros(dk_s.shape, f32)
        dv_s[...] = jnp.zeros(dv_s.shape, f32)

        def update(group, visible):
            p = jnp.exp(dot(k, qb[group]) - lse_ref[group])
            if visible is not None:
                p = jnp.where(visible, p, 0.0)
            dv_s[...] += dot(p.astype(bf16), dob_t[group])
            ds = (p * (dot(v, dob[group]) - delta[group])).astype(bf16)
            dk_s[...] += dot(ds, qb_t[group])
            dqt[group] += dot(k_t, ds)

        over_queries(place, key_group, step, update, keys)
        dkv_ref[blocks, key_group, 0] = dk_s[...].reshape(KEY_BLOCKS, TOKENS, TOKENS).astype(bf16)
        dkv_ref[blocks, key_group, 1] = dv_s[...].reshape(KEY_BLOCKS, TOKENS, TOKENS).astype(bf16)
        return carry

    lax.fori_loop(0, SEG * steps, key_step, 0)
    for group in range(SEG):
        dq_ref[group] = heads_back(dqt[group] * scale)


WHOLE = pl.BlockSpec(memory_space=pltpu.VMEM)


def attention_forward(queries, key_values):
    cycle = key_values.shape[0]
    return pl.pallas_call(
        functools.partial(forward_kernel, cycle),
        out_shape=(
            jax.ShapeDtypeStruct((SEG, TOKENS, TOKENS), bf16),
            jax.ShapeDtypeStruct((SEG, 1, 2 * TOKENS), f32),
        ),
        in_specs=[WHOLE] * 2,
        out_specs=(WHOLE,) * 2,
        scratch_shapes=[
            pltpu.VMEM((SEG, TOKENS, 2 * TOKENS), bf16),
            pltpu.VMEM((SEG, 1, 2 * TOKENS), f32),
            pltpu.VMEM((SEG, 1, 2 * TOKENS), f32),
            pltpu.VMEM((SEG, TOKENS, 2 * TOKENS), f32),
        ],
        compiler_params=pltpu.CompilerParams(vmem_limit_bytes=40 << 20),
        cost_estimate=pl.CostEstimate(
            flops=60_000_000_000, bytes_accessed=9 << 20, transcendentals=0
        ),
    )(queries, key_values)


def attention_backward(queries, key_values, context_grad, context, log_total):
    cycle = key_values.shape[0]
    columns = pltpu.VMEM((SEG, TOKENS, 2 * TOKENS), bf16)
    rows = pltpu.VMEM((SEG, 2 * TOKENS, TOKENS), bf16)
    return pl.pallas_call(
        functools.partial(backward_kernel, cycle),
        out_shape=(
            jax.ShapeDtypeStruct((SEG, TOKENS, TOKENS), bf16),
            jax.ShapeDtypeStruct(key_values.shape, bf16),
        ),
        in_specs=[WHOLE] * 5,
        out_specs=(WHOLE,) * 2,
        scratch_shapes=[
            columns,
            columns,
            rows,
            rows,
            pltpu.VMEM((SEG, 1, 2 * TOKENS), f32),
            pltpu.VMEM((SEG, TOKENS, 2 * TOKENS), f32),
            pltpu.VMEM((KEY_BLOCKS * TOKENS, TOKENS), f32),
            pltpu.VMEM((KEY_BLOCKS * TOKENS, TOKENS), f32),
        ],
        compiler_params=pltpu.CompilerParams(vmem_limit_bytes=48 << 20),
        cost_estimate=pl.CostEstimate(
            flops=80_000_000_000, bytes_accessed=18 << 20, transcendentals=0
        ),
    )(queries, key_values, context_grad, context, log_total)


def per_device(
    hidden_in,
    ln1_gain,
    ln1_bias,
    qkv_weight,
    qv_bias,
    out_weight,
    out_bias,
    ln2_gain,
    ln2_bias,
    fc_weight,
    fc_bias,
    proj_weight,
    proj_bias,
    cotangent,
):
    tokens, width = hidden_in.shape
    seq_count, blk_count, tp_count = (lax.axis_size(name) for name in ("seq", "blk", "tp"))
    head_cols = width // seq_count
    everywhere = ("seq", "blk", "tp")

    def to_heads(matrix):
        kinds = matrix.shape[1] // width
        parts = matrix.reshape(tokens, kinds, seq_count, head_cols).transpose(2, 1, 0, 3)
        return lax.all_to_all(parts, "seq", split_axis=0, concat_axis=0, tiled=True)

    def to_tokens(parts):
        kinds = parts.shape[1]
        moved = lax.all_to_all(parts, "seq", split_axis=0, concat_axis=0, tiled=True)
        return moved.transpose(2, 1, 0, 3).reshape(tokens, kinds * width)

    hidden_f = hidden_in.astype(f32)
    scaled_one, inverse_one, normed_one = normalize(hidden_f, ln1_gain, ln1_bias)
    normed_bf = normed_one.astype(bf16)
    qkv_bias = jnp.concatenate([qv_bias[0], jnp.zeros_like(qv_bias[0]), qv_bias[1]])
    qkv_heads = to_heads((dot(normed_bf, qkv_weight) + qkv_bias).astype(bf16))
    query_heads = qkv_heads[:, 0]
    key_values = lax.all_gather(qkv_heads[:, 1:], ("blk", "tp"), axis=0, tiled=False)
    key_values = key_values.reshape(blk_count * tp_count, SEG, 2, tokens, head_cols)

    cot_bf = cotangent.astype(bf16)
    gathered_cot = lax.all_gather(cot_bf, "tp", axis=0, tiled=True)
    normed_all = lax.all_gather(normed_bf, "seq", axis=0, tiled=True)

    context_heads, log_total = attention_forward(query_heads, key_values)
    context_tokens = to_tokens(context_heads[:, None])

    residual = hidden_f + dot(context_tokens, out_weight) + out_bias
    scaled_two, inverse_two, normed_two = normalize(residual, ln2_gain, ln2_bias)
    normed_two_bf = normed_two.astype(bf16)
    gathered_norm = lax.all_gather(normed_two_bf, "tp", axis=0, tiled=True)
    hidden_pre = dot(gathered_norm, fc_weight) + fc_bias
    gelu_value, gelu_slope = gelu_pair(hidden_pre)
    activation = gelu_value.astype(bf16)
    hidden_grad = dot(gathered_cot, proj_weight.T) * gelu_slope
    hidden_grad_bf = hidden_grad.astype(bf16)
    normed_two_grad = lax.psum_scatter(
        dot(hidden_grad_bf, fc_weight.T).astype(bf16), "tp", scatter_dimension=0, tiled=True
    ).astype(f32)
    residual_grad = cotangent + norm_back(normed_two_grad, scaled_two, inverse_two, ln2_gain)
    residual_grad_bf = residual_grad.astype(bf16)
    context_grad_heads = to_heads(dot(residual_grad_bf, out_weight.T).astype(bf16))[:, 0]

    query_grad, key_value_grad = attention_backward(
        query_heads, key_values, context_grad_heads, context_heads, log_total
    )

    mlp_out = lax.psum_scatter(
        dot(activation, proj_weight).astype(bf16), "tp", scatter_dimension=0, tiled=True
    ).astype(f32)
    block_out = residual + mlp_out + proj_bias
    wide_grads = jnp.concatenate(
        [
            jnp.einsum("td,tf->df", gathered_norm, hidden_grad_bf, preferred_element_type=f32),
            jnp.einsum("tf,td->fd", activation, gathered_cot, preferred_element_type=f32),
        ]
    ).astype(bf16)
    wide_part = lax.psum_scatter(wide_grads, ("seq", "blk"), scatter_dimension=0, tiled=True)
    wide_sum = lax.all_gather(wide_part, ("seq", "blk"), axis=0, tiled=True)
    fc_weight_grad = wide_sum[:width].astype(f32)
    proj_weight_grad = wide_sum[width:].astype(f32)
    fc_bias_grad = lax.psum(jnp.sum(hidden_grad, axis=0), ("seq", "blk"))
    residual_grad_all = lax.all_gather(residual_grad_bf, "seq", axis=0, tiled=True)
    out_part = jnp.einsum(
        "tc,td->cd",
        context_heads.reshape(SEG * tokens, head_cols),
        residual_grad_all,
        preferred_element_type=f32,
    ).astype(bf16)
    early_vectors = lax.psum(
        jnp.stack(
            [
                jnp.sum(residual_grad, axis=0),
                jnp.sum(normed_two_grad * scaled_two, axis=0),
                jnp.sum(normed_two_grad, axis=0),
                jnp.sum(cotangent, axis=0),
            ]
        ),
        everywhere,
    )

    key_value_own = lax.psum_scatter(
        key_value_grad, ("blk", "tp"), scatter_dimension=0, tiled=False
    )
    head_grads = jnp.concatenate([query_grad[:, None], key_value_own], axis=1)
    token_grads = to_tokens(head_grads)
    normed_one_grad = dot(token_grads, qkv_weight.T)
    input_grad = residual_grad + norm_back(normed_one_grad, scaled_one, inverse_one, ln1_gain)
    token_sums = jnp.sum(token_grads.astype(f32), axis=0)
    late_vectors = lax.psum(
        jnp.stack(
            [
                jnp.sum(normed_one_grad * scaled_one, axis=0),
                jnp.sum(normed_one_grad, axis=0),
                token_sums[:width],
                token_sums[2 * width :],
            ]
        ),
        everywhere,
    )
    own_row = lax.axis_index(("seq", "blk")) * (width // (seq_count * blk_count))
    own_rows = width // (seq_count * blk_count)
    early_own = lax.dynamic_slice_in_dim(early_vectors, own_row, own_rows, 1)
    late_own = lax.dynamic_slice_in_dim(late_vectors, own_row, own_rows, 1)

    fine = own_rows // tp_count
    qkv_part = jnp.einsum(
        "gtd,gktf->dkf",
        normed_all.reshape(SEG, tokens, width),
        head_grads,
        preferred_element_type=f32,
    ).astype(bf16)
    qkv_part = qkv_part.reshape(seq_count, blk_count * tp_count, fine * 3 * head_cols)
    qkv_part = qkv_part.transpose(1, 0, 2).reshape(blk_count * tp_count, -1, head_cols)
    out_rows = out_part.reshape(blk_count * tp_count, -1, head_cols)
    weight_part = lax.psum_scatter(
        jnp.concatenate([qkv_part, out_rows], axis=1).reshape(-1, head_cols),
        ("blk", "tp"),
        scatter_dimension=0,
        tiled=True,
    )
    qkv_rows = weight_part[: seq_count * fine * 3].reshape(seq_count, fine * 3, head_cols)
    qkv_rows = lax.all_to_all(qkv_rows, "seq", split_axis=0, concat_axis=0, tiled=True)
    qkv_rows = qkv_rows.reshape(seq_count, fine, 3, head_cols).transpose(1, 2, 0, 3)
    own_weight = jnp.concatenate(
        [
            qkv_rows.reshape(fine, 3 * width),
            weight_part[seq_count * fine * 3 :].reshape(fine, width),
        ],
        axis=1,
    )
    own_weight = lax.all_gather(own_weight, "tp", axis=0, tiled=True).astype(f32)
    return (
        block_out,
        input_grad,
        late_own[0],
        late_own[1],
        own_weight[:, : 3 * width],
        late_own[2:4],
        own_weight[:, 3 * width :],
        early_own[0],
        early_own[1],
        early_own[2],
        fc_weight_grad,
        fc_bias_grad,
        proj_weight_grad,
        early_own[3],
    )


def solution(mesh):
    return jax.shard_map(
        per_device,
        mesh=mesh,
        in_specs=(
            P(("seq", "blk", "tp"), None),
            P(),
            P(),
            P(),
            P(),
            P(),
            P(),
            P(),
            P(),
            P(None, "tp"),
            P("tp"),
            P("tp", None),
            P(),
            P(("seq", "blk", "tp"), None),
        ),
        out_specs=(
            P(("seq", "blk", "tp"), None),
            P(("seq", "blk", "tp"), None),
            P(("seq", "blk")),
            P(("seq", "blk")),
            P(("seq", "blk"), None),
            P(None, ("seq", "blk")),
            P(("seq", "blk"), None),
            P(("seq", "blk")),
            P(("seq", "blk")),
            P(("seq", "blk")),
            P(None, "tp"),
            P("tp"),
            P("tp", None),
            P(("seq", "blk")),
        ),
        check_vma=False,
    )
```

```python
import functools
import math

import jax
import jax.numpy as jnp
from jax import lax
from jax.experimental import pallas as pl
from jax.experimental.pallas import tpu as pltpu
from jax.sharding import Mesh
from jax.sharding import PartitionSpec as P

D = 64
T = 128
SEG = 16
CYC = 8
N = CYC * T
PAIRS = SEG // 2
HEAD_AXES = ("seq", "bh")
KEY_AXES = ("bl", "tp")
ROW_AXES = ("seq", "bh", "bl")

epsilon = 1e-05
gelu_coef = math.sqrt(2.0 / math.pi)
masked_score = -1e30
score_scale = 1.0 / math.sqrt(D)
f32, bf16 = jnp.float32, jnp.bfloat16
WHOLE = pl.BlockSpec(memory_space=pltpu.VMEM)


def normalize(matrix, norm_gain, norm_shift):
    row_mean = jnp.mean(matrix, axis=-1, keepdims=True)
    centered = matrix - row_mean
    variance = jnp.mean(centered * centered, axis=-1, keepdims=True)
    inverse = lax.rsqrt(variance + epsilon)
    scaled = centered * inverse
    return (scaled, inverse, scaled * norm_gain + norm_shift)


def norm_back(upstream_grad, scaled, inverse, norm_gain):
    weighted = upstream_grad * norm_gain
    first_mean = jnp.mean(weighted, axis=-1, keepdims=True)
    second_mean = jnp.mean(weighted * scaled, axis=-1, keepdims=True)
    return inverse * (weighted - first_mean - scaled * second_mean)


def gelu_pair(hidden_pre):
    tanh_arg = gelu_coef * (hidden_pre + 0.044715 * hidden_pre * hidden_pre * hidden_pre)
    tanh_value = jnp.tanh(tanh_arg)
    gelu_value = 0.5 * hidden_pre * (1.0 + tanh_value)
    gelu_slope = 0.5 * (1.0 + tanh_value) + 0.5 * hidden_pre * (
        1.0 - tanh_value * tanh_value
    ) * gelu_coef * (1.0 + 3.0 * 0.044715 * hidden_pre * hidden_pre)
    return (gelu_value, gelu_slope)


def dot(a, b):
    return jnp.dot(a, b, preferred_element_type=f32)


def product(spec, a, b):
    return jnp.einsum(spec, a, b, preferred_element_type=f32)


def pair_of(ref, pair):
    return jnp.concatenate([ref[2 * pair], ref[2 * pair + 1]], axis=1)


def key_place():
    return lax.axis_index("bl") * lax.axis_size("tp") + lax.axis_index("tp")


def visible_keys(group):
    key = lax.broadcasted_iota(jnp.int32, (N, 2 * T), 0) + group * N
    lane = lax.broadcasted_iota(jnp.int32, (N, 2 * T), 1)
    query = (group // 2 * 2 + lane // T) * N + key_place() * T + lane % T
    return key <= query


def over_pairs(group, update):
    own = group // 2
    update(own, visible_keys(group))

    def full(pair, carry):
        update(pair, None)
        return carry

    lax.fori_loop(own + 1, PAIRS, full, 0)


def forward_kernel(q_ref, kv_ref, ctx_ref, lse_ref, qb, m_s, l_s, acc):
    for pair in range(PAIRS):
        q = pair_of(q_ref, pair).astype(f32) * score_scale
        qb[pair] = jnp.concatenate([q, jnp.zeros_like(q)], axis=0).astype(bf16)
    m_s[...] = jnp.full(m_s.shape, masked_score, f32)
    l_s[...] = jnp.zeros(l_s.shape, f32)
    acc[...] = jnp.zeros(acc.shape, f32)

    def key_step(group, carry):
        kv = kv_ref[:, group].reshape(N, T)
        v_t = kv.T[D:]

        def update(pair, visible):
            s = dot(kv, qb[pair])
            if visible is not None:
                s = jnp.where(visible, s, masked_score)
            m_old = m_s[pair]
            m_new = jnp.maximum(m_old, jnp.max(s, axis=0, keepdims=True))
            e = jnp.exp(s - m_new)
            r = jnp.exp(m_old - m_new)
            l_s[pair] = l_s[pair] * r + jnp.sum(e, axis=0, keepdims=True)
            acc[pair] = acc[pair] * r + dot(v_t, e.astype(bf16))
            m_s[pair] = m_new

        over_pairs(group, update)
        return carry

    lax.fori_loop(0, SEG, key_step, 0)
    for pair in range(PAIRS):
        row_sum = l_s[pair]
        o = (acc[pair] / row_sum).astype(bf16)
        ctx_ref[2 * pair] = o[:, :T]
        ctx_ref[2 * pair + 1] = o[:, T:]
        lse_ref[pair] = m_s[pair] + jnp.log(row_sum)


def attention_forward(queries, key_values):
    return pl.pallas_call(
        forward_kernel,
        out_shape=(
            jax.ShapeDtypeStruct((SEG, D, T), bf16),
            jax.ShapeDtypeStruct((PAIRS, 1, 2 * T), f32),
        ),
        in_specs=[WHOLE] * 2,
        out_specs=(WHOLE,) * 2,
        scratch_shapes=[
            pltpu.VMEM((PAIRS, 2 * D, 2 * T), bf16),
            pltpu.VMEM((PAIRS, 1, 2 * T), f32),
            pltpu.VMEM((PAIRS, 1, 2 * T), f32),
            pltpu.VMEM((PAIRS, D, 2 * T), f32),
        ],
        compiler_params=pltpu.CompilerParams(vmem_limit_bytes=40 << 20),
        cost_estimate=pl.CostEstimate(
            flops=60_000_000_000, bytes_accessed=5 << 20, transcendentals=0
        ),
    )(queries, key_values)


def backward_kernel(q_ref, kv_ref, do_ref, ctx_ref, lse_ref, dq_ref, dkv_ref,
                    w, w_t, delta, dqt, dkv_s):
    for pair in range(PAIRS):
        q = pair_of(q_ref, pair).astype(f32) * score_scale
        do = pair_of(do_ref, pair).astype(f32)
        zero = jnp.zeros_like(q)
        both = jnp.concatenate(
            [jnp.concatenate([q, zero], axis=1), jnp.concatenate([zero, do], axis=1)], axis=0
        )
        w[pair] = both.astype(bf16)
        w_t[pair] = both.T.astype(bf16)
        delta[pair] = jnp.sum(do * pair_of(ctx_ref, pair).astype(f32), axis=0, keepdims=True)
    dqt[...] = jnp.zeros(dqt.shape, f32)

    def key_step(step, carry):
        group = SEG - 1 - step
        kv = kv_ref[:, group].reshape(N, T)
        k_t = kv.T[:D]
        dkv_s[...] = jnp.zeros(dkv_s.shape, f32)

        def update(pair, visible):
            e = jnp.exp(dot(kv, w[pair][:, : 2 * T]) - lse_ref[pair])
            if visible is not None:
                e = jnp.where(visible, e, 0.0)
            ds = (e * (dot(kv, w[pair][:, 2 * T :]) - delta[pair])).astype(bf16)
            dkv_s[...] += dot(jnp.concatenate([ds, e.astype(bf16)], axis=1), w_t[pair])
            dqt[pair] += dot(k_t, ds)

        over_pairs(group, update)
        dkv_ref[:, group] = dkv_s[...].reshape(CYC, T, T).astype(bf16)
        return carry

    lax.fori_loop(0, SEG, key_step, 0)
    for pair in range(PAIRS):
        d = (dqt[pair] * score_scale).astype(bf16)
        dq_ref[2 * pair] = d[:, :T]
        dq_ref[2 * pair + 1] = d[:, T:]


def attention_backward(queries, key_values, context_grad, context, log_total):
    return pl.pallas_call(
        backward_kernel,
        out_shape=(
            jax.ShapeDtypeStruct((SEG, D, T), bf16),
            jax.ShapeDtypeStruct(key_values.shape, bf16),
        ),
        in_specs=[WHOLE] * 5,
        out_specs=(WHOLE,) * 2,
        scratch_shapes=[
            pltpu.VMEM((PAIRS, T, 4 * T), bf16),
            pltpu.VMEM((PAIRS, 4 * T, T), bf16),
            pltpu.VMEM((PAIRS, 1, 2 * T), f32),
            pltpu.VMEM((PAIRS, D, 2 * T), f32),
            pltpu.VMEM((N, T), f32),
        ],
        compiler_params=pltpu.CompilerParams(vmem_limit_bytes=48 << 20),
        cost_estimate=pl.CostEstimate(
            flops=75_000_000_000, bytes_accessed=10 << 20, transcendentals=0
        ),
    )(queries, key_values, context_grad, context, log_total)


def per_device(
    hidden_in,
    ln1_gain,
    ln1_bias,
    qkv_weight,
    qv_bias,
    out_weight,
    out_bias,
    ln2_gain,
    ln2_bias,
    fc_weight,
    fc_bias,
    proj_weight,
    proj_bias,
    cotangent,
):
    tokens, width = hidden_in.shape

    def swap_heads(parts):
        return lax.all_to_all(parts, HEAD_AXES, split_axis=0, concat_axis=0, tiled=True)

    cot_bf = cotangent.astype(bf16)
    gathered_cot = lax.all_gather(cot_bf, "tp", axis=0, tiled=True)

    hidden_f = hidden_in.astype(f32)
    scaled_one, inverse_one, normed_one = normalize(hidden_f, ln1_gain, ln1_bias)
    normed_bf = normed_one.astype(bf16)
    q_t = product("td,dc->ct", normed_bf, qkv_weight[:, :width]) + qv_bias[0][:, None]
    kv = dot(normed_bf, qkv_weight[:, width:]) + jnp.concatenate(
        [jnp.zeros_like(qv_bias[1]), qv_bias[1]]
    )
    kv = kv.astype(bf16).reshape(tokens, 2, SEG, D).transpose(2, 0, 1, 3)
    sent = jnp.concatenate(
        [q_t.astype(bf16).reshape(SEG, D, tokens), kv.reshape(SEG, tokens, 2 * D)], axis=1
    )
    arrived = swap_heads(sent)
    query_t, own_kv = arrived[:, :D], arrived[:, D:]
    own_kv, gathered_cot = lax.optimization_barrier((own_kv, gathered_cot))
    key_values = lax.all_gather(own_kv, KEY_AXES, axis=0, tiled=False)
    key_values = key_values.reshape(CYC, SEG, tokens, 2 * D)
    normed_all = lax.all_gather(normed_bf, HEAD_AXES, axis=0, tiled=False)
    normed_all = normed_all.reshape(SEG, tokens, width)
    context_heads, log_total = attention_forward(query_t, key_values)
    context_heads, normed_all = lax.optimization_barrier((context_heads, normed_all))

    context_t = swap_heads(context_heads).reshape(width, tokens)
    residual = hidden_f + product("ct,cd->td", context_t, out_weight) + out_bias
    scaled_two, inverse_two, normed_two = normalize(residual, ln2_gain, ln2_bias)
    gathered_norm = lax.all_gather(normed_two.astype(bf16), "tp", axis=0, tiled=True)
    hidden_pre = dot(gathered_norm, fc_weight) + fc_bias
    gelu_value, gelu_slope = gelu_pair(hidden_pre)
    activation = gelu_value.astype(bf16)
    hidden_grad = dot(gathered_cot, proj_weight.T) * gelu_slope
    hidden_grad_bf = hidden_grad.astype(bf16)
    normed_two_grad = lax.psum_scatter(
        dot(hidden_grad_bf, fc_weight.T).astype(bf16), "tp", scatter_dimension=0, tiled=True
    ).astype(f32)
    residual_grad = cotangent + norm_back(normed_two_grad, scaled_two, inverse_two, ln2_gain)
    residual_grad_bf = residual_grad.astype(bf16)
    context_grad = product("td,cd->ct", residual_grad_bf, out_weight).astype(bf16)
    context_grad_heads = swap_heads(context_grad.reshape(SEG, D, tokens))

    wide_grads = jnp.concatenate(
        [
            product("td,tf->df", gathered_norm, hidden_grad_bf),
            product("tf,td->fd", activation, gathered_cot),
        ]
    ).astype(bf16)
    wide_part = lax.psum_scatter(wide_grads, ROW_AXES, scatter_dimension=0, tiled=True)
    wide_sum = lax.all_gather(wide_part, ROW_AXES, axis=0, tiled=True)
    fc_weight_grad = wide_sum[:width].astype(f32)
    proj_weight_grad = wide_sum[width:].astype(f32)
    mlp_out = lax.psum_scatter(
        dot(activation, proj_weight).astype(bf16), "tp", scatter_dimension=0, tiled=True
    ).astype(f32)
    block_out = residual + mlp_out + proj_bias
    bias_parts = lax.all_gather(jnp.sum(hidden_grad, axis=0).astype(bf16)[None], ROW_AXES, axis=0, tiled=True)
    fc_bias_grad = jnp.sum(bias_parts.astype(f32), axis=0)
    residual_grad_all = lax.all_gather(residual_grad_bf, HEAD_AXES, axis=0, tiled=False)
    residual_grad_all = residual_grad_all.reshape(SEG, tokens, width)

    query_grad, key_value_grad = attention_backward(
        query_t, key_values, context_grad_heads, context_heads, log_total
    )
    key_value_own = lax.psum_scatter(
        key_value_grad, KEY_AXES, scatter_dimension=0, tiled=False
    )
    head_grads = jnp.concatenate([query_grad, key_value_own.transpose(0, 2, 1)], axis=1)
    token_grads = swap_heads(head_grads).reshape(SEG, 3, D, tokens)
    token_grads = token_grads.transpose(1, 0, 2, 3).reshape(3 * width, tokens)
    normed_one_grad = product("ft,df->td", token_grads, qkv_weight)
    input_grad = residual_grad + norm_back(normed_one_grad, scaled_one, inverse_one, ln1_gain)

    fine = D // CYC
    vectors = jnp.stack(
        [
            jnp.sum(residual_grad, axis=0),
            jnp.sum(normed_two_grad * scaled_two, axis=0),
            jnp.sum(normed_two_grad, axis=0),
            jnp.sum(cotangent, axis=0),
            jnp.sum(normed_one_grad * scaled_one, axis=0),
            jnp.sum(normed_one_grad, axis=0),
        ]
    ).astype(bf16)
    count = vectors.shape[0]
    vectors = vectors.reshape(count, SEG, CYC, fine).transpose(2, 1, 0, 3)
    head_sums = jnp.sum(head_grads.astype(f32), axis=(0, 2)).astype(bf16).reshape(3, CYC, fine)
    qkv_part = product("gtd,gft->df", normed_all, head_grads).astype(bf16)
    qkv_part = qkv_part.reshape(SEG, CYC, fine * 3 * D).transpose(1, 0, 2)
    out_part = product("gct,gtd->cd", context_heads, residual_grad_all).astype(bf16)
    packed = jnp.concatenate(
        [
            qkv_part.reshape(CYC, -1),
            vectors.reshape(CYC, -1),
            out_part.reshape(CYC, -1),
            head_sums.transpose(1, 0, 2).reshape(CYC, -1),
        ],
        axis=1,
    )
    length = packed.shape[1]
    padded = -length % (16 * T)
    packed = jnp.pad(packed, ((0, 0), (0, padded)))
    summed = lax.psum_scatter(
        packed.reshape(-1, T), KEY_AXES, scatter_dimension=0, tiled=True
    ).reshape(-1)
    qkv_size, vector_size = SEG * fine * 3 * D, SEG * count * fine
    to_rows = jnp.concatenate(
        [
            summed[:qkv_size].reshape(SEG, -1),
            summed[qkv_size : qkv_size + vector_size].reshape(SEG, -1),
        ],
        axis=1,
    )
    moved = swap_heads(to_rows)
    qkv_rows = moved[:, : fine * 3 * D].reshape(SEG, fine, 3, D).transpose(1, 2, 0, 3)
    vector_rows = jnp.sum(
        moved[:, fine * 3 * D :].astype(f32).reshape(SEG, count, fine), axis=0
    ).astype(bf16)
    rest = summed[qkv_size + vector_size :]
    out_rows = rest[: fine * width].reshape(fine, width)
    bias_rows = rest[fine * width : fine * width + 3 * fine].reshape(3, fine)
    narrow = jnp.concatenate([vector_rows, bias_rows]).T
    own_rows = jnp.concatenate(
        [
            qkv_rows.reshape(fine, 3 * width),
            out_rows,
            jnp.pad(narrow, ((0, 0), (0, T - count - 3))),
        ],
        axis=1,
    )
    own_rows = lax.all_gather(own_rows, "tp", axis=0, tiled=True).astype(f32)
    narrow = own_rows[:, 4 * width :]
    return (
        block_out,
        input_grad,
        narrow[:, 4],
        narrow[:, 5],
        own_rows[:, : 3 * width],
        jnp.stack([narrow[:, count], narrow[:, count + 2]]),
        own_rows[:, 3 * width : 4 * width],
        narrow[:, 0],
        narrow[:, 1],
        narrow[:, 2],
        fc_weight_grad,
        fc_bias_grad,
        proj_weight_grad,
        narrow[:, 3],
    )


def solution(mesh):
    shape = mesh.devices.shape
    split = Mesh(
        mesh.devices.reshape(shape[0], shape[1] // 2, 2, shape[2]), ("seq", "bh", "bl", "tp")
    )
    every = P(("seq", "bh", "bl", "tp"), None)
    rows = ("seq", "bh", "bl")
    return jax.shard_map(
        per_device,
        mesh=split,
        in_specs=(
            every,
            P(),
            P(),
            P(),
            P(),
            P(),
            P(),
            P(),
            P(),
            P(None, "tp"),
            P("tp"),
            P("tp", None),
            P(),
            every,
        ),
        out_specs=(
            every,
            every,
            P(rows),
            P(rows),
            P(rows, None),
            P(None, rows),
            P(rows, None),
            P(rows),
            P(rows),
            P(rows),
            P(None, "tp"),
            P("tp"),
            P("tp", None),
            P(rows),
        ),
        check_vma=False,
    )
```

```python
import functools
import math

import jax
import jax.numpy as jnp
from jax import lax
from jax.experimental import pallas as pl
from jax.experimental.pallas import tpu as pltpu
from jax.sharding import Mesh
from jax.sharding import PartitionSpec as P

D = 64
T = 128
SEG = 16
CYC = 8
N = CYC * T
PAIRS = SEG // 2
HEAD_AXES = ("seq", "bh")
KEY_AXES = ("bl", "tp")
ROW_AXES = ("seq", "bh", "bl")

epsilon = 1e-05
gelu_coef = math.sqrt(2.0 / math.pi)
masked_score = -1e30
score_scale = 1.0 / math.sqrt(D)
f32, bf16 = jnp.float32, jnp.bfloat16
WHOLE = pl.BlockSpec(memory_space=pltpu.VMEM)


def normalize(matrix, norm_gain, norm_shift):
    row_mean = jnp.mean(matrix, axis=-1, keepdims=True)
    centered = matrix - row_mean
    variance = jnp.mean(centered * centered, axis=-1, keepdims=True)
    inverse = lax.rsqrt(variance + epsilon)
    scaled = centered * inverse
    return (scaled, inverse, scaled * norm_gain + norm_shift)


def norm_back(upstream_grad, scaled, inverse, norm_gain):
    weighted = upstream_grad * norm_gain
    first_mean = jnp.mean(weighted, axis=-1, keepdims=True)
    second_mean = jnp.mean(weighted * scaled, axis=-1, keepdims=True)
    return inverse * (weighted - first_mean - scaled * second_mean)


def gelu_pair(hidden_pre):
    tanh_arg = gelu_coef * (hidden_pre + 0.044715 * hidden_pre * hidden_pre * hidden_pre)
    tanh_value = jnp.tanh(tanh_arg)
    gelu_value = 0.5 * hidden_pre * (1.0 + tanh_value)
    gelu_slope = 0.5 * (1.0 + tanh_value) + 0.5 * hidden_pre * (
        1.0 - tanh_value * tanh_value
    ) * gelu_coef * (1.0 + 3.0 * 0.044715 * hidden_pre * hidden_pre)
    return (gelu_value, gelu_slope)


def dot(a, b):
    return jnp.dot(a, b, preferred_element_type=f32)


def product(spec, a, b):
    return jnp.einsum(spec, a, b, preferred_element_type=f32)


def pair_of(ref, pair):
    return jnp.concatenate([ref[2 * pair], ref[2 * pair + 1]], axis=1)


def key_place():
    return lax.axis_index("bl") * lax.axis_size("tp") + lax.axis_index("tp")


def visible_keys(group):
    key = lax.broadcasted_iota(jnp.int32, (N, 2 * T), 0) + group * N
    lane = lax.broadcasted_iota(jnp.int32, (N, 2 * T), 1)
    query = (group // 2 * 2 + lane // T) * N + key_place() * T + lane % T
    return key <= query


def over_pairs(group, update):
    own = group // 2
    update(own, visible_keys(group))

    def full(pair, carry):
        update(pair, None)
        return carry

    lax.fori_loop(own + 1, PAIRS, full, 0)


def group_index(axes):
    index = 0
    for name in axes:
        index = index * lax.axis_size(name) + lax.axis_index(name)
    return index


def group_device(axes, index):
    device = {}
    for name in reversed(axes):
        device[name] = index % lax.axis_size(name)
        index = index // lax.axis_size(name)
    return device


def greet(axes, count):
    me = group_index(axes)
    barrier = pltpu.get_barrier_semaphore()
    for hop in range(1, count):
        pl.semaphore_signal(
            barrier,
            inc=1,
            device_id=group_device(axes, (me + hop) % count),
            device_id_type=pl.DeviceIdType.MESH,
        )
    pl.semaphore_wait(barrier, count - 1)
    return me


def push(source, target, sems, index, axes, peer):
    send_sem, recv_sem = sems
    return pltpu.make_async_remote_copy(
        src_ref=source,
        dst_ref=target,
        send_sem=send_sem.at[index],
        recv_sem=recv_sem.at[index],
        device_id=group_device(axes, peer),
        device_id_type=pl.DeviceIdType.MESH,
    )


def exchange_kernel(axes, count, kind, x_ref, o_ref, *scratch):
    sems = scratch[-2:]
    landing = scratch[0] if kind == "reduce" else o_ref
    me = greet(axes, count)

    def block(place):
        return x_ref if kind == "gather" else x_ref.at[place]

    for hop in range(1, count):
        peer = (me + hop) % count
        push(block(peer), landing.at[me], sems, hop - 1, axes, peer).start()
    if kind != "reduce":
        landing[me] = block(me)[...]
    for hop in range(1, count):
        origin = (me - hop + count) % count
        push(block(me), landing.at[origin], sems, hop - 1, axes, origin).wait_recv()
    if kind == "reduce":
        total = block(me)[...].astype(f32)
        for hop in range(1, count):
            total += landing[(me - hop + count) % count].astype(f32)
        o_ref[...] = total.astype(o_ref.dtype)
    for hop in range(1, count):
        peer = (me + hop) % count
        push(block(peer), landing.at[me], sems, hop - 1, axes, peer).wait_send()


def exchange(x, axes, kind, collective_id, out_dtype=bf16):
    count = 1
    for name in axes:
        count *= lax.axis_size(name)
    block = x.shape if kind == "gather" else x.shape[1:]
    landing = (count,) + block
    scratch = [pltpu.SemaphoreType.DMA((count - 1,))] * 2
    if kind == "reduce":
        scratch = [pltpu.VMEM(landing, x.dtype)] + scratch
    return pl.pallas_call(
        functools.partial(exchange_kernel, axes, count, kind),
        out_shape=jax.ShapeDtypeStruct(block if kind == "reduce" else landing, out_dtype),
        in_specs=[WHOLE],
        out_specs=WHOLE,
        scratch_shapes=scratch,
        compiler_params=pltpu.CompilerParams(
            collective_id=collective_id, has_side_effects=True, vmem_limit_bytes=24 << 20
        ),
        cost_estimate=pl.CostEstimate(
            flops=12_000_000_000, bytes_accessed=4 << 20, transcendentals=0
        ),
    )(x)


FWD_CHUNK = 4
BWD_CHUNK = 2


def forward_kernel(q_ref, own_ref, ctx_ref, lse_ref, kv_ref, qb, m_s, l_s, acc, *sems):
    me = greet(KEY_AXES, CYC)

    def send(chunk, hop, place, peer):
        rows = pl.ds(chunk * FWD_CHUNK, FWD_CHUNK)
        return push(
            own_ref.at[rows], kv_ref.at[place, rows], sems, (chunk, hop - 1), KEY_AXES, peer
        )

    for chunk in range(SEG // FWD_CHUNK):
        for hop in range(1, CYC):
            send(chunk, hop, me, (me + hop) % CYC).start()
    kv_ref[me] = own_ref[...]
    for pair in range(PAIRS):
        q = pair_of(q_ref, pair).astype(f32) * score_scale
        qb[pair] = jnp.concatenate([q, jnp.zeros_like(q)], axis=0).astype(bf16)
    m_s[...] = jnp.full(m_s.shape, masked_score, f32)
    l_s[...] = jnp.zeros(l_s.shape, f32)
    acc[...] = jnp.zeros(acc.shape, f32)

    def key_step(group, carry):
        kv = kv_ref[:, group].reshape(N, T)
        v_t = kv.T[D:]

        def update(pair, visible):
            s = dot(kv, qb[pair])
            if visible is not None:
                s = jnp.where(visible, s, masked_score)
            m_old = m_s[pair]
            m_new = jnp.maximum(m_old, jnp.max(s, axis=0, keepdims=True))
            e = jnp.exp(s - m_new)
            r = jnp.exp(m_old - m_new)
            l_s[pair] = l_s[pair] * r + jnp.sum(e, axis=0, keepdims=True)
            acc[pair] = acc[pair] * r + dot(v_t, e.astype(bf16))
            m_s[pair] = m_new

        over_pairs(group, update)
        return carry

    def chunk_step(chunk, carry):
        for hop in range(1, CYC):
            origin = (me - hop + CYC) % CYC
            send(chunk, hop, origin, origin).wait_recv()
        return lax.fori_loop(chunk * FWD_CHUNK, (chunk + 1) * FWD_CHUNK, key_step, carry)

    lax.fori_loop(0, SEG // FWD_CHUNK, chunk_step, 0)
    for pair in range(PAIRS):
        row_sum = l_s[pair]
        o = (acc[pair] / row_sum).astype(bf16)
        ctx_ref[2 * pair] = o[:, :T]
        ctx_ref[2 * pair + 1] = o[:, T:]
        lse_ref[pair] = m_s[pair] + jnp.log(row_sum)
    for chunk in range(SEG // FWD_CHUNK):
        for hop in range(1, CYC):
            send(chunk, hop, me, (me + hop) % CYC).wait_send()


def attention_forward(queries, own_kv):
    return pl.pallas_call(
        forward_kernel,
        out_shape=(
            jax.ShapeDtypeStruct((SEG, D, T), bf16),
            jax.ShapeDtypeStruct((PAIRS, 1, 2 * T), f32),
            jax.ShapeDtypeStruct((CYC, SEG, T, 2 * D), bf16),
        ),
        in_specs=[WHOLE] * 2,
        out_specs=(WHOLE,) * 3,
        scratch_shapes=[
            pltpu.VMEM((PAIRS, 2 * D, 2 * T), bf16),
            pltpu.VMEM((PAIRS, 1, 2 * T), f32),
            pltpu.VMEM((PAIRS, 1, 2 * T), f32),
            pltpu.VMEM((PAIRS, D, 2 * T), f32),
        ]
        + [pltpu.SemaphoreType.DMA((SEG // FWD_CHUNK, CYC - 1))] * 2,
        compiler_params=pltpu.CompilerParams(
            collective_id=0, has_side_effects=True, vmem_limit_bytes=40 << 20
        ),
        cost_estimate=pl.CostEstimate(
            flops=70_000_000_000, bytes_accessed=5 << 20, transcendentals=0
        ),
    )(queries, own_kv)


def backward_kernel(q_ref, kv_ref, do_ref, ctx_ref, lse_ref, grad_ref,
                    w, w_t, delta, dqt, dkv_s, staged, landed, *sems):
    me = greet(KEY_AXES, CYC)

    def send(chunk, hop, place, source, peer):
        rows = pl.ds(chunk * BWD_CHUNK, BWD_CHUNK)
        return push(
            staged.at[source, rows], landed.at[place, rows], sems, (chunk, hop - 1), KEY_AXES, peer
        )

    for pair in range(PAIRS):
        q = pair_of(q_ref, pair).astype(f32) * score_scale
        do = pair_of(do_ref, pair).astype(f32)
        zero = jnp.zeros_like(q)
        both = jnp.concatenate(
            [jnp.concatenate([q, zero], axis=1), jnp.concatenate([zero, do], axis=1)], axis=0
        )
        w[pair] = both.astype(bf16)
        w_t[pair] = both.T.astype(bf16)
        delta[pair] = jnp.sum(do * pair_of(ctx_ref, pair).astype(f32), axis=0, keepdims=True)
    dqt[...] = jnp.zeros(dqt.shape, f32)

    def key_step(step, carry):
        group = SEG - 1 - step
        kv = kv_ref[:, group].reshape(N, T)
        k_t = kv.T[:D]
        dkv_s[...] = jnp.zeros(dkv_s.shape, f32)

        def update(pair, visible):
            e = jnp.exp(dot(kv, w[pair][:, : 2 * T]) - lse_ref[pair])
            if visible is not None:
                e = jnp.where(visible, e, 0.0)
            ds = (e * (dot(kv, w[pair][:, 2 * T :]) - delta[pair])).astype(bf16)
            dkv_s[...] += dot(jnp.concatenate([ds, e.astype(bf16)], axis=1), w_t[pair])
            dqt[pair] += dot(k_t, ds)

        over_pairs(group, update)
        staged[:, group] = dkv_s[...].reshape(CYC, T, T).astype(bf16)
        return carry

    chunks = SEG // BWD_CHUNK

    def chunk_step(step, carry):
        carry = lax.fori_loop(step * BWD_CHUNK, (step + 1) * BWD_CHUNK, key_step, carry)
        for hop in range(1, CYC):
            peer = (me + hop) % CYC
            send(chunks - 1 - step, hop, me, peer, peer).start()
        return carry

    lax.fori_loop(0, chunks, chunk_step, 0)
    for pair in range(PAIRS):
        d = (dqt[pair] * score_scale).astype(bf16)
        grad_ref[2 * pair, :D] = d[:, :T]
        grad_ref[2 * pair + 1, :D] = d[:, T:]

    def finish(step, carry):
        chunk = chunks - 1 - step
        for hop in range(1, CYC):
            origin = (me - hop + CYC) % CYC
            send(chunk, hop, origin, me, origin).wait_recv()
        for part in range(BWD_CHUNK):
            group = chunk * BWD_CHUNK + part
            total = staged[me, group].astype(f32)
            for hop in range(1, CYC):
                total += landed[(me - hop + CYC) % CYC, group].astype(f32)
            grad_ref[group, D:] = total.T.astype(bf16)
        return carry

    lax.fori_loop(0, chunks, finish, 0)
    for chunk in range(chunks):
        for hop in range(1, CYC):
            peer = (me + hop) % CYC
            send(chunk, hop, me, peer, peer).wait_send()


def attention_backward(queries, key_values, context_grad, context, log_total):
    return pl.pallas_call(
        backward_kernel,
        out_shape=jax.ShapeDtypeStruct((SEG, 3 * D, T), bf16),
        in_specs=[WHOLE] * 5,
        out_specs=WHOLE,
        scratch_shapes=[
            pltpu.VMEM((PAIRS, T, 4 * T), bf16),
            pltpu.VMEM((PAIRS, 4 * T, T), bf16),
            pltpu.VMEM((PAIRS, 1, 2 * T), f32),
            pltpu.VMEM((PAIRS, D, 2 * T), f32),
            pltpu.VMEM((N, T), f32),
            pltpu.VMEM((CYC, SEG, T, T), bf16),
            pltpu.VMEM((CYC, SEG, T, T), bf16),
        ]
        + [pltpu.SemaphoreType.DMA((SEG // BWD_CHUNK, CYC - 1))] * 2,
        compiler_params=pltpu.CompilerParams(
            collective_id=1, has_side_effects=True, vmem_limit_bytes=48 << 20
        ),
        cost_estimate=pl.CostEstimate(
            flops=80_000_000_000, bytes_accessed=10 << 20, transcendentals=0
        ),
    )(queries, key_values, context_grad, context, log_total)


def per_device(
    hidden_in,
    ln1_gain,
    ln1_bias,
    qkv_weight,
    qv_bias,
    out_weight,
    out_bias,
    ln2_gain,
    ln2_bias,
    fc_weight,
    fc_bias,
    proj_weight,
    proj_bias,
    cotangent,
):
    tokens, width = hidden_in.shape

    def swap_heads(parts):
        return lax.all_to_all(parts, HEAD_AXES, split_axis=0, concat_axis=0, tiled=True)

    cot_bf = cotangent.astype(bf16)
    gathered_cot = lax.all_gather(cot_bf, "tp", axis=0, tiled=True)

    hidden_f = hidden_in.astype(f32)
    scaled_one, inverse_one, normed_one = normalize(hidden_f, ln1_gain, ln1_bias)
    normed_bf = normed_one.astype(bf16)
    q_t = product("td,dc->ct", normed_bf, qkv_weight[:, :width]) + qv_bias[0][:, None]
    kv = dot(normed_bf, qkv_weight[:, width:]) + jnp.concatenate(
        [jnp.zeros_like(qv_bias[1]), qv_bias[1]]
    )
    kv = kv.astype(bf16).reshape(tokens, 2, SEG, D).transpose(2, 0, 1, 3)
    sent = jnp.concatenate(
        [q_t.astype(bf16).reshape(SEG, D, tokens), kv.reshape(SEG, tokens, 2 * D)], axis=1
    )
    arrived = swap_heads(sent)
    query_t, own_kv = arrived[:, :D], arrived[:, D:]
    own_kv, gathered_cot = lax.optimization_barrier((own_kv, gathered_cot))
    normed_all = lax.all_gather(normed_bf, HEAD_AXES, axis=0, tiled=False)
    normed_all = normed_all.reshape(SEG, tokens, width)
    context_heads, log_total, key_values = attention_forward(query_t, own_kv)
    context_heads, normed_all = lax.optimization_barrier((context_heads, normed_all))

    context_t = swap_heads(context_heads).reshape(width, tokens)
    residual = hidden_f + product("ct,cd->td", context_t, out_weight) + out_bias
    scaled_two, inverse_two, normed_two = normalize(residual, ln2_gain, ln2_bias)
    gathered_norm = exchange(normed_two.astype(bf16), ("tp",), "gather", 2)
    gathered_norm = gathered_norm.reshape(-1, width)
    hidden_pre = dot(gathered_norm, fc_weight) + fc_bias
    gelu_value, gelu_slope = gelu_pair(hidden_pre)
    activation = gelu_value.astype(bf16)
    hidden_grad = dot(gathered_cot, proj_weight.T) * gelu_slope
    hidden_grad_bf = hidden_grad.astype(bf16)
    normed_two_grad = exchange(
        dot(hidden_grad_bf, fc_weight.T).astype(bf16).reshape(-1, tokens, width), ("tp",), "reduce", 3, f32
    )
    residual_grad = cotangent + norm_back(normed_two_grad, scaled_two, inverse_two, ln2_gain)
    residual_grad_bf = residual_grad.astype(bf16)
    context_grad = product("td,cd->ct", residual_grad_bf, out_weight).astype(bf16)
    context_grad_heads = swap_heads(context_grad.reshape(SEG, D, tokens))

    wide_grads = jnp.concatenate(
        [
            product("td,tf->df", gathered_norm, hidden_grad_bf),
            product("tf,td->fd", activation, gathered_cot),
        ]
    ).astype(bf16)
    context_grad_heads, wide_grads = lax.optimization_barrier((context_grad_heads, wide_grads))
    wide_part = lax.psum_scatter(wide_grads, ROW_AXES, scatter_dimension=0, tiled=True)
    head_grads = attention_backward(
        query_t, key_values, context_grad_heads, context_heads, log_total
    )
    head_grads, wide_part, activation = lax.optimization_barrier((head_grads, wide_part, activation))

    bias_sum = jnp.sum(hidden_grad, axis=0).astype(bf16)
    bias_sum += lax.ppermute(bias_sum, "bl", [(0, 1), (1, 0)])
    riding = jnp.concatenate([residual_grad_bf, jnp.pad(bias_sum[None], ((0, 15), (0, 0)))])
    riding = lax.all_gather(riding, HEAD_AXES, axis=0, tiled=False)
    riding = riding.reshape(SEG, tokens + 16, width)
    residual_grad_all = riding[:, :tokens]
    fc_bias_grad = jnp.sum(riding[:, tokens].astype(f32), axis=0)
    wide_part, riding = lax.optimization_barrier((wide_part, riding))
    wide_sum = lax.all_gather(wide_part, ROW_AXES, axis=0, tiled=True)
    fc_weight_grad = wide_sum[:width].astype(f32)
    proj_weight_grad = wide_sum[width:].astype(f32)
    mlp_out = exchange(
        dot(activation, proj_weight).astype(bf16).reshape(-1, tokens, width), ("tp",), "reduce", 4, f32
    )
    block_out = residual + mlp_out + proj_bias

    token_grads = swap_heads(head_grads).reshape(SEG, 3, D, tokens)
    token_grads = token_grads.transpose(1, 0, 2, 3).reshape(3 * width, tokens)
    normed_one_grad = product("ft,df->td", token_grads, qkv_weight)
    input_grad = residual_grad + norm_back(normed_one_grad, scaled_one, inverse_one, ln1_gain)

    fine = D // CYC
    vectors = jnp.stack(
        [
            jnp.sum(residual_grad, axis=0),
            jnp.sum(normed_two_grad * scaled_two, axis=0),
            jnp.sum(normed_two_grad, axis=0),
            jnp.sum(cotangent, axis=0),
            jnp.sum(normed_one_grad * scaled_one, axis=0),
            jnp.sum(normed_one_grad, axis=0),
        ]
    ).astype(bf16)
    count = vectors.shape[0]
    vectors = vectors.reshape(count, SEG, CYC, fine).transpose(2, 1, 0, 3)
    head_sums = jnp.sum(head_grads.astype(f32), axis=(0, 2)).astype(bf16).reshape(3, CYC, fine)
    qkv_part = product("gtd,gft->df", normed_all, head_grads).astype(bf16)
    qkv_part = qkv_part.reshape(SEG, CYC, fine * 3 * D).transpose(1, 0, 2)
    out_part = product("gct,gtd->cd", context_heads, residual_grad_all).astype(bf16)
    packed = jnp.concatenate(
        [
            qkv_part.reshape(CYC, -1),
            vectors.reshape(CYC, -1),
            out_part.reshape(CYC, -1),
            head_sums.transpose(1, 0, 2).reshape(CYC, -1),
        ],
        axis=1,
    )
    length = packed.shape[1]
    padded = -length % (16 * T)
    packed = jnp.pad(packed, ((0, 0), (0, padded)))
    summed = exchange(packed.reshape(CYC, -1, T), KEY_AXES, "reduce", 5).reshape(-1)
    qkv_size, vector_size = SEG * fine * 3 * D, SEG * count * fine
    to_rows = jnp.concatenate(
        [
            summed[:qkv_size].reshape(SEG, -1),
            summed[qkv_size : qkv_size + vector_size].reshape(SEG, -1),
        ],
        axis=1,
    )
    moved = swap_heads(to_rows)
    qkv_rows = moved[:, : fine * 3 * D].reshape(SEG, fine, 3, D).transpose(1, 2, 0, 3)
    vector_rows = jnp.sum(
        moved[:, fine * 3 * D :].astype(f32).reshape(SEG, count, fine), axis=0
    ).astype(bf16)
    rest = summed[qkv_size + vector_size :]
    out_rows = rest[: fine * width].reshape(fine, width)
    bias_rows = rest[fine * width : fine * width + 3 * fine].reshape(3, fine)
    narrow = jnp.concatenate([vector_rows, bias_rows]).T
    own_rows = jnp.concatenate(
        [
            qkv_rows.reshape(fine, 3 * width),
            out_rows,
            jnp.pad(narrow, ((0, 0), (0, T - count - 3))),
        ],
        axis=1,
    )
    own_rows = lax.all_gather(own_rows, "tp", axis=0, tiled=True).astype(f32)
    narrow = own_rows[:, 4 * width :]
    return (
        block_out,
        input_grad,
        narrow[:, 4],
        narrow[:, 5],
        own_rows[:, : 3 * width],
        jnp.stack([narrow[:, count], narrow[:, count + 2]]),
        own_rows[:, 3 * width : 4 * width],
        narrow[:, 0],
        narrow[:, 1],
        narrow[:, 2],
        fc_weight_grad,
        fc_bias_grad,
        proj_weight_grad,
        narrow[:, 3],
    )


def solution(mesh):
    shape = mesh.devices.shape
    split = Mesh(
        mesh.devices.reshape(shape[0], shape[1] // 2, 2, shape[2]), ("seq", "bh", "bl", "tp")
    )
    every = P(("seq", "bh", "bl", "tp"), None)
    rows = ("seq", "bh", "bl")
    return jax.shard_map(
        per_device,
        mesh=split,
        in_specs=(
            every,
            P(),
            P(),
            P(),
            P(),
            P(),
            P(),
            P(),
            P(),
            P(None, "tp"),
            P("tp"),
            P("tp", None),
            P(),
            every,
        ),
        out_specs=(
            every,
            every,
            P(rows),
            P(rows),
            P(rows, None),
            P(None, rows),
            P(rows, None),
            P(rows),
            P(rows),
            P(rows),
            P(None, "tp"),
            P("tp"),
            P("tp", None),
            P(rows),
        ),
        check_vma=False,
    )
```

```python
import functools
import math

import jax
import jax.numpy as jnp
from jax import lax
from jax.experimental import pallas as pl
from jax.experimental.pallas import tpu as pltpu
from jax.sharding import Mesh
from jax.sharding import PartitionSpec as P

D = 64
T = 128
SEG = 16
CYC = 8
N = CYC * T
PAIRS = SEG // 2
HEAD_AXES = ("seq", "bh")
KEY_AXES = ("bl", "tp")
ROW_AXES = ("seq", "bh", "bl")

epsilon = 1e-05
gelu_coef = math.sqrt(2.0 / math.pi)
masked_score = -1e30
score_scale = 1.0 / math.sqrt(D)
f32, bf16 = jnp.float32, jnp.bfloat16
WHOLE = pl.BlockSpec(memory_space=pltpu.VMEM)


def normalize(matrix, norm_gain, norm_shift):
    row_mean = jnp.mean(matrix, axis=-1, keepdims=True)
    centered = matrix - row_mean
    variance = jnp.mean(centered * centered, axis=-1, keepdims=True)
    inverse = lax.rsqrt(variance + epsilon)
    scaled = centered * inverse
    return (scaled, inverse, scaled * norm_gain + norm_shift)


def norm_back(upstream_grad, scaled, inverse, norm_gain):
    weighted = upstream_grad * norm_gain
    first_mean = jnp.mean(weighted, axis=-1, keepdims=True)
    second_mean = jnp.mean(weighted * scaled, axis=-1, keepdims=True)
    return inverse * (weighted - first_mean - scaled * second_mean)


def gelu_pair(hidden_pre):
    tanh_arg = gelu_coef * (hidden_pre + 0.044715 * hidden_pre * hidden_pre * hidden_pre)
    tanh_value = jnp.tanh(tanh_arg)
    gelu_value = 0.5 * hidden_pre * (1.0 + tanh_value)
    gelu_slope = 0.5 * (1.0 + tanh_value) + 0.5 * hidden_pre * (
        1.0 - tanh_value * tanh_value
    ) * gelu_coef * (1.0 + 3.0 * 0.044715 * hidden_pre * hidden_pre)
    return (gelu_value, gelu_slope)


def dot(a, b):
    return jnp.dot(a, b, preferred_element_type=f32)


def product(spec, a, b):
    return jnp.einsum(spec, a, b, preferred_element_type=f32)


def pair_of(ref, pair):
    return jnp.concatenate([ref[2 * pair], ref[2 * pair + 1]], axis=1)


def key_place():
    return lax.axis_index("bl") * lax.axis_size("tp") + lax.axis_index("tp")


def visible_keys(group):
    key = lax.broadcasted_iota(jnp.int32, (N, 2 * T), 0) + group * N
    lane = lax.broadcasted_iota(jnp.int32, (N, 2 * T), 1)
    query = (group // 2 * 2 + lane // T) * N + key_place() * T + lane % T
    return key <= query


def over_pairs(group, update):
    own = group // 2
    update(own, visible_keys(group))

    def full(pair, carry):
        update(pair, None)
        return carry

    lax.fori_loop(own + 1, PAIRS, full, 0)


def group_index(axes):
    index = 0
    for name in axes:
        index = index * lax.axis_size(name) + lax.axis_index(name)
    return index


def group_device(axes, index):
    device = {}
    for name in reversed(axes):
        device[name] = index % lax.axis_size(name)
        index = index // lax.axis_size(name)
    return device


def size_of(axes):
    count = 1
    for name in axes:
        count *= lax.axis_size(name)
    return count


def greet(*groups):
    barrier = pltpu.get_barrier_semaphore()
    for axes in groups:
        me, count = group_index(axes), size_of(axes)
        for hop in range(1, count):
            pl.semaphore_signal(
                barrier,
                inc=1,
                device_id=group_device(axes, (me + hop) % count),
                device_id_type=pl.DeviceIdType.MESH,
            )
    pl.semaphore_wait(barrier, sum(size_of(axes) - 1 for axes in groups))


def push(source, target, sems, index, axes, peer):
    send_sem, recv_sem = sems
    return pltpu.make_async_remote_copy(
        src_ref=source,
        dst_ref=target,
        send_sem=send_sem.at[index],
        recv_sem=recv_sem.at[index],
        device_id=group_device(axes, peer),
        device_id_type=pl.DeviceIdType.MESH,
    )


class Part:
    def __init__(self, axes, kind, x, out_dtype=bf16):
        self.axes, self.kind, self.count = axes, kind, size_of(axes)
        self.block_shape = x.shape if kind == "gather" else x.shape[1:]
        self.landing = (self.count,) + self.block_shape
        reduced = kind == "reduce"
        self.out = jax.ShapeDtypeStruct(self.block_shape if reduced else self.landing, out_dtype)
        self.scratch = [pltpu.SemaphoreType.DMA((self.count - 1,))] * 2
        if reduced:
            self.scratch = [pltpu.VMEM(self.landing, x.dtype)] + self.scratch

    def bind(self, x_ref, o_ref, scratch):
        self.x_ref, self.o_ref, self.sems = x_ref, o_ref, scratch[-2:]
        self.land = scratch[0] if self.kind == "reduce" else o_ref
        self.me = group_index(self.axes)

    def block(self, place):
        if self.kind == "gather":
            return self.x_ref
        if self.kind == "spread":
            return self.x_ref.at[place // lax.axis_size("tp")]
        return self.x_ref.at[place]

    def copy(self, hop, place, peer):
        return push(self.block(peer), self.land.at[place], self.sems, hop - 1, self.axes, peer)

    def begin(self):
        for hop in range(1, self.count):
            self.copy(hop, self.me, (self.me + hop) % self.count).start()
        if self.kind != "reduce":
            self.land[self.me] = self.block(self.me)[...]

    def finish(self):
        for hop in range(1, self.count):
            origin = (self.me - hop + self.count) % self.count
            self.copy(hop, origin, origin).wait_recv()
        if self.kind == "reduce":
            total = self.block(self.me)[...].astype(f32)
            for hop in range(1, self.count):
                total += self.land[(self.me - hop + self.count) % self.count].astype(f32)
            self.o_ref[...] = total.astype(self.o_ref.dtype)
        for hop in range(1, self.count):
            self.copy(hop, self.me, (self.me + hop) % self.count).wait_send()


def bind_all(parts, inputs, outputs, scratch):
    at = 0
    for part, x_ref, o_ref in zip(parts, inputs, outputs):
        part.bind(x_ref, o_ref, scratch[at : at + len(part.scratch)])
        at += len(part.scratch)


def exchange_kernel(parts, *refs):
    n = len(parts)
    bind_all(parts, refs[:n], refs[n : 2 * n], refs[2 * n :])
    greet(*dict.fromkeys(part.axes for part in parts))
    for part in parts:
        part.begin()
    for part in parts:
        part.finish()


def exchange(collective_id, *transfers):
    parts = [Part(axes, kind, x, *dtype) for x, axes, kind, *dtype in transfers]
    result = pl.pallas_call(
        functools.partial(exchange_kernel, parts),
        out_shape=tuple(part.out for part in parts),
        in_specs=[WHOLE] * len(parts),
        out_specs=(WHOLE,) * len(parts),
        scratch_shapes=[shape for part in parts for shape in part.scratch],
        compiler_params=pltpu.CompilerParams(
            collective_id=collective_id, has_side_effects=True, vmem_limit_bytes=24 << 20
        ),
        cost_estimate=pl.CostEstimate(
            flops=12_000_000_000, bytes_accessed=4 << 20, transcendentals=0
        ),
    )(*(transfer[0] for transfer in transfers))
    return result[0] if len(transfers) == 1 else result


FWD_CHUNK = 4
BWD_CHUNK = 2


def forward_kernel(q_ref, own_ref, ctx_ref, lse_ref, kv_ref, qb, m_s, l_s, acc, *sems):
    greet(KEY_AXES)
    me = group_index(KEY_AXES)

    def send(chunk, hop, place, peer):
        rows = pl.ds(chunk * FWD_CHUNK, FWD_CHUNK)
        return push(
            own_ref.at[rows], kv_ref.at[place, rows], sems, (chunk, hop - 1), KEY_AXES, peer
        )

    for chunk in range(SEG // FWD_CHUNK):
        for hop in range(1, CYC):
            send(chunk, hop, me, (me + hop) % CYC).start()
    kv_ref[me] = own_ref[...]
    for pair in range(PAIRS):
        q = pair_of(q_ref, pair).astype(f32) * score_scale
        qb[pair] = jnp.concatenate([q, jnp.zeros_like(q)], axis=0).astype(bf16)
    m_s[...] = jnp.full(m_s.shape, masked_score, f32)
    l_s[...] = jnp.zeros(l_s.shape, f32)
    acc[...] = jnp.zeros(acc.shape, f32)

    def key_step(group, carry):
        kv = kv_ref[:, group].reshape(N, T)
        v_t = kv.T[D:]

        def update(pair, visible):
            s = dot(kv, qb[pair])
            if visible is not None:
                s = jnp.where(visible, s, masked_score)
            m_old = m_s[pair]
            m_new = jnp.maximum(m_old, jnp.max(s, axis=0, keepdims=True))
            e = jnp.exp(s - m_new)
            r = jnp.exp(m_old - m_new)
            l_s[pair] = l_s[pair] * r + jnp.sum(e, axis=0, keepdims=True)
            acc[pair] = acc[pair] * r + dot(v_t, e.astype(bf16))
            m_s[pair] = m_new

        over_pairs(group, update)
        return carry

    def chunk_step(chunk, carry):
        for hop in range(1, CYC):
            origin = (me - hop + CYC) % CYC
            send(chunk, hop, origin, origin).wait_recv()
        return lax.fori_loop(chunk * FWD_CHUNK, (chunk + 1) * FWD_CHUNK, key_step, carry)

    lax.fori_loop(0, SEG // FWD_CHUNK, chunk_step, 0)
    for pair in range(PAIRS):
        row_sum = l_s[pair]
        o = (acc[pair] / row_sum).astype(bf16)
        ctx_ref[2 * pair] = o[:, :T]
        ctx_ref[2 * pair + 1] = o[:, T:]
        lse_ref[pair] = m_s[pair] + jnp.log(row_sum)
    for chunk in range(SEG // FWD_CHUNK):
        for hop in range(1, CYC):
            send(chunk, hop, me, (me + hop) % CYC).wait_send()


def attention_forward(queries, own_kv):
    return pl.pallas_call(
        forward_kernel,
        out_shape=(
            jax.ShapeDtypeStruct((SEG, D, T), bf16),
            jax.ShapeDtypeStruct((PAIRS, 1, 2 * T), f32),
            jax.ShapeDtypeStruct((CYC, SEG, T, 2 * D), bf16),
        ),
        in_specs=[WHOLE] * 2,
        out_specs=(WHOLE,) * 3,
        scratch_shapes=[
            pltpu.VMEM((PAIRS, 2 * D, 2 * T), bf16),
            pltpu.VMEM((PAIRS, 1, 2 * T), f32),
            pltpu.VMEM((PAIRS, 1, 2 * T), f32),
            pltpu.VMEM((PAIRS, D, 2 * T), f32),
        ]
        + [pltpu.SemaphoreType.DMA((SEG // FWD_CHUNK, CYC - 1))] * 2,
        compiler_params=pltpu.CompilerParams(
            collective_id=0, has_side_effects=True, vmem_limit_bytes=40 << 20
        ),
        cost_estimate=pl.CostEstimate(
            flops=70_000_000_000, bytes_accessed=5 << 20, transcendentals=0
        ),
    )(queries, own_kv)


def backward_kernel(parts, q_ref, kv_ref, do_ref, ctx_ref, lse_ref, *refs):
    n = len(parts)
    grad_ref, w, w_t, delta, dqt, dkv_s, staged, landed, *sems = refs[n : n + 1] + refs[2 * n + 1 :]
    bind_all(parts, refs[:n], refs[n + 1 : 2 * n + 1], sems[2:])
    sems = sems[:2]
    greet(KEY_AXES)
    me = group_index(KEY_AXES)
    for part in parts:
        part.begin()

    def send(chunk, hop, place, source, peer):
        rows = pl.ds(chunk * BWD_CHUNK, BWD_CHUNK)
        return push(
            staged.at[source, rows], landed.at[place, rows], sems, (chunk, hop - 1), KEY_AXES, peer
        )

    for pair in range(PAIRS):
        q = pair_of(q_ref, pair).astype(f32) * score_scale
        do = pair_of(do_ref, pair).astype(f32)
        zero = jnp.zeros_like(q)
        both = jnp.concatenate(
            [jnp.concatenate([q, zero], axis=1), jnp.concatenate([zero, do], axis=1)], axis=0
        )
        w[pair] = both.astype(bf16)
        w_t[pair] = both.T.astype(bf16)
        delta[pair] = jnp.sum(do * pair_of(ctx_ref, pair).astype(f32), axis=0, keepdims=True)
    dqt[...] = jnp.zeros(dqt.shape, f32)

    def key_step(step, carry):
        group = SEG - 1 - step
        kv = kv_ref[:, group].reshape(N, T)
        k_t = kv.T[:D]
        dkv_s[...] = jnp.zeros(dkv_s.shape, f32)

        def update(pair, visible):
            e = jnp.exp(dot(kv, w[pair][:, : 2 * T]) - lse_ref[pair])
            if visible is not None:
                e = jnp.where(visible, e, 0.0)
            ds = (e * (dot(kv, w[pair][:, 2 * T :]) - delta[pair])).astype(bf16)
            dkv_s[...] += dot(jnp.concatenate([ds, e.astype(bf16)], axis=1), w_t[pair])
            dqt[pair] += dot(k_t, ds)

        over_pairs(group, update)
        staged[:, group] = dkv_s[...].reshape(CYC, T, T).astype(bf16)
        return carry

    chunks = SEG // BWD_CHUNK

    def chunk_step(step, carry):
        carry = lax.fori_loop(step * BWD_CHUNK, (step + 1) * BWD_CHUNK, key_step, carry)
        for hop in range(1, CYC):
            peer = (me + hop) % CYC
            send(chunks - 1 - step, hop, me, peer, peer).start()
        return carry

    lax.fori_loop(0, chunks, chunk_step, 0)
    for pair in range(PAIRS):
        d = (dqt[pair] * score_scale).astype(bf16)
        grad_ref[2 * pair, :D] = d[:, :T]
        grad_ref[2 * pair + 1, :D] = d[:, T:]

    def finish(step, carry):
        chunk = chunks - 1 - step
        for hop in range(1, CYC):
            origin = (me - hop + CYC) % CYC
            send(chunk, hop, origin, me, origin).wait_recv()
        for part in range(BWD_CHUNK):
            group = chunk * BWD_CHUNK + part
            total = staged[me, group].astype(f32)
            for hop in range(1, CYC):
                total += landed[(me - hop + CYC) % CYC, group].astype(f32)
            grad_ref[group, D:] = total.T.astype(bf16)
        return carry

    for part in parts:
        part.finish()
    lax.fori_loop(0, chunks, finish, 0)
    for chunk in range(chunks):
        for hop in range(1, CYC):
            peer = (me + hop) % CYC
            send(chunk, hop, me, peer, peer).wait_send()


def attention_backward(queries, key_values, context_grad, context, log_total, *transfers):
    parts = [Part(axes, kind, x, *dtype) for x, axes, kind, *dtype in transfers]
    return pl.pallas_call(
        functools.partial(backward_kernel, parts),
        out_shape=(jax.ShapeDtypeStruct((SEG, 3 * D, T), bf16),) + tuple(part.out for part in parts),
        in_specs=[WHOLE] * (5 + len(parts)),
        out_specs=(WHOLE,) * (1 + len(parts)),
        scratch_shapes=[
            pltpu.VMEM((PAIRS, T, 4 * T), bf16),
            pltpu.VMEM((PAIRS, 4 * T, T), bf16),
            pltpu.VMEM((PAIRS, 1, 2 * T), f32),
            pltpu.VMEM((PAIRS, D, 2 * T), f32),
            pltpu.VMEM((N, T), f32),
            pltpu.VMEM((CYC, SEG, T, T), bf16),
            pltpu.VMEM((CYC, SEG, T, T), bf16),
        ]
        + [pltpu.SemaphoreType.DMA((SEG // BWD_CHUNK, CYC - 1))] * 2
        + [shape for part in parts for shape in part.scratch],
        compiler_params=pltpu.CompilerParams(
            collective_id=1, has_side_effects=True, vmem_limit_bytes=48 << 20
        ),
        cost_estimate=pl.CostEstimate(
            flops=80_000_000_000, bytes_accessed=10 << 20, transcendentals=0
        ),
    )(queries, key_values, context_grad, context, log_total, *(x for x, *_ in transfers))


def per_device(
    hidden_in,
    ln1_gain,
    ln1_bias,
    qkv_weight,
    qv_bias,
    out_weight,
    out_bias,
    ln2_gain,
    ln2_bias,
    fc_weight,
    fc_bias,
    proj_weight,
    proj_bias,
    cotangent,
):
    tokens, width = hidden_in.shape

    def swap_heads(collective_id, parts):
        return exchange(collective_id, (parts, HEAD_AXES, "swap"))

    cot_bf = cotangent.astype(bf16)
    gathered_cot = lax.all_gather(cot_bf, "tp", axis=0, tiled=True)

    hidden_f = hidden_in.astype(f32)
    scaled_one, inverse_one, normed_one = normalize(hidden_f, ln1_gain, ln1_bias)
    normed_bf = normed_one.astype(bf16)
    q_t = product("td,dc->ct", normed_bf, qkv_weight[:, :width]) + qv_bias[0][:, None]
    kv = dot(normed_bf, qkv_weight[:, width:]) + jnp.concatenate(
        [jnp.zeros_like(qv_bias[1]), qv_bias[1]]
    )
    kv = kv.astype(bf16).reshape(tokens, 2, SEG, D).transpose(2, 0, 1, 3)
    sent = jnp.concatenate(
        [q_t.astype(bf16).reshape(SEG, D, tokens), kv.reshape(SEG, tokens, 2 * D)], axis=1
    )
    arrived = swap_heads(2, sent)
    query_t, own_kv = arrived[:, :D], arrived[:, D:]
    own_kv, gathered_cot = lax.optimization_barrier((own_kv, gathered_cot))
    normed_all = lax.all_gather(normed_bf, HEAD_AXES, axis=0, tiled=False)
    normed_all = normed_all.reshape(SEG, tokens, width)
    context_heads, log_total, key_values = attention_forward(query_t, own_kv)
    context_heads, normed_all = lax.optimization_barrier((context_heads, normed_all))

    context_t = swap_heads(3, context_heads).reshape(width, tokens)
    residual = hidden_f + product("ct,cd->td", context_t, out_weight) + out_bias
    scaled_two, inverse_two, normed_two = normalize(residual, ln2_gain, ln2_bias)
    gathered_norm = exchange(4, (normed_two.astype(bf16), ("tp",), "gather"))
    gathered_norm = gathered_norm.reshape(-1, width)
    hidden_pre = dot(gathered_norm, fc_weight) + fc_bias
    gelu_value, gelu_slope = gelu_pair(hidden_pre)
    activation = gelu_value.astype(bf16)
    hidden_grad = dot(gathered_cot, proj_weight.T) * gelu_slope
    hidden_grad_bf = hidden_grad.astype(bf16)
    wide_grads = jnp.concatenate(
        [
            product("td,tf->df", gathered_norm, hidden_grad_bf),
            product("tf,td->fd", activation, gathered_cot),
        ]
    ).astype(bf16)
    norm_parts = dot(hidden_grad_bf, fc_weight.T).astype(bf16).reshape(-1, tokens, width)
    norm_parts, wide_grads = lax.optimization_barrier((norm_parts, wide_grads))
    wide_part = lax.psum_scatter(wide_grads, ROW_AXES, scatter_dimension=0, tiled=True)
    normed_two_grad = exchange(5, (norm_parts, ("tp",), "reduce", f32))
    residual_grad = cotangent + norm_back(normed_two_grad, scaled_two, inverse_two, ln2_gain)
    residual_grad_bf = residual_grad.astype(bf16)
    context_grad = product("td,cd->ct", residual_grad_bf, out_weight).astype(bf16)
    context_grad_heads = swap_heads(6, context_grad.reshape(SEG, D, tokens))

    fine = D // CYC
    mlp_parts = dot(activation, proj_weight).astype(bf16).reshape(-1, tokens, width)
    row_groups = width // fine // 4
    context_rows = context_t.reshape(row_groups, 4, fine, tokens).transpose(1, 0, 2, 3)
    head_grads, mlp_out, grad_tokens, context_tokens = attention_backward(
        query_t,
        key_values,
        context_grad_heads,
        context_heads,
        log_total,
        (mlp_parts, ("tp",), "reduce", f32),
        (residual_grad_bf, ("tp",), "gather"),
        (context_rows.reshape(4, row_groups * fine, tokens), ("tp",), "swap"),
    )
    block_out = residual + mlp_out + proj_bias
    head_grads, wide_part = lax.optimization_barrier((head_grads, wide_part))
    wide_sum = lax.all_gather(wide_part, ROW_AXES, axis=0, tiled=True)
    fc_weight_grad = wide_sum[:width].astype(f32)
    proj_weight_grad = wide_sum[width:].astype(f32)

    out_part = product("gct,gtd->cd", context_tokens, grad_tokens).astype(bf16)
    token_grads, out_rows, bias_parts = exchange(
        7,
        (head_grads, HEAD_AXES, "swap"),
        (out_part.reshape(row_groups, fine, width), ROW_AXES, "reduce"),
        (jnp.sum(hidden_grad, axis=0).reshape(-1, T), ROW_AXES, "gather", f32),
    )
    fc_bias_grad = jnp.sum(bias_parts, axis=0).reshape(-1)
    token_grads = token_grads.reshape(SEG, 3, D, tokens).transpose(1, 0, 2, 3)
    token_grads = token_grads.reshape(3 * width, tokens)
    normed_one_grad = product("ft,df->td", token_grads, qkv_weight)
    input_grad = residual_grad + norm_back(normed_one_grad, scaled_one, inverse_one, ln1_gain)

    vectors = jnp.stack(
        [
            jnp.sum(residual_grad, axis=0),
            jnp.sum(normed_two_grad * scaled_two, axis=0),
            jnp.sum(normed_two_grad, axis=0),
            jnp.sum(cotangent, axis=0),
            jnp.sum(normed_one_grad * scaled_one, axis=0),
            jnp.sum(normed_one_grad, axis=0),
        ]
    ).astype(bf16)
    count = vectors.shape[0]
    vectors = vectors.reshape(count, SEG, CYC, fine).transpose(2, 1, 0, 3)
    head_sums = jnp.sum(head_grads.astype(f32), axis=(0, 2)).astype(bf16).reshape(3, CYC, fine)
    qkv_part = product("gtd,gft->df", normed_all, head_grads).astype(bf16)
    qkv_part = qkv_part.reshape(SEG, CYC, fine * 3 * D).transpose(1, 0, 2)
    packed = jnp.concatenate(
        [
            qkv_part.reshape(CYC, -1),
            vectors.reshape(CYC, -1),
            head_sums.transpose(1, 0, 2).reshape(CYC, -1),
        ],
        axis=1,
    )
    length = packed.shape[1]
    padded = -length % (16 * T)
    packed = jnp.pad(packed, ((0, 0), (0, padded)))
    summed = exchange(8, (packed.reshape(CYC, -1, T), KEY_AXES, "reduce")).reshape(-1)
    qkv_size, vector_size = SEG * fine * 3 * D, SEG * count * fine
    to_rows = jnp.concatenate(
        [
            summed[:qkv_size].reshape(SEG, -1),
            summed[qkv_size : qkv_size + vector_size].reshape(SEG, -1),
        ],
        axis=1,
    )
    to_rows = jnp.pad(to_rows, ((0, 0), (0, -to_rows.shape[1] % (16 * T))))
    bias_rows = summed[qkv_size + vector_size : qkv_size + vector_size + 3 * fine]
    bias_rows = jnp.pad(bias_rows.reshape(3, fine).T, ((0, 0), (0, T - 3)))
    moved, out_rows = exchange(
        9,
        (to_rows.reshape(SEG, -1, T), HEAD_AXES + ("tp",), "spread"),
        (jnp.concatenate([out_rows, bias_rows], axis=1), ("tp",), "gather"),
    )
    own_rows = 4 * fine
    moved = moved.reshape(SEG, 4, -1)
    qkv_rows = moved[:, :, : fine * 3 * D].reshape(SEG, 4, fine, 3, D).transpose(1, 2, 3, 0, 4)
    qkv_rows = qkv_rows.reshape(own_rows, 3 * width).astype(f32)
    narrow = moved[:, :, fine * 3 * D : fine * 3 * D + count * fine].astype(f32)
    narrow = jnp.sum(narrow.reshape(SEG, 4, count, fine), axis=0).transpose(1, 0, 2)
    narrow = narrow.reshape(count, own_rows)
    out_rows = out_rows.reshape(own_rows, -1).astype(f32)
    return (
        block_out,
        input_grad,
        narrow[4],
        narrow[5],
        qkv_rows,
        jnp.stack([out_rows[:, width], out_rows[:, width + 2]]),
        out_rows[:, :width],
        narrow[0],
        narrow[1],
        narrow[2],
        fc_weight_grad,
        fc_bias_grad,
        proj_weight_grad,
        narrow[3],
    )


def solution(mesh):
    shape = mesh.devices.shape
    split = Mesh(
        mesh.devices.reshape(shape[0], shape[1] // 2, 2, shape[2]), ("seq", "bh", "bl", "tp")
    )
    every = P(("seq", "bh", "bl", "tp"), None)
    rows = ("seq", "bh", "bl")
    return jax.shard_map(
        per_device,
        mesh=split,
        in_specs=(
            every,
            P(),
            P(),
            P(),
            P(),
            P(),
            P(),
            P(),
            P(),
            P(None, "tp"),
            P("tp"),
            P("tp", None),
            P(),
            every,
        ),
        out_specs=(
            every,
            every,
            P(rows),
            P(rows),
            P(rows, None),
            P(None, rows),
            P(rows, None),
            P(rows),
            P(rows),
            P(rows),
            P(None, "tp"),
            P("tp"),
            P("tp", None),
            P(rows),
        ),
        check_vma=False,
    )
```

```python
import functools
import math

import jax
import jax.numpy as jnp
from jax import lax
from jax.experimental import pallas as pl
from jax.experimental.pallas import tpu as pltpu
from jax.sharding import Mesh
from jax.sharding import PartitionSpec as P

D = 64
T = 128
SEG = 16
CYC = 8
N = CYC * T
PAIRS = SEG // 2
HEAD_AXES = ("sz", "sc", "bh")
KEY_AXES = ("bl", "tp")
ROW_AXES = ("sz", "sc", "bh", "bl")
CHIP_ROW_AXES = ("sz", "bh", "bl")

epsilon = 1e-05
gelu_coef = math.sqrt(2.0 / math.pi)
masked_score = -1e30
score_scale = 1.0 / math.sqrt(D)
f32, bf16 = jnp.float32, jnp.bfloat16
WHOLE = pl.BlockSpec(memory_space=pltpu.VMEM)


def normalize(matrix, norm_gain, norm_shift):
    row_mean = jnp.mean(matrix, axis=-1, keepdims=True)
    centered = matrix - row_mean
    variance = jnp.mean(centered * centered, axis=-1, keepdims=True)
    inverse = lax.rsqrt(variance + epsilon)
    scaled = centered * inverse
    return (scaled, inverse, scaled * norm_gain + norm_shift)


def norm_back(upstream_grad, scaled, inverse, norm_gain):
    weighted = upstream_grad * norm_gain
    first_mean = jnp.mean(weighted, axis=-1, keepdims=True)
    second_mean = jnp.mean(weighted * scaled, axis=-1, keepdims=True)
    return inverse * (weighted - first_mean - scaled * second_mean)


def gelu_pair(hidden_pre):
    tanh_arg = gelu_coef * (hidden_pre + 0.044715 * hidden_pre * hidden_pre * hidden_pre)
    tanh_value = jnp.tanh(tanh_arg)
    gelu_value = 0.5 * hidden_pre * (1.0 + tanh_value)
    gelu_slope = 0.5 * (1.0 + tanh_value) + 0.5 * hidden_pre * (
        1.0 - tanh_value * tanh_value
    ) * gelu_coef * (1.0 + 3.0 * 0.044715 * hidden_pre * hidden_pre)
    return (gelu_value, gelu_slope)


def dot(a, b):
    return jnp.dot(a, b, preferred_element_type=f32)


def product(spec, a, b):
    return jnp.einsum(spec, a, b, preferred_element_type=f32)


def pair_of(ref, pair):
    return jnp.concatenate([ref[2 * pair], ref[2 * pair + 1]], axis=1)


def key_place():
    return lax.axis_index("bl") * lax.axis_size("tp") + lax.axis_index("tp")


def visible_keys(group):
    key = lax.broadcasted_iota(jnp.int32, (N, 2 * T), 0) + group * N
    lane = lax.broadcasted_iota(jnp.int32, (N, 2 * T), 1)
    query = (group // 2 * 2 + lane // T) * N + key_place() * T + lane % T
    return key <= query


def over_pairs(group, update):
    own = group // 2
    update(own, visible_keys(group))

    def full(pair, carry):
        update(pair, None)
        return carry

    lax.fori_loop(own + 1, PAIRS, full, 0)


def group_index(axes):
    index = 0
    for name in axes:
        index = index * lax.axis_size(name) + lax.axis_index(name)
    return index


def group_device(axes, index):
    device = {}
    for name in reversed(axes):
        device[name] = index % lax.axis_size(name)
        index = index // lax.axis_size(name)
    return device


def size_of(axes):
    count = 1
    for name in axes:
        count *= lax.axis_size(name)
    return count


def greet(*groups):
    barrier = pltpu.get_barrier_semaphore()
    for axes in groups:
        me, count = group_index(axes), size_of(axes)
        for hop in range(1, count):
            pl.semaphore_signal(
                barrier,
                inc=1,
                device_id=group_device(axes, (me + hop) % count),
                device_id_type=pl.DeviceIdType.MESH,
            )
    pl.semaphore_wait(barrier, sum(size_of(axes) - 1 for axes in groups))


def push(source, target, sems, index, axes, peer):
    send_sem, recv_sem = sems
    return pltpu.make_async_remote_copy(
        src_ref=source,
        dst_ref=target,
        send_sem=send_sem.at[index],
        recv_sem=recv_sem.at[index],
        device_id=group_device(axes, peer),
        device_id_type=pl.DeviceIdType.MESH,
    )


class Part:
    def __init__(self, axes, kind, x, out_dtype=bf16):
        self.axes, self.kind, self.count = axes, kind, size_of(axes)
        self.block_shape = x.shape if kind == "gather" else x.shape[1:]
        self.landing = (self.count,) + self.block_shape
        reduced = kind == "reduce"
        self.out = jax.ShapeDtypeStruct(self.block_shape if reduced else self.landing, out_dtype)
        self.scratch = [pltpu.SemaphoreType.DMA((self.count - 1,))] * 2
        if reduced:
            self.scratch = [pltpu.VMEM(self.landing, x.dtype)] + self.scratch

    def bind(self, x_ref, o_ref, scratch):
        self.x_ref, self.o_ref, self.sems = x_ref, o_ref, scratch[-2:]
        self.land = scratch[0] if self.kind == "reduce" else o_ref
        self.me = group_index(self.axes)

    def block(self, place):
        if self.kind == "gather":
            return self.x_ref
        if self.kind == "spread":
            return self.x_ref.at[place // lax.axis_size("tp")]
        return self.x_ref.at[place]

    def copy(self, hop, place, peer):
        return push(self.block(peer), self.land.at[place], self.sems, hop - 1, self.axes, peer)

    def by_rows(self, step):
        rows = self.block_shape[0]
        if rows <= 2 * T:
            step(slice(None))
        else:

            @pl.loop(0, rows // T)
            def _(index):
                step(pl.ds(pl.multiple_of(index * T, T), T))

    def begin(self):
        for hop in range(1, self.count):
            self.copy(hop, self.me, (self.me + hop) % self.count).start()
        if self.kind != "reduce":

            def keep(rows):
                self.land[self.me, rows] = self.block(self.me)[rows]

            self.by_rows(keep)

    def finish(self):
        for hop in range(1, self.count):
            origin = (self.me - hop + self.count) % self.count
            self.copy(hop, origin, origin).wait_recv()
        if self.kind == "reduce":

            def add(rows):
                total = self.block(self.me)[rows].astype(f32)
                for hop in range(1, self.count):
                    place = (self.me - hop + self.count) % self.count
                    total += self.land[place, rows].astype(f32)
                self.o_ref[rows] = total.astype(self.o_ref.dtype)

            self.by_rows(add)
        for hop in range(1, self.count):
            self.copy(hop, self.me, (self.me + hop) % self.count).wait_send()


def bind_all(parts, inputs, outputs, scratch):
    at = 0
    for part, x_ref, o_ref in zip(parts, inputs, outputs):
        part.bind(x_ref, o_ref, scratch[at : at + len(part.scratch)])
        at += len(part.scratch)


def exchange_kernel(parts, *refs):
    n = len(parts)
    bind_all(parts, refs[:n], refs[n : 2 * n], refs[2 * n :])
    groups = list(dict.fromkeys(part.axes for part in parts))
    greet(*(axes for axes in groups if not any(set(axes) < set(other) for other in groups)))
    for part in parts:
        part.begin()
    for part in parts:
        part.finish()


def exchange(collective_id, *transfers):
    parts = [Part(axes, kind, x, *dtype) for x, axes, kind, *dtype in transfers]
    result = pl.pallas_call(
        functools.partial(exchange_kernel, parts),
        out_shape=tuple(part.out for part in parts),
        in_specs=[WHOLE] * len(parts),
        out_specs=(WHOLE,) * len(parts),
        scratch_shapes=[shape for part in parts for shape in part.scratch],
        compiler_params=pltpu.CompilerParams(
            collective_id=collective_id, has_side_effects=True, vmem_limit_bytes=24 << 20
        ),
        cost_estimate=pl.CostEstimate(
            flops=12_000_000_000, bytes_accessed=4 << 20, transcendentals=0
        ),
    )(*(transfer[0] for transfer in transfers))
    return result[0] if len(transfers) == 1 else result


FWD_CHUNK = 4
BWD_CHUNK = 2


def forward_kernel(q_ref, own_ref, ctx_ref, lse_ref, kv_ref, qb, m_s, l_s, acc, *sems):
    greet(KEY_AXES)
    me = group_index(KEY_AXES)

    def send(chunk, hop, place, peer):
        rows = pl.ds(chunk * FWD_CHUNK, FWD_CHUNK)
        return push(
            own_ref.at[rows], kv_ref.at[place, rows], sems, (chunk, hop - 1), KEY_AXES, peer
        )

    for chunk in range(SEG // FWD_CHUNK):
        for hop in range(1, CYC):
            send(chunk, hop, me, (me + hop) % CYC).start()
    kv_ref[me] = own_ref[...]
    for pair in range(PAIRS):
        q = pair_of(q_ref, pair).astype(f32) * score_scale
        qb[pair] = jnp.concatenate([q, jnp.zeros_like(q)], axis=0).astype(bf16)
    m_s[...] = jnp.full(m_s.shape, masked_score, f32)
    l_s[...] = jnp.zeros(l_s.shape, f32)
    acc[...] = jnp.zeros(acc.shape, f32)

    def key_step(group, carry):
        kv = kv_ref[:, group].reshape(N, T)
        v_t = kv.T[D:]

        def update(pair, visible):
            s = dot(kv, qb[pair])
            if visible is not None:
                s = jnp.where(visible, s, masked_score)
            m_old = m_s[pair]
            m_new = jnp.maximum(m_old, jnp.max(s, axis=0, keepdims=True))
            e = jnp.exp(s - m_new)
            r = jnp.exp(m_old - m_new)
            l_s[pair] = l_s[pair] * r + jnp.sum(e, axis=0, keepdims=True)
            acc[pair] = acc[pair] * r + dot(v_t, e.astype(bf16))
            m_s[pair] = m_new

        over_pairs(group, update)
        return carry

    def chunk_step(chunk, carry):
        for hop in range(1, CYC):
            origin = (me - hop + CYC) % CYC
            send(chunk, hop, origin, origin).wait_recv()
        return lax.fori_loop(chunk * FWD_CHUNK, (chunk + 1) * FWD_CHUNK, key_step, carry)

    lax.fori_loop(0, SEG // FWD_CHUNK, chunk_step, 0)
    for pair in range(PAIRS):
        row_sum = l_s[pair]
        o = (acc[pair] / row_sum).astype(bf16)
        ctx_ref[2 * pair] = o[:, :T]
        ctx_ref[2 * pair + 1] = o[:, T:]
        lse_ref[pair] = m_s[pair] + jnp.log(row_sum)
    for chunk in range(SEG // FWD_CHUNK):
        for hop in range(1, CYC):
            send(chunk, hop, me, (me + hop) % CYC).wait_send()


def attention_forward(queries, own_kv):
    return pl.pallas_call(
        forward_kernel,
        out_shape=(
            jax.ShapeDtypeStruct((SEG, D, T), bf16),
            jax.ShapeDtypeStruct((PAIRS, 1, 2 * T), f32),
            jax.ShapeDtypeStruct((CYC, SEG, T, 2 * D), bf16),
        ),
        in_specs=[WHOLE] * 2,
        out_specs=(WHOLE,) * 3,
        scratch_shapes=[
            pltpu.VMEM((PAIRS, 2 * D, 2 * T), bf16),
            pltpu.VMEM((PAIRS, 1, 2 * T), f32),
            pltpu.VMEM((PAIRS, 1, 2 * T), f32),
            pltpu.VMEM((PAIRS, D, 2 * T), f32),
        ]
        + [pltpu.SemaphoreType.DMA((SEG // FWD_CHUNK, CYC - 1))] * 2,
        compiler_params=pltpu.CompilerParams(
            collective_id=0, has_side_effects=True, vmem_limit_bytes=40 << 20
        ),
        cost_estimate=pl.CostEstimate(
            flops=70_000_000_000, bytes_accessed=5 << 20, transcendentals=0
        ),
    )(queries, own_kv)


def backward_kernel(parts, q_ref, kv_ref, do_ref, ctx_ref, lse_ref, *refs):
    n = len(parts)
    grad_ref, *results = refs[n - 1 : 2 * n]
    w, w_t, delta, dqt, dkv_s, staged, landed, *sems = refs[2 * n :]
    bind_all(parts, refs[: n - 1] + (grad_ref,), results, sems[2:])
    sems = sems[:2]
    greet(KEY_AXES, HEAD_AXES)
    me = group_index(KEY_AXES)
    for part in parts[:-1]:
        part.begin()

    def send(chunk, hop, place, source, peer):
        rows = pl.ds(chunk * BWD_CHUNK, BWD_CHUNK)
        return push(
            staged.at[source, rows], landed.at[place, rows], sems, (chunk, hop - 1), KEY_AXES, peer
        )

    for pair in range(PAIRS):
        q = pair_of(q_ref, pair).astype(f32) * score_scale
        do = pair_of(do_ref, pair).astype(f32)
        zero = jnp.zeros_like(q)
        both = jnp.concatenate(
            [jnp.concatenate([q, zero], axis=1), jnp.concatenate([zero, do], axis=1)], axis=0
        )
        w[pair] = both.astype(bf16)
        w_t[pair] = both.T.astype(bf16)
        delta[pair] = jnp.sum(do * pair_of(ctx_ref, pair).astype(f32), axis=0, keepdims=True)
    dqt[...] = jnp.zeros(dqt.shape, f32)

    def key_step(step, carry):
        group = SEG - 1 - step
        kv = kv_ref[:, group].reshape(N, T)
        k_t = kv.T[:D]
        dkv_s[...] = jnp.zeros(dkv_s.shape, f32)

        def update(pair, visible):
            e = jnp.exp(dot(kv, w[pair][:, : 2 * T]) - lse_ref[pair])
            if visible is not None:
                e = jnp.where(visible, e, 0.0)
            ds = (e * (dot(kv, w[pair][:, 2 * T :]) - delta[pair])).astype(bf16)
            dkv_s[...] += dot(jnp.concatenate([ds, e.astype(bf16)], axis=1), w_t[pair])
            dqt[pair] += dot(k_t, ds)

        over_pairs(group, update)
        staged[:, group] = dkv_s[...].reshape(CYC, T, T).astype(bf16)
        return carry

    chunks = SEG // BWD_CHUNK

    def chunk_step(step, carry):
        carry = lax.fori_loop(step * BWD_CHUNK, (step + 1) * BWD_CHUNK, key_step, carry)
        for hop in range(1, CYC):
            peer = (me + hop) % CYC
            send(chunks - 1 - step, hop, me, peer, peer).start()
        return carry

    lax.fori_loop(0, chunks, chunk_step, 0)
    for pair in range(PAIRS):
        d = (dqt[pair] * score_scale).astype(bf16)
        grad_ref[2 * pair, :D] = d[:, :T]
        grad_ref[2 * pair + 1, :D] = d[:, T:]

    def finish(step, carry):
        chunk = chunks - 1 - step
        for hop in range(1, CYC):
            origin = (me - hop + CYC) % CYC
            send(chunk, hop, origin, me, origin).wait_recv()
        for part in range(BWD_CHUNK):
            group = chunk * BWD_CHUNK + part
            total = staged[me, group].astype(f32)
            for hop in range(1, CYC):
                total += landed[(me - hop + CYC) % CYC, group].astype(f32)
            grad_ref[group, D:] = total.T.astype(bf16)
        return carry

    lax.fori_loop(0, chunks, finish, 0)
    parts[-1].begin()
    for part in parts:
        part.finish()
    for chunk in range(chunks):
        for hop in range(1, CYC):
            peer = (me + hop) % CYC
            send(chunk, hop, me, peer, peer).wait_send()


def attention_backward(queries, key_values, context_grad, context, log_total, *transfers):
    grads = jax.ShapeDtypeStruct((SEG, 3 * D, T), bf16)
    parts = [Part(axes, kind, x, *dtype) for x, axes, kind, *dtype in transfers]
    parts.append(Part(HEAD_AXES, "swap", grads))
    return pl.pallas_call(
        functools.partial(backward_kernel, parts),
        out_shape=(grads,) + tuple(part.out for part in parts),
        in_specs=[WHOLE] * (4 + len(parts)),
        out_specs=(WHOLE,) * (1 + len(parts)),
        scratch_shapes=[
            pltpu.VMEM((PAIRS, T, 4 * T), bf16),
            pltpu.VMEM((PAIRS, 4 * T, T), bf16),
            pltpu.VMEM((PAIRS, 1, 2 * T), f32),
            pltpu.VMEM((PAIRS, D, 2 * T), f32),
            pltpu.VMEM((N, T), f32),
            pltpu.VMEM((CYC, SEG, T, T), bf16),
            pltpu.VMEM((CYC, SEG, T, T), bf16),
        ]
        + [pltpu.SemaphoreType.DMA((SEG // BWD_CHUNK, CYC - 1))] * 2
        + [shape for part in parts for shape in part.scratch],
        compiler_params=pltpu.CompilerParams(
            collective_id=1, has_side_effects=True, vmem_limit_bytes=48 << 20
        ),
        cost_estimate=pl.CostEstimate(
            flops=80_000_000_000, bytes_accessed=10 << 20, transcendentals=0
        ),
    )(queries, key_values, context_grad, context, log_total, *(x for x, *_ in transfers))


def per_device(
    hidden_in,
    ln1_gain,
    ln1_bias,
    qkv_weight,
    qv_bias,
    out_weight,
    out_bias,
    ln2_gain,
    ln2_bias,
    fc_weight,
    fc_bias,
    proj_weight,
    proj_bias,
    cotangent,
):
    tokens, width = hidden_in.shape

    def swap_heads(collective_id, parts):
        return exchange(collective_id, (parts, HEAD_AXES, "swap"))

    cot_bf = cotangent.astype(bf16)
    gathered_cot = lax.all_gather(cot_bf, "tp", axis=0, tiled=True)

    hidden_f = hidden_in.astype(f32)
    scaled_one, inverse_one, normed_one = normalize(hidden_f, ln1_gain, ln1_bias)
    normed_bf = normed_one.astype(bf16)
    q_t = product("td,dc->ct", normed_bf, qkv_weight[:, :width]) + qv_bias[0][:, None]
    kv = dot(normed_bf, qkv_weight[:, width:]) + jnp.concatenate(
        [jnp.zeros_like(qv_bias[1]), qv_bias[1]]
    )
    kv = kv.astype(bf16).reshape(tokens, 2, SEG, D).transpose(2, 0, 1, 3)
    sent = jnp.concatenate(
        [q_t.astype(bf16).reshape(SEG, D, tokens), kv.reshape(SEG, tokens, 2 * D)], axis=1
    )
    arrived = swap_heads(2, sent)
    query_t, own_kv = arrived[:, :D], arrived[:, D:]
    own_kv, gathered_cot = lax.optimization_barrier((own_kv, gathered_cot))
    normed_core = lax.all_gather(normed_bf, ("sz", "bh"), axis=0, tiled=True)
    context_heads, log_total, key_values = attention_forward(query_t, own_kv)
    context_heads, normed_core = lax.optimization_barrier((context_heads, normed_core))

    context_t = swap_heads(3, context_heads).reshape(width, tokens)
    residual = hidden_f + product("ct,cd->td", context_t, out_weight) + out_bias
    scaled_two, inverse_two, normed_two = normalize(residual, ln2_gain, ln2_bias)
    gathered_norm = exchange(4, (normed_two.astype(bf16), ("tp",), "gather"))
    gathered_norm = gathered_norm.reshape(-1, width)
    hidden_pre = dot(gathered_norm, fc_weight) + fc_bias
    gelu_value, gelu_slope = gelu_pair(hidden_pre)
    activation = gelu_value.astype(bf16)
    hidden_grad = dot(gathered_cot, proj_weight.T) * gelu_slope
    hidden_grad_bf = hidden_grad.astype(bf16)
    wide_grads = jnp.concatenate(
        [
            product("td,tf->df", gathered_norm, hidden_grad_bf),
            product("tf,td->fd", activation, gathered_cot),
        ]
    ).astype(bf16)
    norm_parts = dot(hidden_grad_bf, fc_weight.T).astype(bf16).reshape(-1, tokens, width)
    normed_two_grad, wide_core = exchange(
        5,
        (norm_parts, ("tp",), "reduce", f32),
        (wide_grads.reshape(2, width, width), ("sc",), "reduce"),
    )
    wide_part = lax.psum_scatter(wide_core, CHIP_ROW_AXES, scatter_dimension=0, tiled=True)
    wide_core = lax.all_gather(wide_part, CHIP_ROW_AXES, axis=0, tiled=True)
    residual_grad = cotangent + norm_back(normed_two_grad, scaled_two, inverse_two, ln2_gain)
    residual_grad_bf = residual_grad.astype(bf16)
    context_grad = product("td,cd->ct", residual_grad_bf, out_weight).astype(bf16)
    context_grad_heads = swap_heads(6, context_grad.reshape(SEG, D, tokens))

    fine = D // CYC
    mlp_parts = dot(activation, proj_weight).astype(bf16).reshape(-1, tokens, width)
    row_groups = width // fine // 4
    context_rows = context_t.reshape(row_groups, 4, fine, tokens).transpose(1, 0, 2, 3)
    head_grads, mlp_out, grad_tokens, context_tokens, normed_all, token_grads = attention_backward(
        query_t,
        key_values,
        context_grad_heads,
        context_heads,
        log_total,
        (mlp_parts, ("tp",), "reduce", f32),
        (residual_grad_bf, ("tp",), "gather"),
        (context_rows.reshape(4, row_groups * fine, tokens), ("tp",), "swap"),
        (normed_core, ("sc",), "gather"),
    )
    block_out = residual + mlp_out + proj_bias
    token_grads = token_grads.reshape(SEG, 3, D, tokens).transpose(1, 0, 2, 3)
    token_grads = token_grads.reshape(3 * width, tokens)
    normed_one_grad = product("ft,df->td", token_grads, qkv_weight)
    input_grad = residual_grad + norm_back(normed_one_grad, scaled_one, inverse_one, ln1_gain)

    vectors = jnp.stack(
        [
            jnp.sum(residual_grad, axis=0),
            jnp.sum(normed_two_grad * scaled_two, axis=0),
            jnp.sum(normed_two_grad, axis=0),
            jnp.sum(cotangent, axis=0),
            jnp.sum(normed_one_grad * scaled_one, axis=0),
            jnp.sum(normed_one_grad, axis=0),
        ]
    ).astype(bf16)
    count = vectors.shape[0]
    vectors = vectors.reshape(count, SEG, CYC, fine).transpose(2, 1, 0, 3)
    head_sums = jnp.sum(head_grads.astype(f32), axis=(0, 2)).astype(bf16).reshape(3, CYC, fine)
    by_core = head_grads.reshape(-1, 2, 2, 3 * D, tokens).transpose(1, 0, 2, 3, 4)
    qkv_part = product(
        "gtd,gft->df",
        normed_all.reshape(SEG, tokens, width),
        by_core.reshape(SEG, 3 * D, tokens),
    ).astype(bf16)
    qkv_part = qkv_part.reshape(SEG, CYC, fine * 3 * D).transpose(1, 0, 2)
    packed = jnp.concatenate(
        [
            qkv_part.reshape(CYC, -1),
            vectors.reshape(CYC, -1),
            head_sums.transpose(1, 0, 2).reshape(CYC, -1),
        ],
        axis=1,
    )
    length = packed.shape[1]
    padded = -length % (16 * T)
    packed = jnp.pad(packed, ((0, 0), (0, padded)))
    out_part = product("gct,gtd->cd", context_tokens, grad_tokens).astype(bf16)
    summed, out_rows, bias_parts = exchange(
        8,
        (packed.reshape(CYC, -1, T), KEY_AXES, "reduce"),
        (out_part.reshape(row_groups, fine, width), ROW_AXES, "reduce"),
        (jnp.sum(hidden_grad, axis=0).reshape(-1, T), ROW_AXES, "gather", f32),
    )
    fc_bias_grad = jnp.sum(bias_parts, axis=0).reshape(-1)
    summed = summed.reshape(-1)
    qkv_size, vector_size = SEG * fine * 3 * D, SEG * count * fine
    to_rows = jnp.concatenate(
        [
            summed[:qkv_size].reshape(SEG, -1),
            summed[qkv_size : qkv_size + vector_size].reshape(SEG, -1),
        ],
        axis=1,
    )
    to_rows = jnp.pad(to_rows, ((0, 0), (0, -to_rows.shape[1] % (16 * T))))
    bias_rows = summed[qkv_size + vector_size : qkv_size + vector_size + 3 * fine]
    bias_rows = jnp.pad(bias_rows.reshape(3, fine).T, ((0, 0), (0, T - 3)))
    moved, out_rows, wide_sum = exchange(
        9,
        (to_rows.reshape(SEG, -1, T), HEAD_AXES + ("tp",), "spread"),
        (jnp.concatenate([out_rows, bias_rows], axis=1), ("tp",), "gather"),
        (wide_core, ("sc",), "gather"),
    )
    fc_weight_grad = wide_sum[0].astype(f32)
    proj_weight_grad = wide_sum[1].astype(f32)
    own_rows = 4 * fine
    moved = moved.reshape(SEG, 4, -1)
    qkv_rows = moved[:, :, : fine * 3 * D].reshape(SEG, 4, fine, 3, D).transpose(1, 2, 3, 0, 4)
    qkv_rows = qkv_rows.reshape(own_rows, 3 * width).astype(f32)
    narrow = moved[:, :, fine * 3 * D : fine * 3 * D + count * fine].astype(f32)
    narrow = jnp.sum(narrow.reshape(SEG, 4, count, fine), axis=0).transpose(1, 0, 2)
    narrow = narrow.reshape(count, own_rows)
    out_rows = out_rows.reshape(own_rows, -1).astype(f32)
    return (
        block_out,
        input_grad,
        narrow[4],
        narrow[5],
        qkv_rows,
        jnp.stack([out_rows[:, width], out_rows[:, width + 2]]),
        out_rows[:, :width],
        narrow[0],
        narrow[1],
        narrow[2],
        fc_weight_grad,
        fc_bias_grad,
        proj_weight_grad,
        narrow[3],
    )


def solution(mesh):
    shape = mesh.devices.shape
    split = Mesh(
        mesh.devices.reshape(shape[0] // 2, 2, shape[1] // 2, 2, shape[2]),
        ("sz", "sc", "bh", "bl", "tp"),
    )
    every = P(("sz", "sc", "bh", "bl", "tp"), None)
    rows = ("sz", "sc", "bh", "bl")
    return jax.shard_map(
        per_device,
        mesh=split,
        in_specs=(
            every,
            P(),
            P(),
            P(),
            P(),
            P(),
            P(),
            P(),
            P(),
            P(None, "tp"),
            P("tp"),
            P("tp", None),
            P(),
            every,
        ),
        out_specs=(
            every,
            every,
            P(rows),
            P(rows),
            P(rows, None),
            P(None, rows),
            P(rows, None),
            P(rows),
            P(rows),
            P(rows),
            P(None, "tp"),
            P("tp"),
            P("tp", None),
            P(rows),
        ),
        check_vma=False,
    )
```

```python
import functools
import math

import jax
import jax.numpy as jnp
from jax import lax
from jax.experimental import pallas as pl
from jax.experimental.pallas import tpu as pltpu
from jax.sharding import Mesh
from jax.sharding import PartitionSpec as P

D = 64
T = 128
SEG = 16
CYC = 8
N = CYC * T
PAIRS = SEG // 2
HEAD_AXES = ("sz", "sc", "bh")
KEY_AXES = ("bl", "tp")
ROW_AXES = ("sz", "sc", "bh", "bl")
CHIP_ROW_AXES = ("sz", "bh", "bl")

epsilon = 1e-05
gelu_coef = math.sqrt(2.0 / math.pi)
masked_score = -1e30
score_scale = 1.0 / math.sqrt(D)
f32, bf16 = jnp.float32, jnp.bfloat16
WHOLE = pl.BlockSpec(memory_space=pltpu.VMEM)


def normalize(matrix, norm_gain, norm_shift):
    row_mean = jnp.mean(matrix, axis=-1, keepdims=True)
    centered = matrix - row_mean
    variance = jnp.mean(centered * centered, axis=-1, keepdims=True)
    inverse = lax.rsqrt(variance + epsilon)
    scaled = centered * inverse
    return (scaled, inverse, scaled * norm_gain + norm_shift)


def norm_back(upstream_grad, scaled, inverse, norm_gain):
    weighted = upstream_grad * norm_gain
    first_mean = jnp.mean(weighted, axis=-1, keepdims=True)
    second_mean = jnp.mean(weighted * scaled, axis=-1, keepdims=True)
    return inverse * (weighted - first_mean - scaled * second_mean)


def gelu_pair(hidden_pre):
    tanh_arg = gelu_coef * (hidden_pre + 0.044715 * hidden_pre * hidden_pre * hidden_pre)
    tanh_value = jnp.tanh(tanh_arg)
    gelu_value = 0.5 * hidden_pre * (1.0 + tanh_value)
    gelu_slope = 0.5 * (1.0 + tanh_value) + 0.5 * hidden_pre * (
        1.0 - tanh_value * tanh_value
    ) * gelu_coef * (1.0 + 3.0 * 0.044715 * hidden_pre * hidden_pre)
    return (gelu_value, gelu_slope)


def dot(a, b):
    return jnp.dot(a, b, preferred_element_type=f32)


def product(spec, a, b):
    return jnp.einsum(spec, a, b, preferred_element_type=f32)


def pair_of(ref, pair):
    return jnp.concatenate([ref[2 * pair], ref[2 * pair + 1]], axis=1)


def key_place():
    return lax.axis_index("bl") * lax.axis_size("tp") + lax.axis_index("tp")


def visible_keys(group):
    key = lax.broadcasted_iota(jnp.int32, (N, 2 * T), 0) + group * N
    lane = lax.broadcasted_iota(jnp.int32, (N, 2 * T), 1)
    query = (group // 2 * 2 + lane // T) * N + key_place() * T + lane % T
    return key <= query


def over_pairs(group, update):
    own = group // 2
    update(own, visible_keys(group))

    def full(pair, carry):
        update(pair, None)
        return carry

    lax.fori_loop(own + 1, PAIRS, full, 0)


def group_index(axes):
    index = 0
    for name in axes:
        index = index * lax.axis_size(name) + lax.axis_index(name)
    return index


def group_device(axes, index):
    device = {}
    for name in reversed(axes):
        device[name] = index % lax.axis_size(name)
        index = index // lax.axis_size(name)
    return device


def size_of(axes):
    count = 1
    for name in axes:
        count *= lax.axis_size(name)
    return count


def greet(*groups):
    barrier = pltpu.get_barrier_semaphore()
    for axes in groups:
        me, count = group_index(axes), size_of(axes)
        for hop in range(1, count):
            pl.semaphore_signal(
                barrier,
                inc=1,
                device_id=group_device(axes, (me + hop) % count),
                device_id_type=pl.DeviceIdType.MESH,
            )
    pl.semaphore_wait(barrier, sum(size_of(axes) - 1 for axes in groups))


def push(source, target, sems, index, axes, peer):
    send_sem, recv_sem = sems
    return pltpu.make_async_remote_copy(
        src_ref=source,
        dst_ref=target,
        send_sem=send_sem.at[index],
        recv_sem=recv_sem.at[index],
        device_id=group_device(axes, peer),
        device_id_type=pl.DeviceIdType.MESH,
    )


class Part:
    def __init__(self, axes, kind, x, out_dtype=bf16):
        self.axes, self.kind, self.count = axes, kind, size_of(axes)
        self.block_shape = x.shape if kind == "gather" else x.shape[1:]
        self.landing = (self.count,) + self.block_shape
        reduced = kind == "reduce"
        self.out = jax.ShapeDtypeStruct(self.block_shape if reduced else self.landing, out_dtype)
        self.scratch = [pltpu.SemaphoreType.DMA((self.count - 1,))] * 2
        if reduced:
            self.scratch = [pltpu.VMEM(self.landing, x.dtype)] + self.scratch

    def bind(self, x_ref, o_ref, scratch):
        self.x_ref, self.o_ref, self.sems = x_ref, o_ref, scratch[-2:]
        self.land = scratch[0] if self.kind == "reduce" else o_ref
        self.me = group_index(self.axes)

    def block(self, place):
        if self.kind == "gather":
            return self.x_ref
        if self.kind == "spread":
            return self.x_ref.at[place // lax.axis_size("tp")]
        return self.x_ref.at[place]

    def copy(self, hop, place, peer):
        return push(self.block(peer), self.land.at[place], self.sems, hop - 1, self.axes, peer)

    def by_rows(self, step):
        rows = self.block_shape[0]
        if rows <= 2 * T:
            step(slice(None))
        else:

            @pl.loop(0, rows // T)
            def _(index):
                step(pl.ds(pl.multiple_of(index * T, T), T))

    def begin(self):
        for hop in range(1, self.count):
            self.copy(hop, self.me, (self.me + hop) % self.count).start()
        if self.kind != "reduce":

            def keep(rows):
                self.land[self.me, rows] = self.block(self.me)[rows]

            self.by_rows(keep)

    def finish(self):
        for hop in range(1, self.count):
            origin = (self.me - hop + self.count) % self.count
            self.copy(hop, origin, origin).wait_recv()
        if self.kind == "reduce":

            def add(rows):
                total = self.block(self.me)[rows].astype(f32)
                for hop in range(1, self.count):
                    place = (self.me - hop + self.count) % self.count
                    total += self.land[place, rows].astype(f32)
                self.o_ref[rows] = total.astype(self.o_ref.dtype)

            self.by_rows(add)
        for hop in range(1, self.count):
            self.copy(hop, self.me, (self.me + hop) % self.count).wait_send()


def bind_all(parts, inputs, outputs, scratch):
    at = 0
    for part, x_ref, o_ref in zip(parts, inputs, outputs):
        part.bind(x_ref, o_ref, scratch[at : at + len(part.scratch)])
        at += len(part.scratch)


def exchange_kernel(parts, *refs):
    n = len(parts)
    bind_all(parts, refs[:n], refs[n : 2 * n], refs[2 * n :])
    groups = list(dict.fromkeys(part.axes for part in parts))
    greet(*(axes for axes in groups if not any(set(axes) < set(other) for other in groups)))
    for part in parts:
        part.begin()
    for part in parts:
        part.finish()


def exchange(collective_id, *transfers):
    parts = [Part(axes, kind, x, *dtype) for x, axes, kind, *dtype in transfers]
    result = pl.pallas_call(
        functools.partial(exchange_kernel, parts),
        out_shape=tuple(part.out for part in parts),
        in_specs=[WHOLE] * len(parts),
        out_specs=(WHOLE,) * len(parts),
        scratch_shapes=[shape for part in parts for shape in part.scratch],
        compiler_params=pltpu.CompilerParams(
            collective_id=collective_id, has_side_effects=True, vmem_limit_bytes=24 << 20
        ),
        cost_estimate=pl.CostEstimate(
            flops=12_000_000_000, bytes_accessed=4 << 20, transcendentals=0
        ),
    )(*(transfer[0] for transfer in transfers))
    return result[0] if len(transfers) == 1 else result


FWD_CHUNK = 1
FWD_AHEAD = 3
BWD_CHUNK = 2
BWD_OTHERS = 2


def forward_kernel(q_ref, own_ref, ctx_ref, lse_ref, kv_ref, qb, m_s, l_s, acc, *sems):
    greet(KEY_AXES)
    me = group_index(KEY_AXES)

    def send(chunk, hop, place, peer):
        rows = pl.ds(chunk * FWD_CHUNK, FWD_CHUNK)
        return push(
            own_ref.at[rows], kv_ref.at[place, rows], sems, (chunk, hop - 1), KEY_AXES, peer
        )

    chunks = SEG // FWD_CHUNK

    def send_all(chunk):
        for hop in range(1, CYC):
            send(chunk, hop, me, (me + hop) % CYC).start()

    for chunk in range(FWD_AHEAD):
        send_all(chunk)
    kv_ref[me] = own_ref[...]
    for pair in range(PAIRS):
        q = pair_of(q_ref, pair).astype(f32) * score_scale
        qb[pair] = jnp.concatenate([q, jnp.zeros_like(q)], axis=0).astype(bf16)
    m_s[...] = jnp.full(m_s.shape, masked_score, f32)
    l_s[...] = jnp.zeros(l_s.shape, f32)
    acc[...] = jnp.zeros(acc.shape, f32)

    def key_step(group, carry):
        kv = kv_ref[:, group].reshape(N, T)
        v_t = kv.T[D:]

        def update(pair, visible):
            s = dot(kv, qb[pair])
            if visible is not None:
                s = jnp.where(visible, s, masked_score)
            m_old = m_s[pair]
            m_new = jnp.maximum(m_old, jnp.max(s, axis=0, keepdims=True))
            e = jnp.exp(s - m_new)
            r = jnp.exp(m_old - m_new)
            l_s[pair] = l_s[pair] * r + jnp.sum(e, axis=0, keepdims=True)
            acc[pair] = acc[pair] * r + dot(v_t, e.astype(bf16))
            m_s[pair] = m_new

        over_pairs(group, update)
        return carry

    def chunk_step(chunk, carry):
        @pl.when(chunk + FWD_AHEAD < chunks)
        def _():
            send_all(chunk + FWD_AHEAD)

        for hop in range(1, CYC):
            origin = (me - hop + CYC) % CYC
            send(chunk, hop, origin, origin).wait_recv()
        return lax.fori_loop(chunk * FWD_CHUNK, (chunk + 1) * FWD_CHUNK, key_step, carry)

    lax.fori_loop(0, chunks, chunk_step, 0)
    for pair in range(PAIRS):
        row_sum = l_s[pair]
        o = (acc[pair] / row_sum).astype(bf16)
        ctx_ref[2 * pair] = o[:, :T]
        ctx_ref[2 * pair + 1] = o[:, T:]
        lse_ref[pair] = m_s[pair] + jnp.log(row_sum)

    @pl.loop(0, chunks)
    def _(chunk):
        for hop in range(1, CYC):
            send(chunk, hop, me, (me + hop) % CYC).wait_send()


def attention_forward(queries, own_kv):
    return pl.pallas_call(
        forward_kernel,
        out_shape=(
            jax.ShapeDtypeStruct((SEG, D, T), bf16),
            jax.ShapeDtypeStruct((PAIRS, 1, 2 * T), f32),
            jax.ShapeDtypeStruct((CYC, SEG, T, 2 * D), bf16),
        ),
        in_specs=[WHOLE] * 2,
        out_specs=(WHOLE,) * 3,
        scratch_shapes=[
            pltpu.VMEM((PAIRS, 2 * D, 2 * T), bf16),
            pltpu.VMEM((PAIRS, 1, 2 * T), f32),
            pltpu.VMEM((PAIRS, 1, 2 * T), f32),
            pltpu.VMEM((PAIRS, D, 2 * T), f32),
        ]
        + [pltpu.SemaphoreType.DMA((SEG // FWD_CHUNK, CYC - 1))] * 2,
        compiler_params=pltpu.CompilerParams(
            collective_id=0, has_side_effects=True, vmem_limit_bytes=40 << 20
        ),
        cost_estimate=pl.CostEstimate(
            flops=70_000_000_000, bytes_accessed=5 << 20, transcendentals=0
        ),
    )(queries, own_kv)


def backward_kernel(parts, q_ref, kv_ref, do_ref, ctx_ref, lse_ref, *refs):
    n = len(parts)
    grad_ref, *results = refs[n - 1 : 2 * n]
    w, w_t, delta, dqt, dkv_s, staged, landed, *sems = refs[2 * n :]
    bind_all(parts, refs[: n - 1] + (grad_ref,), results, sems[2:])
    sems = sems[:2]
    greet(KEY_AXES, HEAD_AXES)
    me = group_index(KEY_AXES)

    def send(chunk, hop, place, source, peer):
        rows = pl.ds(chunk * BWD_CHUNK, BWD_CHUNK)
        return push(
            staged.at[source, rows], landed.at[place, rows], sems, (chunk, hop - 1), KEY_AXES, peer
        )

    for pair in range(PAIRS):
        q = pair_of(q_ref, pair).astype(f32) * score_scale
        do = pair_of(do_ref, pair).astype(f32)
        zero = jnp.zeros_like(q)
        both = jnp.concatenate(
            [jnp.concatenate([q, zero], axis=1), jnp.concatenate([zero, do], axis=1)], axis=0
        )
        w[pair] = both.astype(bf16)
        w_t[pair] = both.T.astype(bf16)
        delta[pair] = jnp.sum(do * pair_of(ctx_ref, pair).astype(f32), axis=0, keepdims=True)
    dqt[...] = jnp.zeros(dqt.shape, f32)

    def key_step(step, carry):
        group = SEG - 1 - step
        kv = kv_ref[:, group].reshape(N, T)
        k_t = kv.T[:D]
        dkv_s[...] = jnp.zeros(dkv_s.shape, f32)

        def update(pair, visible):
            e = jnp.exp(dot(kv, w[pair][:, : 2 * T]) - lse_ref[pair])
            if visible is not None:
                e = jnp.where(visible, e, 0.0)
            ds = (e * (dot(kv, w[pair][:, 2 * T :]) - delta[pair])).astype(bf16)
            dkv_s[...] += dot(jnp.concatenate([ds, e.astype(bf16)], axis=1), w_t[pair])
            dqt[pair] += dot(k_t, ds)

        over_pairs(group, update)
        staged[:, group] = dkv_s[...].reshape(CYC, T, T).astype(bf16)
        return carry

    chunks = SEG // BWD_CHUNK

    def chunk_step(step, carry):
        carry = lax.fori_loop(step * BWD_CHUNK, (step + 1) * BWD_CHUNK, key_step, carry)
        for hop in range(1, CYC):
            peer = (me + hop) % CYC
            send(chunks - 1 - step, hop, me, peer, peer).start()

        @pl.when(step == BWD_OTHERS)
        def _():
            for part in parts[:-1]:
                part.begin()

        return carry

    lax.fori_loop(0, chunks, chunk_step, 0)
    for pair in range(PAIRS):
        d = (dqt[pair] * score_scale).astype(bf16)
        grad_ref[2 * pair, :D] = d[:, :T]
        grad_ref[2 * pair + 1, :D] = d[:, T:]

    def finish(step, carry):
        chunk = chunks - 1 - step
        for hop in range(1, CYC):
            origin = (me - hop + CYC) % CYC
            send(chunk, hop, origin, me, origin).wait_recv()
        for part in range(BWD_CHUNK):
            group = chunk * BWD_CHUNK + part
            total = staged[me, group].astype(f32)
            for hop in range(1, CYC):
                total += landed[(me - hop + CYC) % CYC, group].astype(f32)
            grad_ref[group, D:] = total.T.astype(bf16)
        return carry

    lax.fori_loop(0, chunks, finish, 0)
    parts[-1].begin()
    for part in parts:
        part.finish()

    @pl.loop(0, chunks)
    def _(chunk):
        for hop in range(1, CYC):
            peer = (me + hop) % CYC
            send(chunk, hop, me, peer, peer).wait_send()


def attention_backward(queries, key_values, context_grad, context, log_total, *transfers):
    grads = jax.ShapeDtypeStruct((SEG, 3 * D, T), bf16)
    parts = [Part(axes, kind, x, *dtype) for x, axes, kind, *dtype in transfers]
    parts.append(Part(HEAD_AXES, "swap", grads))
    return pl.pallas_call(
        functools.partial(backward_kernel, parts),
        out_shape=(grads,) + tuple(part.out for part in parts),
        in_specs=[WHOLE] * (4 + len(parts)),
        out_specs=(WHOLE,) * (1 + len(parts)),
        scratch_shapes=[
            pltpu.VMEM((PAIRS, T, 4 * T), bf16),
            pltpu.VMEM((PAIRS, 4 * T, T), bf16),
            pltpu.VMEM((PAIRS, 1, 2 * T), f32),
            pltpu.VMEM((PAIRS, D, 2 * T), f32),
            pltpu.VMEM((N, T), f32),
            pltpu.VMEM((CYC, SEG, T, T), bf16),
            pltpu.VMEM((CYC, SEG, T, T), bf16),
        ]
        + [pltpu.SemaphoreType.DMA((SEG // BWD_CHUNK, CYC - 1))] * 2
        + [shape for part in parts for shape in part.scratch],
        compiler_params=pltpu.CompilerParams(
            collective_id=1, has_side_effects=True, vmem_limit_bytes=48 << 20
        ),
        cost_estimate=pl.CostEstimate(
            flops=80_000_000_000, bytes_accessed=10 << 20, transcendentals=0
        ),
    )(queries, key_values, context_grad, context, log_total, *(x for x, *_ in transfers))


def per_device(
    hidden_in,
    ln1_gain,
    ln1_bias,
    qkv_weight,
    qv_bias,
    out_weight,
    out_bias,
    ln2_gain,
    ln2_bias,
    fc_weight,
    fc_bias,
    proj_weight,
    proj_bias,
    cotangent,
):
    tokens, width = hidden_in.shape

    def swap_heads(collective_id, parts):
        return exchange(collective_id, (parts, HEAD_AXES, "swap"))

    cot_bf = cotangent.astype(bf16)
    gathered_cot = lax.all_gather(cot_bf, "tp", axis=0, tiled=True)

    hidden_f = hidden_in.astype(f32)
    scaled_one, inverse_one, normed_one = normalize(hidden_f, ln1_gain, ln1_bias)
    normed_bf = normed_one.astype(bf16)
    q_t = product("td,dc->ct", normed_bf, qkv_weight[:, :width]) + qv_bias[0][:, None]
    kv = dot(normed_bf, qkv_weight[:, width:]) + jnp.concatenate(
        [jnp.zeros_like(qv_bias[1]), qv_bias[1]]
    )
    kv = kv.astype(bf16).reshape(tokens, 2, SEG, D).transpose(2, 0, 1, 3)
    sent = jnp.concatenate(
        [q_t.astype(bf16).reshape(SEG, D, tokens), kv.reshape(SEG, tokens, 2 * D)], axis=1
    )
    arrived = swap_heads(2, sent)
    query_t, own_kv = arrived[:, :D], arrived[:, D:]
    own_kv, gathered_cot = lax.optimization_barrier((own_kv, gathered_cot))
    normed_core = lax.all_gather(normed_bf, ("sz", "bh"), axis=0, tiled=True)
    context_heads, log_total, key_values = attention_forward(query_t, own_kv)
    context_heads, normed_core = lax.optimization_barrier((context_heads, normed_core))

    context_t = swap_heads(3, context_heads).reshape(width, tokens)
    residual = hidden_f + product("ct,cd->td", context_t, out_weight) + out_bias
    scaled_two, inverse_two, normed_two = normalize(residual, ln2_gain, ln2_bias)
    gathered_norm = exchange(4, (normed_two.astype(bf16), ("tp",), "gather"))
    gathered_norm = gathered_norm.reshape(-1, width)
    hidden_pre = dot(gathered_norm, fc_weight) + fc_bias
    gelu_value, gelu_slope = gelu_pair(hidden_pre)
    activation = gelu_value.astype(bf16)
    hidden_grad = dot(gathered_cot, proj_weight.T) * gelu_slope
    hidden_grad_bf = hidden_grad.astype(bf16)
    wide_grads = jnp.concatenate(
        [
            product("td,tf->df", gathered_norm, hidden_grad_bf),
            product("tf,td->fd", activation, gathered_cot),
        ]
    ).astype(bf16)
    norm_parts = dot(hidden_grad_bf, fc_weight.T).astype(bf16).reshape(-1, tokens, width)
    normed_two_grad, wide_core, bias_pair = exchange(
        5,
        (norm_parts, ("tp",), "reduce", f32),
        (wide_grads.reshape(2, width, width), ("sc",), "reduce"),
        (jnp.sum(hidden_grad, axis=0).reshape(-1, T), ("bl",), "gather", f32),
    )
    wide_part = lax.psum_scatter(wide_core, CHIP_ROW_AXES, scatter_dimension=0, tiled=True)
    wide_core = lax.all_gather(wide_part, CHIP_ROW_AXES, axis=0, tiled=True)
    residual_grad = cotangent + norm_back(normed_two_grad, scaled_two, inverse_two, ln2_gain)
    residual_grad_bf = residual_grad.astype(bf16)
    context_grad = product("td,cd->ct", residual_grad_bf, out_weight).astype(bf16)
    context_grad_heads = swap_heads(6, context_grad.reshape(SEG, D, tokens))

    fine = D // CYC
    mlp_parts = dot(activation, proj_weight).astype(bf16).reshape(-1, tokens, width)
    row_groups = width // fine // 4
    context_rows = context_t.reshape(row_groups, 4, fine, tokens).transpose(1, 0, 2, 3)
    (
        head_grads,
        mlp_out,
        grad_tokens,
        context_tokens,
        normed_all,
        bias_parts,
        token_grads,
    ) = attention_backward(
        query_t,
        key_values,
        context_grad_heads,
        context_heads,
        log_total,
        (mlp_parts, ("tp",), "reduce", f32),
        (residual_grad_bf, ("tp",), "gather"),
        (context_rows.reshape(4, row_groups * fine, tokens), ("tp",), "swap"),
        (normed_core, ("sc",), "gather"),
        (jnp.sum(bias_pair, axis=0), HEAD_AXES, "gather", f32),
    )
    block_out = residual + mlp_out + proj_bias
    token_grads = token_grads.reshape(SEG, 3, D, tokens).transpose(1, 0, 2, 3)
    token_grads = token_grads.reshape(3 * width, tokens)
    normed_one_grad = product("ft,df->td", token_grads, qkv_weight)
    input_grad = residual_grad + norm_back(normed_one_grad, scaled_one, inverse_one, ln1_gain)

    vectors = jnp.stack(
        [
            jnp.sum(residual_grad, axis=0),
            jnp.sum(normed_two_grad * scaled_two, axis=0),
            jnp.sum(normed_two_grad, axis=0),
            jnp.sum(cotangent, axis=0),
            jnp.sum(normed_one_grad * scaled_one, axis=0),
            jnp.sum(normed_one_grad, axis=0),
        ]
    ).astype(bf16)
    vectors = vectors.reshape(-1, SEG, CYC, fine).transpose(2, 1, 0, 3)
    head_sums = jnp.sum(head_grads.astype(f32), axis=(0, 2)).astype(bf16).reshape(3, CYC, fine)
    own_head = jnp.arange(SEG)[None, :, None, None] == group_index(HEAD_AXES)
    head_sums = jnp.where(own_head, head_sums.transpose(1, 0, 2)[:, None], 0)
    narrow = jnp.concatenate([vectors, head_sums], axis=2)
    count = narrow.shape[2]
    narrow = narrow.reshape(CYC, SEG, 1, count * fine)
    by_core = head_grads.reshape(-1, 2, 2, 3 * D, tokens).transpose(1, 0, 2, 3, 4)
    qkv_part = product(
        "gtd,gft->df",
        normed_all.reshape(SEG, tokens, width),
        by_core.reshape(SEG, 3 * D, tokens),
    ).astype(bf16)
    qkv_lines = fine * 3 * D // T
    qkv_part = qkv_part.reshape(SEG, CYC, qkv_lines, T).transpose(1, 0, 2, 3)
    packed = jnp.concatenate(
        [qkv_part, jnp.pad(narrow, ((0, 0), (0, 0), (0, 15 - qkv_lines), (0, T - count * fine)))],
        axis=2,
    )
    out_part = product("gct,gtd->cd", context_tokens, grad_tokens).astype(bf16)
    summed, out_rows = exchange(
        7,
        (packed, KEY_AXES, "reduce"),
        (out_part.reshape(row_groups, fine, width), ROW_AXES, "reduce"),
    )
    fc_bias_grad = jnp.sum(bias_parts, axis=0).reshape(-1)
    moved, out_rows, wide_sum = exchange(
        8,
        (summed, HEAD_AXES + ("tp",), "spread"),
        (out_rows, ("tp",), "gather"),
        (wide_core, ("sc",), "gather"),
    )
    fc_weight_grad = wide_sum[0].astype(f32)
    proj_weight_grad = wide_sum[1].astype(f32)
    own_rows = 4 * fine
    moved = moved.reshape(SEG, 4, -1, T)
    qkv_rows = moved[:, :, :qkv_lines].reshape(SEG, 4, fine, 3, D).transpose(1, 2, 3, 0, 4)
    qkv_rows = qkv_rows.reshape(own_rows, 3 * width).astype(f32)
    narrow = jnp.sum(moved[:, :, qkv_lines, : count * fine].astype(f32), axis=0)
    narrow = narrow.reshape(4, count, fine).transpose(1, 0, 2).reshape(count, own_rows)
    out_rows = out_rows.reshape(own_rows, width).astype(f32)
    return (
        block_out,
        input_grad,
        narrow[4],
        narrow[5],
        qkv_rows,
        jnp.stack([narrow[6], narrow[8]]),
        out_rows,
        narrow[0],
        narrow[1],
        narrow[2],
        fc_weight_grad,
        fc_bias_grad,
        proj_weight_grad,
        narrow[3],
    )


def solution(mesh):
    shape = mesh.devices.shape
    split = Mesh(
        mesh.devices.reshape(shape[0] // 2, 2, shape[1] // 2, 2, shape[2]),
        ("sz", "sc", "bh", "bl", "tp"),
    )
    every = P(("sz", "sc", "bh", "bl", "tp"), None)
    rows = ("sz", "sc", "bh", "bl")
    return jax.shard_map(
        per_device,
        mesh=split,
        in_specs=(
            every,
            P(),
            P(),
            P(),
            P(),
            P(),
            P(),
            P(),
            P(),
            P(None, "tp"),
            P("tp"),
            P("tp", None),
            P(),
            every,
        ),
        out_specs=(
            every,
            every,
            P(rows),
            P(rows),
            P(rows, None),
            P(None, rows),
            P(rows, None),
            P(rows),
            P(rows),
            P(rows),
            P(None, "tp"),
            P("tp"),
            P("tp", None),
            P(rows),
        ),
        check_vma=False,
    )
```

```python
import functools
import math

import jax
import jax.numpy as jnp
from jax import lax
from jax.experimental import pallas as pl
from jax.experimental.pallas import tpu as pltpu
from jax.sharding import Mesh
from jax.sharding import PartitionSpec as P

D = 64
T = 128
SEG = 16
CYC = 8
N = CYC * T
PAIRS = SEG // 2
HEAD_AXES = ("sz", "sc", "bh")
KEY_AXES = ("bl", "tp")
ROW_AXES = ("sz", "sc", "bh", "bl")
CHIP_ROW_AXES = ("sz", "bh", "bl")

epsilon = 1e-05
gelu_coef = math.sqrt(2.0 / math.pi)
masked_score = -1e30
score_scale = 1.0 / math.sqrt(D)
f32, bf16 = jnp.float32, jnp.bfloat16
WHOLE = pl.BlockSpec(memory_space=pltpu.VMEM)


def normalize(matrix, norm_gain, norm_shift):
    row_mean = jnp.mean(matrix, axis=-1, keepdims=True)
    centered = matrix - row_mean
    variance = jnp.mean(centered * centered, axis=-1, keepdims=True)
    inverse = lax.rsqrt(variance + epsilon)
    scaled = centered * inverse
    return (scaled, inverse, scaled * norm_gain + norm_shift)


def norm_back(upstream_grad, scaled, inverse, norm_gain):
    weighted = upstream_grad * norm_gain
    first_mean = jnp.mean(weighted, axis=-1, keepdims=True)
    second_mean = jnp.mean(weighted * scaled, axis=-1, keepdims=True)
    return inverse * (weighted - first_mean - scaled * second_mean)


def gelu_pair(hidden_pre):
    tanh_arg = gelu_coef * (hidden_pre + 0.044715 * hidden_pre * hidden_pre * hidden_pre)
    tanh_value = jnp.tanh(tanh_arg)
    gelu_value = 0.5 * hidden_pre * (1.0 + tanh_value)
    gelu_slope = 0.5 * (1.0 + tanh_value) + 0.5 * hidden_pre * (
        1.0 - tanh_value * tanh_value
    ) * gelu_coef * (1.0 + 3.0 * 0.044715 * hidden_pre * hidden_pre)
    return (gelu_value, gelu_slope)


def dot(a, b):
    return jnp.dot(a, b, preferred_element_type=f32)


def product(spec, a, b):
    return jnp.einsum(spec, a, b, preferred_element_type=f32)


def pair_of(ref, pair):
    return jnp.concatenate([ref[2 * pair], ref[2 * pair + 1]], axis=1)


def key_place():
    return lax.axis_index("bl") * lax.axis_size("tp") + lax.axis_index("tp")


def visible_keys(group):
    key = lax.broadcasted_iota(jnp.int32, (N, 2 * T), 0) + group * N
    lane = lax.broadcasted_iota(jnp.int32, (N, 2 * T), 1)
    query = (group // 2 * 2 + lane // T) * N + key_place() * T + lane % T
    return key <= query


def over_pairs(group, update):
    own = group // 2
    update(own, visible_keys(group))

    def full(pair, carry):
        update(pair, None)
        return carry

    lax.fori_loop(own + 1, PAIRS, full, 0)


def group_index(axes):
    index = 0
    for name in axes:
        index = index * lax.axis_size(name) + lax.axis_index(name)
    return index


def group_device(axes, index):
    device = {}
    for name in reversed(axes):
        device[name] = index % lax.axis_size(name)
        index = index // lax.axis_size(name)
    return device


def size_of(axes):
    count = 1
    for name in axes:
        count *= lax.axis_size(name)
    return count


def greet(*groups):
    barrier = pltpu.get_barrier_semaphore()
    for axes in groups:
        me, count = group_index(axes), size_of(axes)
        for hop in range(1, count):
            pl.semaphore_signal(
                barrier,
                inc=1,
                device_id=group_device(axes, (me + hop) % count),
                device_id_type=pl.DeviceIdType.MESH,
            )
    pl.semaphore_wait(barrier, sum(size_of(axes) - 1 for axes in groups))


def push(source, target, sems, index, axes, peer):
    send_sem, recv_sem = sems
    return pltpu.make_async_remote_copy(
        src_ref=source,
        dst_ref=target,
        send_sem=send_sem.at[index],
        recv_sem=recv_sem.at[index],
        device_id=group_device(axes, peer),
        device_id_type=pl.DeviceIdType.MESH,
    )


class Part:
    def __init__(self, axes, kind, x, out_dtype=bf16):
        self.axes, self.kind, self.count = axes, kind, size_of(axes)
        self.block_shape = x.shape if kind == "gather" else x.shape[1:]
        self.landing = (self.count,) + self.block_shape
        reduced = kind == "reduce"
        self.out = jax.ShapeDtypeStruct(self.block_shape if reduced else self.landing, out_dtype)
        self.scratch = [pltpu.SemaphoreType.DMA((self.count - 1,))] * 2
        if reduced:
            self.scratch = [pltpu.VMEM(self.landing, x.dtype)] + self.scratch

    def bind(self, x_ref, o_ref, scratch):
        self.x_ref, self.o_ref, self.sems = x_ref, o_ref, scratch[-2:]
        self.land = scratch[0] if self.kind == "reduce" else o_ref
        self.me = group_index(self.axes)

    def block(self, place):
        if self.kind == "gather":
            return self.x_ref
        if self.kind == "spread":
            return self.x_ref.at[place // lax.axis_size("tp")]
        return self.x_ref.at[place]

    def copy(self, hop, place, peer):
        return push(self.block(peer), self.land.at[place], self.sems, hop - 1, self.axes, peer)

    def by_rows(self, step):
        rows = self.block_shape[0]
        if rows <= 2 * T:
            step(slice(None))
        else:

            @pl.loop(0, rows // T)
            def _(index):
                step(pl.ds(pl.multiple_of(index * T, T), T))

    def begin(self):
        for hop in range(1, self.count):
            self.copy(hop, self.me, (self.me + hop) % self.count).start()
        if self.kind != "reduce":

            def keep(rows):
                self.land[self.me, rows] = self.block(self.me)[rows]

            self.by_rows(keep)

    def finish(self):
        for hop in range(1, self.count):
            origin = (self.me - hop + self.count) % self.count
            self.copy(hop, origin, origin).wait_recv()
        if self.kind == "reduce":

            def add(rows):
                total = self.block(self.me)[rows].astype(f32)
                for hop in range(1, self.count):
                    place = (self.me - hop + self.count) % self.count
                    total += self.land[place, rows].astype(f32)
                self.o_ref[rows] = total.astype(self.o_ref.dtype)

            self.by_rows(add)
        for hop in range(1, self.count):
            self.copy(hop, self.me, (self.me + hop) % self.count).wait_send()


def bind_all(parts, inputs, outputs, scratch):
    at = 0
    for part, x_ref, o_ref in zip(parts, inputs, outputs):
        part.bind(x_ref, o_ref, scratch[at : at + len(part.scratch)])
        at += len(part.scratch)


def exchange_kernel(parts, *refs):
    n = len(parts)
    bind_all(parts, refs[:n], refs[n : 2 * n], refs[2 * n :])
    groups = list(dict.fromkeys(part.axes for part in parts))
    greet(*(axes for axes in groups if not any(set(axes) < set(other) for other in groups)))
    for part in parts:
        part.begin()
    for part in parts:
        part.finish()


def exchange(collective_id, *transfers):
    parts = [Part(axes, kind, x, *dtype) for x, axes, kind, *dtype in transfers]
    result = pl.pallas_call(
        functools.partial(exchange_kernel, parts),
        out_shape=tuple(part.out for part in parts),
        in_specs=[WHOLE] * len(parts),
        out_specs=(WHOLE,) * len(parts),
        scratch_shapes=[shape for part in parts for shape in part.scratch],
        compiler_params=pltpu.CompilerParams(
            collective_id=collective_id, has_side_effects=True, vmem_limit_bytes=24 << 20
        ),
        cost_estimate=pl.CostEstimate(
            flops=12_000_000_000, bytes_accessed=4 << 20, transcendentals=0
        ),
    )(*(transfer[0] for transfer in transfers))
    return result[0] if len(transfers) == 1 else result


FWD_CHUNK = 1
FWD_AHEAD = 3
BWD_CHUNK = 2
BWD_OTHERS = 2


def forward_kernel(q_ref, own_ref, ctx_ref, lse_ref, kv_ref, qb, m_s, l_s, acc, *sems):
    greet(KEY_AXES)
    me = group_index(KEY_AXES)

    def send(chunk, hop, place, peer):
        rows = pl.ds(chunk * FWD_CHUNK, FWD_CHUNK)
        return push(
            own_ref.at[rows], kv_ref.at[place, rows], sems, (chunk, hop - 1), KEY_AXES, peer
        )

    chunks = SEG // FWD_CHUNK

    def send_all(chunk):
        for hop in range(1, CYC):
            send(chunk, hop, me, (me + hop) % CYC).start()

    for chunk in range(FWD_AHEAD):
        send_all(chunk)
    kv_ref[me] = own_ref[...]
    for pair in range(PAIRS):
        q = pair_of(q_ref, pair).astype(f32) * score_scale
        qb[pair] = jnp.concatenate([q, jnp.zeros_like(q)], axis=0).astype(bf16)
    m_s[...] = jnp.full(m_s.shape, masked_score, f32)
    l_s[...] = jnp.zeros(l_s.shape, f32)
    acc[...] = jnp.zeros(acc.shape, f32)

    def key_step(group, carry):
        kv = kv_ref[:, group].reshape(N, T)
        v_t = kv.T[D:]

        def update(pair, visible):
            s = dot(kv, qb[pair])
            if visible is not None:
                s = jnp.where(visible, s, masked_score)
            m_old = m_s[pair]
            m_new = jnp.maximum(m_old, jnp.max(s, axis=0, keepdims=True))
            e = jnp.exp(s - m_new)
            r = jnp.exp(m_old - m_new)
            l_s[pair] = l_s[pair] * r + jnp.sum(e, axis=0, keepdims=True)
            acc[pair] = acc[pair] * r + dot(v_t, e.astype(bf16))
            m_s[pair] = m_new

        over_pairs(group, update)
        return carry

    def chunk_step(chunk, carry):
        @pl.when(chunk + FWD_AHEAD < chunks)
        def _():
            send_all(chunk + FWD_AHEAD)

        for hop in range(1, CYC):
            origin = (me - hop + CYC) % CYC
            send(chunk, hop, origin, origin).wait_recv()
        return lax.fori_loop(chunk * FWD_CHUNK, (chunk + 1) * FWD_CHUNK, key_step, carry)

    lax.fori_loop(0, chunks, chunk_step, 0)
    for pair in range(PAIRS):
        row_sum = l_s[pair]
        o = (acc[pair] / row_sum).astype(bf16)
        ctx_ref[2 * pair] = o[:, :T]
        ctx_ref[2 * pair + 1] = o[:, T:]
        lse_ref[pair] = m_s[pair] + jnp.log(row_sum)

    @pl.loop(0, chunks)
    def _(chunk):
        for hop in range(1, CYC):
            send(chunk, hop, me, (me + hop) % CYC).wait_send()


def attention_forward(queries, own_kv):
    return pl.pallas_call(
        forward_kernel,
        out_shape=(
            jax.ShapeDtypeStruct((SEG, D, T), bf16),
            jax.ShapeDtypeStruct((PAIRS, 1, 2 * T), f32),
            jax.ShapeDtypeStruct((CYC, SEG, T, 2 * D), bf16),
        ),
        in_specs=[WHOLE] * 2,
        out_specs=(WHOLE,) * 3,
        scratch_shapes=[
            pltpu.VMEM((PAIRS, 2 * D, 2 * T), bf16),
            pltpu.VMEM((PAIRS, 1, 2 * T), f32),
            pltpu.VMEM((PAIRS, 1, 2 * T), f32),
            pltpu.VMEM((PAIRS, D, 2 * T), f32),
        ]
        + [pltpu.SemaphoreType.DMA((SEG // FWD_CHUNK, CYC - 1))] * 2,
        compiler_params=pltpu.CompilerParams(
            collective_id=0, has_side_effects=True, vmem_limit_bytes=40 << 20
        ),
        cost_estimate=pl.CostEstimate(
            flops=70_000_000_000, bytes_accessed=5 << 20, transcendentals=0
        ),
    )(queries, own_kv)


def backward_kernel(parts, q_ref, kv_ref, do_ref, ctx_ref, lse_ref, *refs):
    n = len(parts)
    grad_ref, *results = refs[n - 1 : 2 * n]
    w, w_t, delta, dqt, dkv_s, staged, landed, *sems = refs[2 * n :]
    bind_all(parts, refs[: n - 1] + (grad_ref,), results, sems[2:])
    sems = sems[:2]
    greet(KEY_AXES, HEAD_AXES)
    me = group_index(KEY_AXES)

    def send(chunk, hop, place, source, peer):
        rows = pl.ds(chunk * BWD_CHUNK, BWD_CHUNK)
        return push(
            staged.at[source, rows], landed.at[place, rows], sems, (chunk, hop - 1), KEY_AXES, peer
        )

    for pair in range(PAIRS):
        q = pair_of(q_ref, pair).astype(f32) * score_scale
        do = pair_of(do_ref, pair).astype(f32)
        zero = jnp.zeros_like(q)
        both = jnp.concatenate(
            [jnp.concatenate([q, zero], axis=1), jnp.concatenate([zero, do], axis=1)], axis=0
        )
        w[pair] = both.astype(bf16)
        w_t[pair] = both.T.astype(bf16)
        delta[pair] = jnp.sum(do * pair_of(ctx_ref, pair).astype(f32), axis=0, keepdims=True)
    dqt[...] = jnp.zeros(dqt.shape, f32)

    def key_step(step, carry):
        group = SEG - 1 - step
        kv = kv_ref[:, group].reshape(N, T)
        k_t = kv.T[:D]
        dkv_s[...] = jnp.zeros(dkv_s.shape, f32)

        def update(pair, visible):
            e = jnp.exp(dot(kv, w[pair][:, : 2 * T]) - lse_ref[pair])
            if visible is not None:
                e = jnp.where(visible, e, 0.0)
            ds = (e * (dot(kv, w[pair][:, 2 * T :]) - delta[pair])).astype(bf16)
            dkv_s[...] += dot(jnp.concatenate([ds, e.astype(bf16)], axis=1), w_t[pair])
            dqt[pair] += dot(k_t, ds)

        over_pairs(group, update)
        staged[:, group] = dkv_s[...].reshape(CYC, T, T).astype(bf16)
        return carry

    chunks = SEG // BWD_CHUNK

    def chunk_step(step, carry):
        carry = lax.fori_loop(step * BWD_CHUNK, (step + 1) * BWD_CHUNK, key_step, carry)
        for hop in range(1, CYC):
            peer = (me + hop) % CYC
            send(chunks - 1 - step, hop, me, peer, peer).start()

        @pl.when(step == BWD_OTHERS)
        def _():
            for part in parts[:-1]:
                part.begin()

        return carry

    lax.fori_loop(0, chunks, chunk_step, 0)
    for pair in range(PAIRS):
        d = (dqt[pair] * score_scale).astype(bf16)
        grad_ref[2 * pair, :D] = d[:, :T]
        grad_ref[2 * pair + 1, :D] = d[:, T:]

    def finish(step, carry):
        chunk = chunks - 1 - step
        for hop in range(1, CYC):
            origin = (me - hop + CYC) % CYC
            send(chunk, hop, origin, me, origin).wait_recv()
        for part in range(BWD_CHUNK):
            group = chunk * BWD_CHUNK + part
            total = staged[me, group].astype(f32)
            for hop in range(1, CYC):
                total += landed[(me - hop + CYC) % CYC, group].astype(f32)
            grad_ref[group, D:] = total.T.astype(bf16)
        return carry

    lax.fori_loop(0, chunks, finish, 0)
    parts[-1].begin()
    for part in parts:
        part.finish()

    @pl.loop(0, chunks)
    def _(chunk):
        for hop in range(1, CYC):
            peer = (me + hop) % CYC
            send(chunk, hop, me, peer, peer).wait_send()


def attention_backward(queries, key_values, context_grad, context, log_total, *transfers):
    grads = jax.ShapeDtypeStruct((SEG, 3 * D, T), bf16)
    parts = [Part(axes, kind, x, *dtype) for x, axes, kind, *dtype in transfers]
    parts.append(Part(HEAD_AXES, "swap", grads))
    return pl.pallas_call(
        functools.partial(backward_kernel, parts),
        out_shape=(grads,) + tuple(part.out for part in parts),
        in_specs=[WHOLE] * (4 + len(parts)),
        out_specs=(WHOLE,) * (1 + len(parts)),
        scratch_shapes=[
            pltpu.VMEM((PAIRS, T, 4 * T), bf16),
            pltpu.VMEM((PAIRS, 4 * T, T), bf16),
            pltpu.VMEM((PAIRS, 1, 2 * T), f32),
            pltpu.VMEM((PAIRS, D, 2 * T), f32),
            pltpu.VMEM((N, T), f32),
            pltpu.VMEM((CYC, SEG, T, T), bf16),
            pltpu.VMEM((CYC, SEG, T, T), bf16),
        ]
        + [pltpu.SemaphoreType.DMA((SEG // BWD_CHUNK, CYC - 1))] * 2
        + [shape for part in parts for shape in part.scratch],
        compiler_params=pltpu.CompilerParams(
            collective_id=1, has_side_effects=True, vmem_limit_bytes=48 << 20
        ),
        cost_estimate=pl.CostEstimate(
            flops=80_000_000_000, bytes_accessed=10 << 20, transcendentals=0
        ),
    )(queries, key_values, context_grad, context, log_total, *(x for x, *_ in transfers))


def per_device(
    hidden_in,
    ln1_gain,
    ln1_bias,
    qkv_weight,
    qv_bias,
    out_weight,
    out_bias,
    ln2_gain,
    ln2_bias,
    fc_weight,
    fc_bias,
    proj_weight,
    proj_bias,
    cotangent,
):
    tokens, width = hidden_in.shape

    def swap_heads(collective_id, parts):
        return exchange(collective_id, (parts, HEAD_AXES, "swap"))

    cot_bf = cotangent.astype(bf16)
    gathered_cot = lax.all_gather(cot_bf, "tp", axis=0, tiled=True)

    hidden_f = hidden_in.astype(f32)
    scaled_one, inverse_one, normed_one = normalize(hidden_f, ln1_gain, ln1_bias)
    normed_bf = normed_one.astype(bf16)
    q_t = product("td,dc->ct", normed_bf, qkv_weight[:, :width]) + qv_bias[0][:, None]
    kv = dot(normed_bf, qkv_weight[:, width:]) + jnp.concatenate(
        [jnp.zeros_like(qv_bias[1]), qv_bias[1]]
    )
    kv = kv.astype(bf16).reshape(tokens, 2, SEG, D).transpose(2, 0, 1, 3)
    sent = jnp.concatenate(
        [q_t.astype(bf16).reshape(SEG, D, tokens), kv.reshape(SEG, tokens, 2 * D)], axis=1
    )
    arrived = swap_heads(2, sent)
    query_t, own_kv = arrived[:, :D], arrived[:, D:]
    own_kv, gathered_cot = lax.optimization_barrier((own_kv, gathered_cot))
    normed_core = lax.all_gather(normed_bf, ("sz", "bh"), axis=0, tiled=True)
    context_heads, log_total, key_values = attention_forward(query_t, own_kv)

    context_t = swap_heads(3, context_heads).reshape(width, tokens)
    residual = hidden_f + product("ct,cd->td", context_t, out_weight) + out_bias
    residual, normed_core = lax.optimization_barrier((residual, normed_core))
    scaled_two, inverse_two, normed_two = normalize(residual, ln2_gain, ln2_bias)
    gathered_norm = exchange(4, (normed_two.astype(bf16), ("tp",), "gather"))
    gathered_norm = gathered_norm.reshape(-1, width)
    hidden_pre = dot(gathered_norm, fc_weight) + fc_bias
    gelu_value, gelu_slope = gelu_pair(hidden_pre)
    activation = gelu_value.astype(bf16)
    hidden_grad = dot(gathered_cot, proj_weight.T) * gelu_slope
    hidden_grad_bf = hidden_grad.astype(bf16)
    wide_grads = jnp.concatenate(
        [
            product("td,tf->df", gathered_norm, hidden_grad_bf),
            product("tf,td->fd", activation, gathered_cot),
        ]
    ).astype(bf16)
    norm_parts = dot(hidden_grad_bf, fc_weight.T).astype(bf16).reshape(-1, tokens, width)
    mlp_parts = dot(activation, proj_weight).astype(bf16)
    mlp_parts, norm_parts = lax.optimization_barrier((mlp_parts, norm_parts))
    mlp_out = lax.psum_scatter(mlp_parts, "tp", scatter_dimension=0, tiled=True)
    normed_two_grad, wide_core, bias_pair = exchange(
        5,
        (norm_parts, ("tp",), "reduce", f32),
        (wide_grads.reshape(2, width, width), ("sc",), "reduce"),
        (jnp.sum(hidden_grad, axis=0).reshape(-1, T), ("bl",), "gather", f32),
    )
    wide_part = lax.psum_scatter(wide_core, CHIP_ROW_AXES, scatter_dimension=0, tiled=True)
    residual_grad = cotangent + norm_back(normed_two_grad, scaled_two, inverse_two, ln2_gain)
    residual_grad_bf = residual_grad.astype(bf16)
    context_grad = product("td,cd->ct", residual_grad_bf, out_weight).astype(bf16)
    context_grad_heads = swap_heads(6, context_grad.reshape(SEG, D, tokens))

    fine = D // CYC
    row_groups = width // fine // 4
    context_rows = context_t.reshape(row_groups, 4, fine, tokens).transpose(1, 0, 2, 3)
    (
        head_grads,
        grad_tokens,
        context_tokens,
        normed_all,
        bias_parts,
        token_grads,
    ) = attention_backward(
        query_t,
        key_values,
        context_grad_heads,
        context_heads,
        log_total,
        (residual_grad_bf, ("tp",), "gather"),
        (context_rows.reshape(4, row_groups * fine, tokens), ("tp",), "swap"),
        (normed_core, ("sc",), "gather"),
        (jnp.sum(bias_pair, axis=0), HEAD_AXES, "gather", f32),
    )
    head_grads, normed_all, token_grads, wide_part, mlp_out = lax.optimization_barrier(
        (head_grads, normed_all, token_grads, wide_part, mlp_out)
    )
    block_out = residual + mlp_out.astype(f32) + proj_bias
    wide_sum = lax.all_gather(wide_part, ROW_AXES, axis=0, tiled=True)
    wide_sum = wide_sum.reshape(-1, 2, width // 4, width)
    token_grads = token_grads.reshape(SEG, 3, D, tokens).transpose(1, 0, 2, 3)
    token_grads = token_grads.reshape(3 * width, tokens)
    normed_one_grad = product("ft,df->td", token_grads, qkv_weight)
    input_grad = residual_grad + norm_back(normed_one_grad, scaled_one, inverse_one, ln1_gain)

    vectors = jnp.stack(
        [
            jnp.sum(residual_grad, axis=0),
            jnp.sum(normed_two_grad * scaled_two, axis=0),
            jnp.sum(normed_two_grad, axis=0),
            jnp.sum(cotangent, axis=0),
            jnp.sum(normed_one_grad * scaled_one, axis=0),
            jnp.sum(normed_one_grad, axis=0),
        ]
    ).astype(bf16)
    vectors = vectors.reshape(-1, SEG, CYC, fine).transpose(2, 1, 0, 3)
    head_sums = jnp.sum(head_grads.astype(f32), axis=(0, 2)).astype(bf16).reshape(3, CYC, fine)
    own_head = jnp.arange(SEG)[None, :, None, None] == group_index(HEAD_AXES)
    head_sums = jnp.where(own_head, head_sums.transpose(1, 0, 2)[:, None], 0)
    narrow = jnp.concatenate([vectors, head_sums], axis=2)
    count = narrow.shape[2]
    narrow = narrow.reshape(CYC, SEG, 1, count * fine)
    by_core = head_grads.reshape(-1, 2, 2, 3 * D, tokens).transpose(1, 0, 2, 3, 4)
    qkv_part = product(
        "gtd,gft->df",
        normed_all.reshape(SEG, tokens, width),
        by_core.reshape(SEG, 3 * D, tokens),
    ).astype(bf16)
    qkv_lines = fine * 3 * D // T
    qkv_part = qkv_part.reshape(SEG, CYC, qkv_lines, T).transpose(1, 0, 2, 3)
    packed = jnp.concatenate(
        [qkv_part, jnp.pad(narrow, ((0, 0), (0, 0), (0, 15 - qkv_lines), (0, T - count * fine)))],
        axis=2,
    )
    out_part = product("gct,gtd->cd", context_tokens, grad_tokens).astype(bf16)
    summed, out_rows = exchange(
        7,
        (packed, KEY_AXES, "reduce"),
        (out_part.reshape(row_groups, fine, width), ROW_AXES, "reduce"),
    )
    fc_bias_grad = jnp.sum(bias_parts, axis=0).reshape(-1)
    moved, out_rows = exchange(
        8,
        (summed, HEAD_AXES + ("tp",), "spread"),
        (out_rows, ("tp",), "gather"),
    )
    fc_weight_grad = wide_sum[:, 0].reshape(width, width).astype(f32)
    proj_weight_grad = wide_sum[:, 1].reshape(width, width).astype(f32)
    own_rows = 4 * fine
    moved = moved.reshape(SEG, 4, -1, T)
    qkv_rows = moved[:, :, :qkv_lines].reshape(SEG, 4, fine, 3, D).transpose(1, 2, 3, 0, 4)
    qkv_rows = qkv_rows.reshape(own_rows, 3 * width).astype(f32)
    narrow = jnp.sum(moved[:, :, qkv_lines, : count * fine].astype(f32), axis=0)
    narrow = narrow.reshape(4, count, fine).transpose(1, 0, 2).reshape(count, own_rows)
    out_rows = out_rows.reshape(own_rows, width).astype(f32)
    return (
        block_out,
        input_grad,
        narrow[4],
        narrow[5],
        qkv_rows,
        jnp.stack([narrow[6], narrow[8]]),
        out_rows,
        narrow[0],
        narrow[1],
        narrow[2],
        fc_weight_grad,
        fc_bias_grad,
        proj_weight_grad,
        narrow[3],
    )


def solution(mesh):
    shape = mesh.devices.shape
    split = Mesh(
        mesh.devices.reshape(shape[0] // 2, 2, shape[1] // 2, 2, shape[2]),
        ("sz", "sc", "bh", "bl", "tp"),
    )
    every = P(("sz", "sc", "bh", "bl", "tp"), None)
    rows = ("sz", "sc", "bh", "bl")
    return jax.shard_map(
        per_device,
        mesh=split,
        in_specs=(
            every,
            P(),
            P(),
            P(),
            P(),
            P(),
            P(),
            P(),
            P(),
            P(None, "tp"),
            P("tp"),
            P("tp", None),
            P(),
            every,
        ),
        out_specs=(
            every,
            every,
            P(rows),
            P(rows),
            P(rows, None),
            P(None, rows),
            P(rows, None),
            P(rows),
            P(rows),
            P(rows),
            P(None, "tp"),
            P("tp"),
            P("tp", None),
            P(rows),
        ),
        check_vma=False,
    )
```

```python
import functools
import math

import jax
import jax.numpy as jnp
from jax import lax
from jax.experimental import pallas as pl
from jax.experimental.pallas import tpu as pltpu
from jax.sharding import Mesh
from jax.sharding import PartitionSpec as P

D = 64
T = 128
SEG = 16
CYC = 8
N = CYC * T
PAIRS = SEG // 2
HEAD_AXES = ("sz", "sc", "bh")
KEY_AXES = ("bl", "tp")
ROW_AXES = ("sz", "sc", "bh", "bl")
CHIP_ROW_AXES = ("sz", "bh", "bl")

epsilon = 1e-05
gelu_coef = math.sqrt(2.0 / math.pi)
masked_score = -1e30
score_scale = 1.0 / math.sqrt(D)
f32, bf16 = jnp.float32, jnp.bfloat16
WHOLE = pl.BlockSpec(memory_space=pltpu.VMEM)


def normalize(matrix, norm_gain, norm_shift):
    row_mean = jnp.mean(matrix, axis=-1, keepdims=True)
    centered = matrix - row_mean
    variance = jnp.mean(centered * centered, axis=-1, keepdims=True)
    inverse = lax.rsqrt(variance + epsilon)
    scaled = centered * inverse
    return (scaled, inverse, scaled * norm_gain + norm_shift)


def norm_back(upstream_grad, scaled, inverse, norm_gain):
    weighted = upstream_grad * norm_gain
    first_mean = jnp.mean(weighted, axis=-1, keepdims=True)
    second_mean = jnp.mean(weighted * scaled, axis=-1, keepdims=True)
    return inverse * (weighted - first_mean - scaled * second_mean)


def gelu_pair(hidden_pre):
    tanh_arg = gelu_coef * (hidden_pre + 0.044715 * hidden_pre * hidden_pre * hidden_pre)
    tanh_value = jnp.tanh(tanh_arg)
    gelu_value = 0.5 * hidden_pre * (1.0 + tanh_value)
    gelu_slope = 0.5 * (1.0 + tanh_value) + 0.5 * hidden_pre * (
        1.0 - tanh_value * tanh_value
    ) * gelu_coef * (1.0 + 3.0 * 0.044715 * hidden_pre * hidden_pre)
    return (gelu_value, gelu_slope)


def dot(a, b):
    return jnp.dot(a, b, preferred_element_type=f32)


def product(spec, a, b):
    return jnp.einsum(spec, a, b, preferred_element_type=f32)


def pair_of(ref, pair):
    return jnp.concatenate([ref[2 * pair], ref[2 * pair + 1]], axis=1)


def key_place():
    return lax.axis_index("bl") * lax.axis_size("tp") + lax.axis_index("tp")


def visible_keys(group):
    key = lax.broadcasted_iota(jnp.int32, (N, 2 * T), 0) + group * N
    lane = lax.broadcasted_iota(jnp.int32, (N, 2 * T), 1)
    query = (group // 2 * 2 + lane // T) * N + key_place() * T + lane % T
    return key <= query


def over_pairs(group, update):
    own = group // 2
    update(own, visible_keys(group))

    def full(pair, carry):
        update(pair, None)
        return carry

    lax.fori_loop(own + 1, PAIRS, full, 0)


def group_index(axes):
    index = 0
    for name in axes:
        index = index * lax.axis_size(name) + lax.axis_index(name)
    return index


def group_device(axes, index):
    device = {}
    for name in reversed(axes):
        device[name] = index % lax.axis_size(name)
        index = index // lax.axis_size(name)
    return device


def size_of(axes):
    count = 1
    for name in axes:
        count *= lax.axis_size(name)
    return count


def greet(*groups):
    barrier = pltpu.get_barrier_semaphore()
    for axes in groups:
        me, count = group_index(axes), size_of(axes)
        for hop in range(1, count):
            pl.semaphore_signal(
                barrier,
                inc=1,
                device_id=group_device(axes, (me + hop) % count),
                device_id_type=pl.DeviceIdType.MESH,
            )
    pl.semaphore_wait(barrier, sum(size_of(axes) - 1 for axes in groups))


def push(source, target, sems, index, axes, peer):
    send_sem, recv_sem = sems
    return pltpu.make_async_remote_copy(
        src_ref=source,
        dst_ref=target,
        send_sem=send_sem.at[index],
        recv_sem=recv_sem.at[index],
        device_id=group_device(axes, peer),
        device_id_type=pl.DeviceIdType.MESH,
    )


class Part:
    def __init__(self, axes, kind, x, out_dtype=bf16):
        self.axes, self.kind, self.count = axes, kind, size_of(axes)
        self.block_shape = x.shape if kind == "gather" else x.shape[1:]
        self.landing = (self.count,) + self.block_shape
        reduced = kind == "reduce"
        self.out = jax.ShapeDtypeStruct(self.block_shape if reduced else self.landing, out_dtype)
        self.scratch = [pltpu.SemaphoreType.DMA((self.count - 1,))] * 2
        if reduced:
            self.scratch = [pltpu.VMEM(self.landing, x.dtype)] + self.scratch

    def bind(self, x_ref, o_ref, scratch):
        self.x_ref, self.o_ref, self.sems = x_ref, o_ref, scratch[-2:]
        self.land = scratch[0] if self.kind == "reduce" else o_ref
        self.me = group_index(self.axes)

    def block(self, place):
        if self.kind == "gather":
            return self.x_ref
        if self.kind == "spread":
            return self.x_ref.at[place // lax.axis_size("tp")]
        return self.x_ref.at[place]

    def copy(self, hop, place, peer):
        return push(self.block(peer), self.land.at[place], self.sems, hop - 1, self.axes, peer)

    def by_rows(self, step):
        rows = self.block_shape[0]
        if rows <= 2 * T:
            step(slice(None))
        else:

            @pl.loop(0, rows // T)
            def _(index):
                step(pl.ds(pl.multiple_of(index * T, T), T))

    def begin(self):
        for hop in range(1, self.count):
            self.copy(hop, self.me, (self.me + hop) % self.count).start()
        if self.kind != "reduce":

            def keep(rows):
                self.land[self.me, rows] = self.block(self.me)[rows]

            self.by_rows(keep)

    def finish(self):
        for hop in range(1, self.count):
            origin = (self.me - hop + self.count) % self.count
            self.copy(hop, origin, origin).wait_recv()
        if self.kind == "reduce":

            def add(rows):
                total = self.block(self.me)[rows].astype(f32)
                for hop in range(1, self.count):
                    place = (self.me - hop + self.count) % self.count
                    total += self.land[place, rows].astype(f32)
                self.o_ref[rows] = total.astype(self.o_ref.dtype)

            self.by_rows(add)
        for hop in range(1, self.count):
            self.copy(hop, self.me, (self.me + hop) % self.count).wait_send()


def bind_all(parts, inputs, outputs, scratch):
    at = 0
    for part, x_ref, o_ref in zip(parts, inputs, outputs):
        part.bind(x_ref, o_ref, scratch[at : at + len(part.scratch)])
        at += len(part.scratch)


def exchange_kernel(parts, *refs):
    n = len(parts)
    bind_all(parts, refs[:n], refs[n : 2 * n], refs[2 * n :])
    groups = list(dict.fromkeys(part.axes for part in parts))
    greet(*(axes for axes in groups if not any(set(axes) < set(other) for other in groups)))
    for part in parts:
        part.begin()
    for part in parts:
        part.finish()


def exchange(collective_id, *transfers):
    parts = [Part(axes, kind, x, *dtype) for x, axes, kind, *dtype in transfers]
    result = pl.pallas_call(
        functools.partial(exchange_kernel, parts),
        out_shape=tuple(part.out for part in parts),
        in_specs=[WHOLE] * len(parts),
        out_specs=(WHOLE,) * len(parts),
        scratch_shapes=[shape for part in parts for shape in part.scratch],
        compiler_params=pltpu.CompilerParams(
            collective_id=collective_id, has_side_effects=True, vmem_limit_bytes=24 << 20
        ),
        cost_estimate=pl.CostEstimate(
            flops=12_000_000_000, bytes_accessed=4 << 20, transcendentals=0
        ),
    )(*(transfer[0] for transfer in transfers))
    return result[0] if len(transfers) == 1 else result


FWD_CHUNK = 1
FWD_AHEAD = 3
BWD_CHUNK = 2
BWD_OTHERS = 2


def forward_kernel(q_ref, own_ref, ctx_ref, lse_ref, kv_ref, qb, m_s, l_s, acc, *sems):
    greet(KEY_AXES)
    me = group_index(KEY_AXES)

    def send(chunk, hop, place, peer):
        rows = pl.ds(chunk * FWD_CHUNK, FWD_CHUNK)
        return push(
            own_ref.at[rows], kv_ref.at[place, rows], sems, (chunk, hop - 1), KEY_AXES, peer
        )

    chunks = SEG // FWD_CHUNK

    def send_all(chunk):
        for hop in range(1, CYC):
            send(chunk, hop, me, (me + hop) % CYC).start()

    for chunk in range(FWD_AHEAD):
        send_all(chunk)
    kv_ref[me] = own_ref[...]
    for pair in range(PAIRS):
        q = pair_of(q_ref, pair).astype(f32) * score_scale
        qb[pair] = jnp.concatenate([q, jnp.zeros_like(q)], axis=0).astype(bf16)
    m_s[...] = jnp.full(m_s.shape, masked_score, f32)
    l_s[...] = jnp.zeros(l_s.shape, f32)
    acc[...] = jnp.zeros(acc.shape, f32)

    def key_step(group, carry):
        kv = kv_ref[:, group].reshape(N, T)
        v_t = kv.T[D:]

        def update(pair, visible):
            s = dot(kv, qb[pair])
            if visible is not None:
                s = jnp.where(visible, s, masked_score)
            m_old = m_s[pair]
            m_new = jnp.maximum(m_old, jnp.max(s, axis=0, keepdims=True))
            e = jnp.exp(s - m_new)
            r = jnp.exp(m_old - m_new)
            l_s[pair] = l_s[pair] * r + jnp.sum(e, axis=0, keepdims=True)
            acc[pair] = acc[pair] * r + dot(v_t, e.astype(bf16))
            m_s[pair] = m_new

        over_pairs(group, update)
        return carry

    def chunk_step(chunk, carry):
        @pl.when(chunk + FWD_AHEAD < chunks)
        def _():
            send_all(chunk + FWD_AHEAD)

        for hop in range(1, CYC):
            origin = (me - hop + CYC) % CYC
            send(chunk, hop, origin, origin).wait_recv()
        return lax.fori_loop(chunk * FWD_CHUNK, (chunk + 1) * FWD_CHUNK, key_step, carry)

    lax.fori_loop(0, chunks, chunk_step, 0)
    for pair in range(PAIRS):
        row_sum = l_s[pair]
        o = (acc[pair] / row_sum).astype(bf16)
        ctx_ref[2 * pair] = o[:, :T]
        ctx_ref[2 * pair + 1] = o[:, T:]
        lse_ref[pair] = m_s[pair] + jnp.log(row_sum)

    @pl.loop(0, chunks)
    def _(chunk):
        for hop in range(1, CYC):
            send(chunk, hop, me, (me + hop) % CYC).wait_send()


def attention_forward(queries, own_kv):
    return pl.pallas_call(
        forward_kernel,
        out_shape=(
            jax.ShapeDtypeStruct((SEG, D, T), bf16),
            jax.ShapeDtypeStruct((PAIRS, 1, 2 * T), f32),
            jax.ShapeDtypeStruct((CYC, SEG, T, 2 * D), bf16),
        ),
        in_specs=[WHOLE] * 2,
        out_specs=(WHOLE,) * 3,
        scratch_shapes=[
            pltpu.VMEM((PAIRS, 2 * D, 2 * T), bf16),
            pltpu.VMEM((PAIRS, 1, 2 * T), f32),
            pltpu.VMEM((PAIRS, 1, 2 * T), f32),
            pltpu.VMEM((PAIRS, D, 2 * T), f32),
        ]
        + [pltpu.SemaphoreType.DMA((SEG // FWD_CHUNK, CYC - 1))] * 2,
        compiler_params=pltpu.CompilerParams(
            collective_id=0, has_side_effects=True, vmem_limit_bytes=40 << 20
        ),
        cost_estimate=pl.CostEstimate(
            flops=70_000_000_000, bytes_accessed=5 << 20, transcendentals=0
        ),
    )(queries, own_kv)


def backward_kernel(parts, q_ref, kv_ref, do_ref, ctx_ref, lse_ref, *refs):
    n = len(parts)
    grad_ref, *results = refs[n - 1 : 2 * n]
    w, w_t, delta, dqt, dkv_s, staged, landed, *sems = refs[2 * n :]
    bind_all(parts, refs[: n - 1] + (grad_ref,), results, sems[2:])
    sems = sems[:2]
    greet(KEY_AXES, HEAD_AXES)
    me = group_index(KEY_AXES)

    def send(chunk, hop, place, source, peer):
        rows = pl.ds(chunk * BWD_CHUNK, BWD_CHUNK)
        return push(
            staged.at[source, rows], landed.at[place, rows], sems, (chunk, hop - 1), KEY_AXES, peer
        )

    for pair in range(PAIRS):
        q = pair_of(q_ref, pair).astype(f32) * score_scale
        do = pair_of(do_ref, pair).astype(f32)
        zero = jnp.zeros_like(q)
        both = jnp.concatenate(
            [jnp.concatenate([q, zero], axis=1), jnp.concatenate([zero, do], axis=1)], axis=0
        )
        w[pair] = both.astype(bf16)
        w_t[pair] = both.T.astype(bf16)
        delta[pair] = jnp.sum(do * pair_of(ctx_ref, pair).astype(f32), axis=0, keepdims=True)
    dqt[...] = jnp.zeros(dqt.shape, f32)

    def key_step(step, carry):
        group = SEG - 1 - step
        kv = kv_ref[:, group].reshape(N, T)
        k_t = kv.T[:D]
        dkv_s[...] = jnp.zeros(dkv_s.shape, f32)

        def update(pair, visible):
            e = jnp.exp(dot(kv, w[pair][:, : 2 * T]) - lse_ref[pair])
            if visible is not None:
                e = jnp.where(visible, e, 0.0)
            ds = (e * (dot(kv, w[pair][:, 2 * T :]) - delta[pair])).astype(bf16)
            dkv_s[...] += dot(jnp.concatenate([ds, e.astype(bf16)], axis=1), w_t[pair])
            dqt[pair] += dot(k_t, ds)

        over_pairs(group, update)
        staged[:, group] = dkv_s[...].reshape(CYC, T, T).astype(bf16)
        return carry

    chunks = SEG // BWD_CHUNK

    def chunk_step(step, carry):
        carry = lax.fori_loop(step * BWD_CHUNK, (step + 1) * BWD_CHUNK, key_step, carry)
        for hop in range(1, CYC):
            peer = (me + hop) % CYC
            send(chunks - 1 - step, hop, me, peer, peer).start()

        @pl.when(step == BWD_OTHERS)
        def _():
            for part in parts[:-1]:
                part.begin()

        return carry

    lax.fori_loop(0, chunks, chunk_step, 0)
    for pair in range(PAIRS):
        d = (dqt[pair] * score_scale).astype(bf16)
        grad_ref[2 * pair, :D] = d[:, :T]
        grad_ref[2 * pair + 1, :D] = d[:, T:]

    def finish(step, carry):
        chunk = chunks - 1 - step
        for hop in range(1, CYC):
            origin = (me - hop + CYC) % CYC
            send(chunk, hop, origin, me, origin).wait_recv()
        for part in range(BWD_CHUNK):
            group = chunk * BWD_CHUNK + part
            total = staged[me, group].astype(f32)
            for hop in range(1, CYC):
                total += landed[(me - hop + CYC) % CYC, group].astype(f32)
            grad_ref[group, D:] = total.T.astype(bf16)
        return carry

    lax.fori_loop(0, chunks, finish, 0)
    parts[-1].begin()
    for part in parts:
        part.finish()

    @pl.loop(0, chunks)
    def _(chunk):
        for hop in range(1, CYC):
            peer = (me + hop) % CYC
            send(chunk, hop, me, peer, peer).wait_send()


def attention_backward(queries, key_values, context_grad, context, log_total, *transfers):
    grads = jax.ShapeDtypeStruct((SEG, 3 * D, T), bf16)
    parts = [Part(axes, kind, x, *dtype) for x, axes, kind, *dtype in transfers]
    parts.append(Part(HEAD_AXES, "swap", grads))
    return pl.pallas_call(
        functools.partial(backward_kernel, parts),
        out_shape=(grads,) + tuple(part.out for part in parts),
        in_specs=[WHOLE] * (4 + len(parts)),
        out_specs=(WHOLE,) * (1 + len(parts)),
        scratch_shapes=[
            pltpu.VMEM((PAIRS, T, 4 * T), bf16),
            pltpu.VMEM((PAIRS, 4 * T, T), bf16),
            pltpu.VMEM((PAIRS, 1, 2 * T), f32),
            pltpu.VMEM((PAIRS, D, 2 * T), f32),
            pltpu.VMEM((N, T), f32),
            pltpu.VMEM((CYC, SEG, T, T), bf16),
            pltpu.VMEM((CYC, SEG, T, T), bf16),
        ]
        + [pltpu.SemaphoreType.DMA((SEG // BWD_CHUNK, CYC - 1))] * 2
        + [shape for part in parts for shape in part.scratch],
        compiler_params=pltpu.CompilerParams(
            collective_id=1, has_side_effects=True, vmem_limit_bytes=48 << 20
        ),
        cost_estimate=pl.CostEstimate(
            flops=80_000_000_000, bytes_accessed=10 << 20, transcendentals=0
        ),
    )(queries, key_values, context_grad, context, log_total, *(x for x, *_ in transfers))


def per_device(
    hidden_in,
    ln1_gain,
    ln1_bias,
    qkv_weight,
    qv_bias,
    out_weight,
    out_bias,
    ln2_gain,
    ln2_bias,
    fc_weight,
    fc_bias,
    proj_weight,
    proj_bias,
    cotangent,
):
    tokens, width = hidden_in.shape

    def swap_heads(collective_id, parts):
        return exchange(collective_id, (parts, HEAD_AXES, "swap"))

    cot_bf = cotangent.astype(bf16)
    gathered_cot = lax.all_gather(cot_bf, "tp", axis=0, tiled=True)

    hidden_f = hidden_in.astype(f32)
    scaled_one, inverse_one, normed_one = normalize(hidden_f, ln1_gain, ln1_bias)
    normed_bf = normed_one.astype(bf16)
    q_t = product("td,dc->ct", normed_bf, qkv_weight[:, :width]) + qv_bias[0][:, None]
    kv = dot(normed_bf, qkv_weight[:, width:]) + jnp.concatenate(
        [jnp.zeros_like(qv_bias[1]), qv_bias[1]]
    )
    kv = kv.astype(bf16).reshape(tokens, 2, SEG, D).transpose(2, 0, 1, 3)
    sent = jnp.concatenate(
        [q_t.astype(bf16).reshape(SEG, D, tokens), kv.reshape(SEG, tokens, 2 * D)], axis=1
    )
    arrived = swap_heads(2, sent)
    query_t, own_kv = arrived[:, :D], arrived[:, D:]
    own_kv, gathered_cot = lax.optimization_barrier((own_kv, gathered_cot))
    normed_core = lax.all_gather(normed_bf, ("sz", "bh"), axis=0, tiled=True)
    context_heads, log_total, key_values = attention_forward(query_t, own_kv)

    context_t = swap_heads(3, context_heads).reshape(width, tokens)
    residual = hidden_f + product("ct,cd->td", context_t, out_weight) + out_bias
    residual, normed_core = lax.optimization_barrier((residual, normed_core))
    scaled_two, inverse_two, normed_two = normalize(residual, ln2_gain, ln2_bias)
    gathered_norm = exchange(4, (normed_two.astype(bf16), ("tp",), "gather"))
    gathered_norm = gathered_norm.reshape(-1, width)
    hidden_pre = dot(gathered_norm, fc_weight) + fc_bias
    gelu_value, gelu_slope = gelu_pair(hidden_pre)
    activation = gelu_value.astype(bf16)
    hidden_grad = dot(gathered_cot, proj_weight.T) * gelu_slope
    hidden_grad_bf = hidden_grad.astype(bf16)
    wide_grads = jnp.concatenate(
        [
            product("td,tf->df", gathered_norm, hidden_grad_bf),
            product("tf,td->fd", activation, gathered_cot),
        ]
    ).astype(bf16)
    norm_parts = dot(hidden_grad_bf, fc_weight.T).astype(bf16).reshape(-1, tokens, width)
    normed_two_grad, wide_core, bias_pair = exchange(
        5,
        (norm_parts, ("tp",), "reduce", f32),
        (wide_grads.reshape(2, width, width), ("sc",), "reduce"),
        (jnp.sum(hidden_grad, axis=0).reshape(-1, T), ("bl",), "gather", f32),
    )
    wide_part = lax.psum_scatter(wide_core, CHIP_ROW_AXES, scatter_dimension=0, tiled=True)
    residual_grad = cotangent + norm_back(normed_two_grad, scaled_two, inverse_two, ln2_gain)
    residual_grad_bf = residual_grad.astype(bf16)
    context_grad = product("td,cd->ct", residual_grad_bf, out_weight).astype(bf16)
    context_grad_heads = swap_heads(6, context_grad.reshape(SEG, D, tokens))

    fine = D // CYC
    row_groups = width // fine // 4
    context_rows = context_t.reshape(row_groups, 4, fine, tokens).transpose(1, 0, 2, 3)
    (
        head_grads,
        grad_tokens,
        context_tokens,
        normed_all,
        bias_parts,
        token_grads,
    ) = attention_backward(
        query_t,
        key_values,
        context_grad_heads,
        context_heads,
        log_total,
        (residual_grad_bf, ("tp",), "gather"),
        (context_rows.reshape(4, row_groups * fine, tokens), ("tp",), "swap"),
        (normed_core, ("sc",), "gather"),
        (jnp.sum(bias_pair, axis=0), HEAD_AXES, "gather", f32),
    )
    head_grads, normed_all, token_grads, wide_part, activation = lax.optimization_barrier(
        (head_grads, normed_all, token_grads, wide_part, activation)
    )
    wide_sum = lax.all_gather(wide_part, ROW_AXES, axis=0, tiled=True)
    wide_sum = wide_sum.reshape(-1, 2, width // 4, width)
    token_grads = token_grads.reshape(SEG, 3, D, tokens).transpose(1, 0, 2, 3)
    token_grads = token_grads.reshape(3 * width, tokens)
    normed_one_grad = product("ft,df->td", token_grads, qkv_weight)
    input_grad = residual_grad + norm_back(normed_one_grad, scaled_one, inverse_one, ln1_gain)

    vectors = jnp.stack(
        [
            jnp.sum(residual_grad, axis=0),
            jnp.sum(normed_two_grad * scaled_two, axis=0),
            jnp.sum(normed_two_grad, axis=0),
            jnp.sum(cotangent, axis=0),
            jnp.sum(normed_one_grad * scaled_one, axis=0),
            jnp.sum(normed_one_grad, axis=0),
        ]
    ).astype(bf16)
    vectors = vectors.reshape(-1, SEG, CYC, fine).transpose(2, 1, 0, 3)
    head_sums = jnp.sum(head_grads.astype(f32), axis=(0, 2)).astype(bf16).reshape(3, CYC, fine)
    own_head = jnp.arange(SEG)[None, :, None, None] == group_index(HEAD_AXES)
    head_sums = jnp.where(own_head, head_sums.transpose(1, 0, 2)[:, None], 0)
    narrow = jnp.concatenate([vectors, head_sums], axis=2)
    count = narrow.shape[2]
    narrow = narrow.reshape(CYC, SEG, 1, count * fine)
    by_core = head_grads.reshape(-1, 2, 2, 3 * D, tokens).transpose(1, 0, 2, 3, 4)
    qkv_part = product(
        "gtd,gft->df",
        normed_all.reshape(SEG, tokens, width),
        by_core.reshape(SEG, 3 * D, tokens),
    ).astype(bf16)
    qkv_lines = fine * 3 * D // T
    qkv_part = qkv_part.reshape(SEG, CYC, qkv_lines, T).transpose(1, 0, 2, 3)
    packed = jnp.concatenate(
        [qkv_part, jnp.pad(narrow, ((0, 0), (0, 0), (0, 15 - qkv_lines), (0, T - count * fine)))],
        axis=2,
    )
    out_part = product("gct,gtd->cd", context_tokens, grad_tokens).astype(bf16)
    mlp_parts = dot(activation, proj_weight).astype(bf16).reshape(-1, tokens, width)
    summed, out_rows, mlp_out = exchange(
        7,
        (packed, KEY_AXES, "reduce"),
        (out_part.reshape(row_groups, fine, width), ROW_AXES, "reduce"),
        (mlp_parts, ("tp",), "reduce", f32),
    )
    block_out = residual + mlp_out + proj_bias
    fc_bias_grad = jnp.sum(bias_parts, axis=0).reshape(-1)
    moved, out_rows = exchange(
        8,
        (summed, HEAD_AXES + ("tp",), "spread"),
        (out_rows, ("tp",), "gather"),
    )
    fc_weight_grad = wide_sum[:, 0].reshape(width, width).astype(f32)
    proj_weight_grad = wide_sum[:, 1].reshape(width, width).astype(f32)
    own_rows = 4 * fine
    moved = moved.reshape(SEG, 4, -1, T)
    qkv_rows = moved[:, :, :qkv_lines].reshape(SEG, 4, fine, 3, D).transpose(1, 2, 3, 0, 4)
    qkv_rows = qkv_rows.reshape(own_rows, 3 * width).astype(f32)
    narrow = jnp.sum(moved[:, :, qkv_lines, : count * fine].astype(f32), axis=0)
    narrow = narrow.reshape(4, count, fine).transpose(1, 0, 2).reshape(count, own_rows)
    out_rows = out_rows.reshape(own_rows, width).astype(f32)
    return (
        block_out,
        input_grad,
        narrow[4],
        narrow[5],
        qkv_rows,
        jnp.stack([narrow[6], narrow[8]]),
        out_rows,
        narrow[0],
        narrow[1],
        narrow[2],
        fc_weight_grad,
        fc_bias_grad,
        proj_weight_grad,
        narrow[3],
    )


def solution(mesh):
    shape = mesh.devices.shape
    split = Mesh(
        mesh.devices.reshape(shape[0] // 2, 2, shape[1] // 2, 2, shape[2]),
        ("sz", "sc", "bh", "bl", "tp"),
    )
    every = P(("sz", "sc", "bh", "bl", "tp"), None)
    rows = ("sz", "sc", "bh", "bl")
    return jax.shard_map(
        per_device,
        mesh=split,
        in_specs=(
            every,
            P(),
            P(),
            P(),
            P(),
            P(),
            P(),
            P(),
            P(),
            P(None, "tp"),
            P("tp"),
            P("tp", None),
            P(),
            every,
        ),
        out_specs=(
            every,
            every,
            P(rows),
            P(rows),
            P(rows, None),
            P(None, rows),
            P(rows, None),
            P(rows),
            P(rows),
            P(rows),
            P(None, "tp"),
            P("tp"),
            P("tp", None),
            P(rows),
        ),
        check_vma=False,
    )
```
